32 devices in a mesh: tm: 4 (over z), lon: 8 (over y, x, core).
Axes of the slice: x: 2, y: 2, z: 4, core: 2. Of those that a mesh axis runs over, the one named last changes fastest.
Arguments:
- rhs_state: float32 [4, 3, 1024, 2048], P('tm', None, None, 'lon'), may hold values from -30 to 30
- innovations: float32 [4, 8192], P('tm', 'lon'), may hold values from -6 to 6
- trajectory: bfloat16 [4, 2, 3, 1024, 2048], P('tm', None, None, None, 'lon'), may hold values from -1 to 1.5, as said below
- model_var: float32 [4, 3, 1024, 2048], P('tm', None, None, 'lon'), may hold values from 0.2 to 2
- obs_var: float32 [4, 8192], P('tm', 'lon'), may hold values from 0.2 to 2
- obs_index: int32 [4, 8192], P('tm', 'lon'), may hold values from 0 to 786431, as said below
- control_rhs: float32 [4, 3, 1024, 2048], P('tm', None, None, 'lon'), may hold values from -30 to 30
Outputs:
- multiplier_out: float32 [4, 3, 1024, 2048], P('tm', None, None, 'lon')
- obs_dual_out: float32 [4, 8192], P('tm', 'lon')
- increment_out: float32 [4, 3, 1024, 2048], P('tm', None, None, 'lon')
The draws below stay inside these ranges and needn't reach their ends.
Inputs may be any that keep to these rules, and one draw needn't show every extreme that they name: obs_index[k, j] = (field 1024 + row) * 256 + column with field 0 to 2, row 0 to 1023 and column 0 to 255 within the band j // 1024; an index may repeat. Field 0 of trajectory is the depth, fields 1 and 2 the winds.
All inputs are finite; a program needn't handle non-finite values.
Results may differ from the reference program's by a relative error of at most 0.0003.
Values sent between devices are 32-bit elements; how exact they have to be, the bound alone decides.
No kernel may reach another device: no remote copies, remote signals or barrier semaphores. Data moves between devices by JAX's collectives and lax.ppermute only.
A program may use at most 192 MiB of HBM per device.

```python
import math
import jax
import jax.numpy as jnp
from jax import lax

LAT = 1024
LON_DEV = 256
OBS_DEV = 1024
STEPS = 2
SUBWIN = 4
NLON = 2048
NOBS = 8192


def ramp_factor():
    column = jnp.arange(NLON, dtype=jnp.float32)
    window = jnp.arange(SUBWIN, dtype=jnp.float32)
    return (1.0 + 2.0 * column / (NLON - 1))[None, None, None, :] * (1.0 + window / (SUBWIN - 1))[:, None, None, None]


def band_envelope(key):
    phase = jax.random.randint(key, (SUBWIN, 3, LAT, 1), 0, 4)
    column = jnp.arange(NLON, dtype=jnp.int32)[None, None, None, :]
    inside = column % LON_DEV
    edge = (inside < 2) | (inside >= LON_DEV - 2)
    heavy = (column + phase) % 4 == 0
    return jnp.where(edge | heavy, 1.0, 0.05).astype(jnp.float32)


def drawn_values(key_one):
    shape = (SUBWIN, 3, LAT, NLON)
    return jnp.clip(jax.random.normal(key_one, shape, jnp.float32), -4.0, 4.0)


def draw_rhs_state(key, part):
    key_one = jax.random.fold_in(key, 0)
    key_three = jax.random.fold_in(key, 2)
    values = drawn_values(key_one)
    return (values * ramp_factor() * band_envelope(key_three)).astype(jnp.float32)


def draw_control_rhs(key, part):
    own_key = jax.random.fold_in(key, 11)
    key_one = jax.random.fold_in(own_key, 0)
    key_three = jax.random.fold_in(own_key, 2)
    values = drawn_values(key_one)
    return (values * ramp_factor() * band_envelope(key_three)).astype(jnp.float32)


def draw_trajectory(key, part):
    key_one, key_two = jax.random.split(key, 2)
    depth = jax.random.uniform(key_one, (SUBWIN, STEPS, 1, LAT, NLON), jnp.float32, 0.5, 1.5)
    winds = jax.random.uniform(key_two, (SUBWIN, STEPS, 2, LAT, NLON), jnp.float32, -1.0, 1.0)
    return jnp.concatenate([depth, winds], axis=2).astype(jnp.bfloat16)


def draw_obs_index(key, part):
    key_one, key_two, key_three = jax.random.split(key, 3)
    field_pick = jax.random.randint(key_one, (SUBWIN, NOBS), 0, 3)
    row_pick = jax.random.randint(key_two, (SUBWIN, NOBS), 0, LAT)
    column = jax.random.randint(key_three, (SUBWIN, NOBS), 0, LON_DEV)
    flat_index = (field_pick * LAT + row_pick) * LON_DEV + column
    flat_index = flat_index.at[:, 0].set(0)
    flat_index = flat_index.at[:, NOBS - 1].set(3 * LAT * LON_DEV - 1)
    return flat_index.astype(jnp.int32)


def levels(rng, shape, cuts, smallest, largest):
    factor_of = 1.0
    for axis_at, shards_of in cuts:
        steps = jax.random.uniform(jax.random.fold_in(jax.random.fold_in(rng, 6), axis_at), (shards_of,), jnp.float32, smallest / len(cuts), largest / len(cuts))
        factor_of = factor_of * jnp.repeat(jnp.exp(steps), shape[axis_at] // shards_of).reshape((-1,) + (1,) * (len(shape) - 1 - axis_at))
    return factor_of


def centred(rng, dims, width, reach, pieces=(), kind=jnp.bfloat16):
    gain = levels(rng, dims, pieces, -0.22, 0.18) if pieces else 1.0
    values = jax.random.normal(rng, dims, jnp.float32) * width * gain
    return jnp.minimum(jnp.maximum(values, -reach), reach).astype(kind)


def setup_inputs(seed: int = 0) -> dict:
    keys = jax.random.split(jax.random.key(seed), 8)
    rhs_state = draw_rhs_state(jax.random.fold_in(keys[7], 71), 0)
    innovations = centred(keys[1], (SUBWIN, NOBS), 1.0, 6.0, ((0, 4), (1, 8)), jnp.float32)
    trajectory = draw_trajectory(jax.random.fold_in(keys[7], 71), 0)
    model_var = jnp.clip(jnp.exp(math.log(2.0) - 2.3025851 * jax.random.uniform(keys[3], (SUBWIN, 3, LAT, NLON), jnp.float32) ** levels(keys[3], (SUBWIN, 3, LAT, NLON), ((0, 4), (3, 8)), -0.2, 0.2)), 0.2, 2.0)
    obs_var = jnp.clip(jnp.exp(math.log(2.0) - 2.3025851 * jax.random.uniform(keys[4], (SUBWIN, NOBS), jnp.float32) ** levels(keys[4], (SUBWIN, NOBS), ((0, 4), (1, 8)), -0.2, 0.2)), 0.2, 2.0)
    obs_index = draw_obs_index(jax.random.fold_in(keys[7], 71), 0)
    control_rhs = draw_control_rhs(jax.random.fold_in(keys[7], 71), 0)
    return {"rhs_state": rhs_state, "innovations": innovations, "trajectory": trajectory, "model_var": model_var, "obs_var": obs_var, "obs_index": obs_index, "control_rhs": control_rhs}


courant = 0.25
coriolis = 0.2

def coriolis_rows(rows):
    position = jnp.arange(rows, dtype=jnp.float32)
    return (coriolis * ((2.0 * position + 1.0) / rows - 1.0))[:, None]

def periodic_x(field):
    return 0.5 * (jnp.roll(field, -1, axis=2) - jnp.roll(field, 1, axis=2))

def walled_y(field):
    padded = jnp.pad(field, ((0, 0), (1, 1), (0, 0)))
    return 0.5 * (padded[:, 2:, :] - padded[:, :-2, :])

def tangent_step(current, x_diffs, traj_step, rotation):
    mean_depth = traj_step[0].astype(jnp.float32)
    mean_east = traj_step[1].astype(jnp.float32)
    mean_north = traj_step[2].astype(jnp.float32)
    y_diffs = walled_y(current)
    height = current[0]
    east_wind = current[1]
    north_wind = current[2]
    new_height = height - courant * (mean_depth * (x_diffs[1] + y_diffs[2]) + mean_east * x_diffs[0] + mean_north * y_diffs[0])
    new_east = east_wind - courant * (x_diffs[0] + mean_east * x_diffs[1] + mean_north * y_diffs[1]) + rotation * north_wind
    new_north = north_wind - courant * (y_diffs[0] + mean_east * x_diffs[2] + mean_north * y_diffs[2]) - rotation * east_wind
    return jnp.stack([new_height, new_east, new_north])

def east_fluxes(adjoint, traj_step):
    mean_depth = traj_step[0].astype(jnp.float32)
    mean_east = traj_step[1].astype(jnp.float32)
    return jnp.stack([mean_east * adjoint[0] + adjoint[1], mean_depth * adjoint[0] + mean_east * adjoint[1], mean_east * adjoint[2]])

def north_fluxes(adjoint, traj_step):
    mean_depth = traj_step[0].astype(jnp.float32)
    mean_north = traj_step[2].astype(jnp.float32)
    return jnp.stack([mean_north * adjoint[0] + adjoint[2], mean_north * adjoint[1], mean_depth * adjoint[0] + mean_north * adjoint[2]])

def adjoint_step(adjoint, x_diffs, traj_step, rotation):
    y_diffs = walled_y(north_fluxes(adjoint, traj_step))
    new_height = adjoint[0] + courant * (x_diffs[0] + y_diffs[0])
    new_east = adjoint[1] + courant * (x_diffs[1] + y_diffs[1]) - rotation * adjoint[2]
    new_north = adjoint[2] + courant * (x_diffs[2] + y_diffs[2]) + rotation * adjoint[1]
    return jnp.stack([new_height, new_east, new_north])

def forward_run(increment, traj_sub):
    rotation = coriolis_rows(increment.shape[1])
    current = increment
    for step_number in range(traj_sub.shape[0]):
        current = tangent_step(current, periodic_x(current), traj_sub[step_number], rotation)
    return current

def backward_run(adjoint, traj_sub):
    rotation = coriolis_rows(adjoint.shape[1])
    for step_number in reversed(range(traj_sub.shape[0])):
        fluxes = periodic_x(east_fluxes(adjoint, traj_sub[step_number]))
        adjoint = adjoint_step(adjoint, fluxes, traj_sub[step_number], rotation)
    return adjoint

def global_index(obs_index, full_lon):
    band_width = LON_DEV
    position = jnp.arange(obs_index.shape[1], dtype=jnp.int32)
    band_pick = (position // OBS_DEV).astype(jnp.int32)
    plane = (obs_index // band_width).astype(jnp.int32)
    column = (obs_index % band_width).astype(jnp.int32)
    return (plane * full_lon + band_pick[None, :] * band_width + column).astype(jnp.int32)

def apply_saddle(vector, trajectory, model_var, obs_var, flat_index):
    multiplier, obs_dual, increment = vector
    count = increment.shape[0]
    advanced = lax.map(lambda pair: forward_run(pair[0], pair[1]), (increment, trajectory))
    earlier = jnp.concatenate([jnp.zeros_like(advanced[:1]), advanced[:-1]], axis=0)
    later = jnp.concatenate([multiplier[1:], jnp.zeros_like(multiplier[:1])], axis=0)
    pulled = lax.map(lambda pair: backward_run(pair[0], pair[1]), (later, trajectory))
    flat = increment.reshape(count, -1)
    observed = jnp.take_along_axis(flat, flat_index, axis=1)
    cells = flat.shape[1]
    spread = jax.vmap(lambda where, values: jnp.zeros((cells,), jnp.float32).at[where].add(values))(flat_index, obs_dual)
    row_one = model_var * multiplier + increment - earlier
    row_two = obs_var * obs_dual + observed
    row_three = multiplier - pulled + spread.reshape(increment.shape)
    return (row_one, row_two, row_three)

def precondition(vector, model_var, obs_var):
    return (vector[2], vector[1] / obs_var, vector[0] - model_var * vector[2])

def inner_product(first_vec, second_vec):
    return jnp.sum(first_vec[0] * second_vec[0]) + jnp.sum(first_vec[1] * second_vec[1]) + jnp.sum(first_vec[2] * second_vec[2])

def scaled(vector, factor):
    return tuple((block * factor for block in vector))

def minus_scaled(vector, other, factor):
    return tuple((block - factor * piece for block, piece in zip(vector, other)))

def reference(rhs_state, innovations, trajectory, model_var, obs_var, obs_index, control_rhs):
    flat_index = global_index(obs_index, rhs_state.shape[3])
    start = (rhs_state, innovations, control_rhs)
    beta = jnp.sqrt(inner_product(start, start))
    basis_zero = scaled(start, 1.0 / beta)
    precond_zero = precondition(basis_zero, model_var, obs_var)
    image = apply_saddle(precond_zero, trajectory, model_var, obs_var, flat_index)
    diag_first = inner_product(basis_zero, image)
    image = minus_scaled(image, basis_zero, diag_first)
    below_first = jnp.sqrt(inner_product(image, image))
    basis_one = scaled(image, 1.0 / below_first)
    precond_one = precondition(basis_one, model_var, obs_var)
    image = apply_saddle(precond_one, trajectory, model_var, obs_var, flat_index)
    upper_second = inner_product(basis_zero, image)
    diag_second = inner_product(basis_one, image)
    image = minus_scaled(image, basis_zero, upper_second)
    image = minus_scaled(image, basis_one, diag_second)
    below_second = jnp.sqrt(inner_product(image, image))
    gram_zero = diag_first * diag_first + below_first * below_first
    gram_cross = diag_first * upper_second + below_first * diag_second
    gram_one = upper_second * upper_second + diag_second * diag_second + below_second * below_second
    target_zero = beta * diag_first
    target_one = beta * upper_second
    determinant = gram_zero * gram_one - gram_cross * gram_cross
    weight_zero = (gram_one * target_zero - gram_cross * target_one) / determinant
    weight_one = (gram_zero * target_one - gram_cross * target_zero) / determinant
    result = tuple((block_a * weight_zero + block_b * weight_one for block_a, block_b in zip(precond_zero, precond_one)))
    return (result[0], result[1], result[2])
```

```python
import jax
import jax.numpy as jnp
from jax import lax
from jax.sharding import PartitionSpec as P

courant = 0.25
coriolis = 0.2


def passed_along(block, axis, distance):
    devices = range(lax.axis_size(axis))
    route = [(i - distance, i) for i in devices if i - distance in devices]
    return lax.ppermute(block, axis, route)


def with_halo(shard, sides, width):
    for axis, dim in sides:
        peers, length = (lax.axis_size(axis), shard.shape[dim])
        up = [(i, (i + 1) % peers) for i in range(peers)]
        down = [(j, i) for i, j in up]
        last = lax.slice_in_dim(shard, length - width, length, axis=dim)
        first = lax.slice_in_dim(shard, 0, width, axis=dim)
        before = lax.ppermute(last, axis, up)
        after = lax.ppermute(first, axis, down)
        shard = jnp.concatenate([before, shard, after], axis=dim)
    return shard


def coriolis_rows(rows):
    position = jnp.arange(rows, dtype=jnp.float32)
    return (coriolis * ((2.0 * position + 1.0) / rows - 1.0))[:, None]


def centered_x(extended):
    return 0.5 * (extended[:, :, 2:] - extended[:, :, :-2])


def walled_y(field):
    padded = jnp.pad(field, ((0, 0), (1, 1), (0, 0)))
    return 0.5 * (padded[:, 2:, :] - padded[:, :-2, :])


def tangent_step(current, x_diffs, traj_step, rotation):
    mean_depth = traj_step[0].astype(jnp.float32)
    mean_east = traj_step[1].astype(jnp.float32)
    mean_north = traj_step[2].astype(jnp.float32)
    y_diffs = walled_y(current)
    height = current[0]
    east_wind = current[1]
    north_wind = current[2]
    new_height = height - courant * (
        mean_depth * (x_diffs[1] + y_diffs[2]) + mean_east * x_diffs[0] + mean_north * y_diffs[0]
    )
    new_east = (
        east_wind
        - courant * (x_diffs[0] + mean_east * x_diffs[1] + mean_north * y_diffs[1])
        + rotation * north_wind
    )
    new_north = (
        north_wind
        - courant * (y_diffs[0] + mean_east * x_diffs[2] + mean_north * y_diffs[2])
        - rotation * east_wind
    )
    return jnp.stack([new_height, new_east, new_north])


def east_fluxes(adjoint, traj_step):
    mean_depth = traj_step[0].astype(jnp.float32)
    mean_east = traj_step[1].astype(jnp.float32)
    return jnp.stack(
        [
            mean_east * adjoint[0] + adjoint[1],
            mean_depth * adjoint[0] + mean_east * adjoint[1],
            mean_east * adjoint[2],
        ]
    )


def north_fluxes(adjoint, traj_step):
    mean_depth = traj_step[0].astype(jnp.float32)
    mean_north = traj_step[2].astype(jnp.float32)
    return jnp.stack(
        [
            mean_north * adjoint[0] + adjoint[2],
            mean_north * adjoint[1],
            mean_depth * adjoint[0] + mean_north * adjoint[2],
        ]
    )


def adjoint_step(adjoint, x_diffs, traj_step, rotation):
    y_diffs = walled_y(north_fluxes(adjoint, traj_step))
    new_height = adjoint[0] + courant * (x_diffs[0] + y_diffs[0])
    new_east = adjoint[1] + courant * (x_diffs[1] + y_diffs[1]) - rotation * adjoint[2]
    new_north = adjoint[2] + courant * (x_diffs[2] + y_diffs[2]) + rotation * adjoint[1]
    return jnp.stack([new_height, new_east, new_north])


def shifted(vector, traj_dev, model_part, obs_part, local_index, rotation):
    first, middle, last = vector
    increment = first - model_part * last
    obs_dual = middle / obs_part
    steps_total = traj_dev.shape[0]
    later = passed_along(last, "tm", -1)
    current = increment
    adjoint = later
    for step_number in range(steps_total):
        extended = with_halo(current, (("lon", 2),), 1)
        current = tangent_step(current, centered_x(extended), traj_dev[step_number], rotation)
    for step_number in reversed(range(steps_total)):
        fluxes = east_fluxes(adjoint, traj_dev[step_number])
        extended = with_halo(fluxes, (("lon", 2),), 1)
        adjoint = adjoint_step(adjoint, centered_x(extended), traj_dev[step_number], rotation)
    earlier = passed_along(current, "tm", 1)
    flat_inc = increment.reshape(-1)
    observed = flat_inc[local_index]
    spread = jnp.zeros_like(flat_inc).at[local_index].add(obs_dual).reshape(increment.shape)
    return (-earlier, observed, spread - adjoint)


def local_product(first_vec, second_vec):
    return (
        jnp.sum(first_vec[0] * second_vec[0])
        + jnp.sum(first_vec[1] * second_vec[1])
        + jnp.sum(first_vec[2] * second_vec[2])
    )


def mesh_sums(values):
    axes = ("tm", "lon")
    count = lax.axis_size("tm") * lax.axis_size("lon")
    row = jnp.zeros((128,), jnp.float32)
    for position, value in enumerate(values):
        row = row.at[position].set(value)
    sent = jnp.broadcast_to(row, (count, 8, 128))
    received = lax.all_to_all(sent, axes, 0, 0)
    total = jnp.sum(received[:, 0, :], axis=0)
    return [total[position] for position in range(len(values))]


def weights(s00, s01, s02, s11, s12, s22):
    alpha = s01 / s00
    t11 = s11 - alpha * s01
    along = (s12 - alpha * s02) / t11
    beta = jnp.sqrt(s00)
    gamma = 1.0 / jnp.sqrt(t11)
    h00 = 1.0 + alpha
    h10_square = t11 / s00
    h10 = jnp.sqrt(h10_square)
    h01 = (s02 - alpha * s01) * gamma / beta
    h11 = 1.0 - alpha + along
    h21_square = (s22 - s02 * (s02 / s00) - along * (s12 - alpha * s02)) / t11
    g00 = h00 * h00 + h10_square
    g01 = h00 * h01 + h10 * h11
    g11 = h01 * h01 + h11 * h11 + h21_square
    q0 = beta * h00
    q1 = beta * h01
    det = g00 * g11 - g01 * g01
    y0 = (g11 * q0 - g01 * q1) / det
    y1 = (g00 * q1 - g01 * q0) / det
    c1 = y1 * gamma
    return (y0 / beta - c1 * alpha, c1)


def shards(rhs_state, innovations, trajectory, model_var, obs_var, obs_index, control_rhs):
    local_index = obs_index[0]
    rotation = coriolis_rows(rhs_state.shape[2])
    traj_dev = trajectory[0]
    model_part = model_var[0]
    obs_part = obs_var[0]
    b0 = (rhs_state[0], innovations[0], control_rhs[0])
    b1 = shifted(b0, traj_dev, model_part, obs_part, local_index, rotation)
    b2 = shifted(b1, traj_dev, model_part, obs_part, local_index, rotation)
    c0, c1 = weights(
        *mesh_sums(
            [
                local_product(b0, b0),
                local_product(b0, b1),
                local_product(b0, b2),
                local_product(b1, b1),
                local_product(b1, b2),
                local_product(b2, b2),
            ]
        )
    )
    first, middle, last = (c0 * p + c1 * q for p, q in zip(b0, b1))
    return (last[None], (middle / obs_part)[None], (first - model_part * last)[None])


def solution(mesh):
    in_specs = (
        P("tm", None, None, "lon"),
        P("tm", "lon"),
        P("tm", None, None, None, "lon"),
        P("tm", None, None, "lon"),
        P("tm", "lon"),
        P("tm", "lon"),
        P("tm", None, None, "lon"),
    )
    out_specs = (P("tm", None, None, "lon"), P("tm", "lon"), P("tm", None, None, "lon"))
    return jax.shard_map(shards, mesh=mesh, in_specs=in_specs, out_specs=out_specs, check_vma=False)
```

```python
import functools

import jax
import jax.numpy as jnp
from jax import lax
from jax.experimental import pallas as pl
from jax.experimental.pallas import tpu as pltpu
from jax.sharding import PartitionSpec as P

courant = 0.25
coriolis = 0.2
slope = 0.5 * courant

LANE = 128
GROUP = 16
MARGIN = 8
HALO = 4
TRAJ, INC, VAR, LAST, PLANES = 0, 6, 9, 12, 16
F32 = jnp.float32
PARAMS = pltpu.CompilerParams(vmem_limit_bytes=56 * 1024 * 1024)


def iota(shape, dim):
    return lax.broadcasted_iota(jnp.int32, shape, dim)


def spread_shift(plane):
    return (LANE - (8 * plane + HALO)) % LANE


def pack_shift(plane):
    return (8 * plane + HALO) % LANE


def edges_of(planes, rows):
    lane = iota((rows, LANE), 1)
    packed = jnp.zeros((rows, LANE), F32)
    for number, plane in enumerate(planes):
        both = jnp.where(lane < LANE // 2, plane[:, :LANE], plane[:, LANE:])
        packed = jnp.where(lane // 8 == number, pltpu.roll(both, pack_shift(number), 1), packed)
    return packed


def split_edges(turned, to_right, to_left, count):
    top = iota((8, turned.shape[1]), 0) < HALO
    for pair in range(count // 2):
        even = turned[16 * pair : 16 * pair + 8]
        odd = turned[16 * pair + 8 : 16 * pair + 16]
        to_right[8 * pair : 8 * pair + 8, :] = jnp.where(top, even, pltpu.roll(odd, HALO, 0))
        to_left[8 * pair : 8 * pair + 8, :] = jnp.where(top, pltpu.roll(even, HALO, 0), odd)


def joined_edges(from_left, from_right, count):
    top = iota((8, from_left.shape[1]), 0) < HALO
    pieces = []
    for pair in range(count // 2):
        left = from_left[8 * pair : 8 * pair + 8]
        right = from_right[8 * pair : 8 * pair + 8]
        pieces.append(jnp.where(top, left, pltpu.roll(right, HALO, 0)))
        pieces.append(jnp.where(top, pltpu.roll(left, HALO, 0), right))
    return jnp.concatenate(pieces, axis=0)


def padded_turn(message):
    rest = LANE - message.shape[0]
    if rest:
        message = jnp.concatenate([message, jnp.zeros((rest, message.shape[1]), F32)], axis=0)
    return message.T


def edges_kernel(first, last, variance, traj, to_right, to_left, increment):
    rows = first.shape[1]
    planes = [traj[p].astype(F32) for p in range(6)]
    for f in range(3):
        value = first[f] - variance[f] * last[f]
        increment[f] = value
        planes.append(value)
    planes += [variance[f] for f in range(3)]
    planes += [last[f] for f in range(3)]
    split_edges(edges_of(planes, rows).T, to_right, to_left, PLANES)


def edges_call(first, last, variance, traj):
    rows = first.shape[1]
    block = pl.BlockSpec((3, LANE, 2 * LANE), lambda i: (0, i, 0))
    sent = pl.BlockSpec((PLANES * HALO, LANE), lambda i: (0, i))
    return pl.pallas_call(
        edges_kernel,
        grid=(rows // LANE,),
        in_specs=[block, block, block, pl.BlockSpec((6, LANE, 2 * LANE), lambda i: (0, i, 0))],
        out_specs=[sent, sent, block],
        out_shape=[jax.ShapeDtypeStruct((PLANES * HALO, rows), F32)] * 2
        + [jax.ShapeDtypeStruct(first.shape, F32)],
        compiler_params=PARAMS,
        cost_estimate=pl.CostEstimate(flops=10**6, bytes_accessed=16 * 2**20, transcendentals=0),
        name="edges",
    )(first, last, variance, traj)


def spread_edges_kernel(spread, to_right, to_left):
    planes = [spread[f] for f in range(3)]
    split_edges(edges_of(planes, spread.shape[1]).T, to_right, to_left, 4)


def spread_edges_call(spread):
    rows = spread.shape[1]
    sent = pl.BlockSpec((16, LANE), lambda i: (0, i))
    return pl.pallas_call(
        spread_edges_kernel,
        grid=(rows // LANE,),
        in_specs=[pl.BlockSpec((3, LANE, 2 * LANE), lambda i: (0, i, 0))],
        out_specs=[sent, sent],
        out_shape=[jax.ShapeDtypeStruct((16, rows), F32)] * 2,
        compiler_params=PARAMS,
        cost_estimate=pl.CostEstimate(flops=10**6, bytes_accessed=3 * 2**20, transcendentals=0),
        name="spread_edges",
    )(spread)


def x_differences(tiles, first_lane, last_lane):
    ahead = [pltpu.roll(t, LANE - 1, 1) for t in tiles]
    behind = [pltpu.roll(t, 1, 1) for t in tiles]
    return [
        jnp.where(last_lane, ahead[(t + 1) % 3], ahead[t])
        - jnp.where(first_lane, behind[(t - 1) % 3], behind[t])
        for t in range(3)
    ]


def rotation_at(start, total):
    position = (iota((GROUP, LANE), 0) + start).astype(F32)
    return coriolis * ((2.0 * position + 1.0) / total - 1.0)


def lane_ends():
    lane = iota((GROUP, LANE), 1)
    return lane == 0, lane == LANE - 1


def traj_tiles(traj, packed_ref, step, start):
    packed = packed_ref[pl.ds(start, GROUP), :]
    out = []
    for field in range(3):
        plane = 3 * step + field
        out.append(
            [traj[plane, pl.ds(start, GROUP), t * LANE : (t + 1) * LANE].astype(F32) for t in range(2)]
            + [pltpu.roll(packed, spread_shift(TRAJ + plane), 1)]
        )
    return out


def load_rows(ref, start, offset):
    return [[ref[f, t, pl.ds(start + (MARGIN + offset), GROUP), :] for t in range(3)] for f in range(3)]


def store_rows(ref, start, value):
    for f in range(3):
        for t in range(3):
            ref[f, t, pl.ds(start + MARGIN, GROUP), :] = value[f][t]


def clear_margins(ref):
    rows = ref.shape[2]
    zero = jnp.zeros((MARGIN, LANE), F32)
    for f in range(3):
        for t in range(3):
            ref[f, t, 0:MARGIN, :] = zero
            ref[f, t, rows - MARGIN : rows, :] = zero


def tangent_rows(source, traj, packed_ref, step, start, total):
    here, above, below = (load_rows(source, start, k) for k in (0, 1, -1))
    trajectory = traj_tiles(traj, packed_ref, step, start)
    turn = rotation_at(start, total)
    ends = lane_ends()
    dx = [x_differences(here[f], *ends) for f in range(3)]
    new = [[], [], []]
    for t in range(3):
        b, e, n = (trajectory[f][t] for f in range(3))
        h, u, v = (here[f][t] for f in range(3))
        xh, xu, xv = (dx[f][t] for f in range(3))
        yh, yu, yv = (above[f][t] - below[f][t] for f in range(3))
        new[0].append(h - slope * (b * (xu + yv) + e * xh + n * yh))
        new[1].append(u - slope * (xh + e * xu + n * yu) + turn * v)
        new[2].append(v - slope * (yh + e * xv + n * yv) - turn * u)
    return new


def north_rows(field, trajectory):
    out = [[], [], []]
    for t in range(3):
        b, _, n = (trajectory[f][t] for f in range(3))
        p, q, w = (field[f][t] for f in range(3))
        out[0].append(n * p + w)
        out[1].append(n * q)
        out[2].append(b * p + n * w)
    return out


def adjoint_rows(source, flux, traj, packed_ref, step, start, total):
    here = load_rows(source, start, 0)
    above, below = (load_rows(flux, start, k) for k in (1, -1))
    trajectory = traj_tiles(traj, packed_ref, step, start)
    turn = rotation_at(start, total)
    ends = lane_ends()
    east = [[], [], []]
    for t in range(3):
        b, e, _ = (trajectory[f][t] for f in range(3))
        p, q, w = (here[f][t] for f in range(3))
        east[0].append(e * p + q)
        east[1].append(b * p + e * q)
        east[2].append(e * w)
    dx = [x_differences(east[f], *ends) for f in range(3)]
    new = [[], [], []]
    for t in range(3):
        p, q, w = (here[f][t] for f in range(3))
        change = [slope * (dx[f][t] + (above[f][t] - below[f][t])) for f in range(3)]
        new[0].append(p + change[0])
        new[1].append(q + change[1] - turn * w)
        new[2].append(w + change[2] + turn * q)
    return new


def over_rows(total, body):
    def step(i, carry):
        body(pl.multiple_of(i * GROUP, GROUP))
        return carry

    lax.fori_loop(0, total // GROUP, step, 0)


def turn_in(message, packed_ref):
    for j in range(message.shape[1] // LANE):
        packed_ref[j * LANE : (j + 1) * LANE, :] = padded_turn(message[:, j * LANE : (j + 1) * LANE])


def turn_out(packed_ref, message):
    for j in range(message.shape[1] // LANE):
        turned = packed_ref[j * LANE : (j + 1) * LANE, :].T
        message[:, j * LANE : (j + 1) * LANE] = turned[: message.shape[0]]


def pack_three(halo_tiles):
    lane = iota((GROUP, LANE), 1) // 8
    packed = jnp.zeros((GROUP, LANE), F32)
    for f in range(3):
        packed = jnp.where(lane == f, pltpu.roll(halo_tiles[f], pack_shift(f), 1), packed)
    return packed


def wide_scratch(rows):
    return pltpu.VMEM((3, 3, rows + 2 * MARGIN, LANE), F32)


def tile_of(ref, f, start, t):
    return ref[f, pl.ds(start, GROUP), t * LANE : (t + 1) * LANE]


def set_tile(ref, f, start, t, value):
    ref[f, pl.ds(start, GROUP), t * LANE : (t + 1) * LANE] = value


def run_tangent(get, traj, packed_ref, wide_a, wide_b, total, put):
    clear_margins(wide_a)
    clear_margins(wide_b)
    over_rows(total, lambda s: store_rows(wide_a, s, get(s)))
    over_rows(
        total, lambda s: store_rows(wide_b, s, tangent_rows(wide_a, traj, packed_ref, 0, s, total))
    )
    over_rows(total, lambda s: put(s, tangent_rows(wide_b, traj, packed_ref, 1, s, total)))


def run_adjoint(get, traj, packed_ref, wide_a, wide_b, flux_a, flux_b, total, put):
    clear_margins(flux_a)
    clear_margins(flux_b)

    def begin(s):
        field = get(s)
        store_rows(wide_a, s, field)
        store_rows(flux_a, s, north_rows(field, traj_tiles(traj, packed_ref, 1, s)))

    def middle(s):
        field = adjoint_rows(wide_a, flux_a, traj, packed_ref, 1, s, total)
        store_rows(wide_b, s, field)
        store_rows(flux_b, s, north_rows(field, traj_tiles(traj, packed_ref, 0, s)))

    over_rows(total, begin)
    over_rows(total, middle)
    over_rows(total, lambda s: put(s, adjoint_rows(wide_b, flux_b, traj, packed_ref, 0, s, total)))


def tangent_first_kernel(
    increment, traj, from_left, from_right, ahead, ahead_edges, packed, last_edges, wide_a, wide_b, own
):
    total = increment.shape[1]
    for j in range(total // LANE):
        cut = slice(j * LANE, (j + 1) * LANE)
        joined = joined_edges(from_left[:, cut], from_right[:, cut], PLANES)
        last_edges[:, cut] = joined[8 * LAST : 8 * LAST + 24]
        packed[cut, :] = joined.T

    def get(s):
        lanes = packed[pl.ds(s, GROUP), :]
        return [
            [tile_of(increment, f, s, 0), tile_of(increment, f, s, 1), pltpu.roll(lanes, spread_shift(INC + f), 1)]
            for f in range(3)
        ]

    def put(s, new):
        for f in range(3):
            for t in range(2):
                set_tile(ahead, f, s, t, -new[f][t])
        own[pl.ds(s, GROUP), :] = pack_three([-new[f][2] for f in range(3)])

    run_tangent(get, traj, packed, wide_a, wide_b, total, put)
    turn_out(own, ahead_edges)


def whole(count):
    return [pl.BlockSpec(memory_space=pltpu.VMEM)] * count


def cost(mib, steps=2):
    return pl.CostEstimate(flops=steps * 40 * 2**20, bytes_accessed=mib * 2**20, transcendentals=0)


def tangent_first(increment, traj, from_left, from_right):
    rows = increment.shape[1]
    return pl.pallas_call(
        tangent_first_kernel,
        in_specs=whole(4),
        out_specs=whole(4),
        out_shape=[
            jax.ShapeDtypeStruct(increment.shape, F32),
            jax.ShapeDtypeStruct((24, rows), F32),
            jax.ShapeDtypeStruct((rows, LANE), F32),
            jax.ShapeDtypeStruct((24, rows), F32),
        ],
        scratch_shapes=[wide_scratch(rows)] * 2 + [pltpu.VMEM((rows, LANE), F32)],
        compiler_params=PARAMS,
        cost_estimate=cost(10),
        name="tangent_first",
    )(increment, traj, from_left, from_right)


def adjoint_first_kernel(
    later, later_edges, traj, packed, spread, z_left, z_right, pulled, pulled_edges,
    wide_a, wide_b, flux_a, flux_b, own, z_own,
):
    total = later.shape[1]
    turn_in(later_edges, own)
    for j in range(total // LANE):
        cut = slice(j * LANE, (j + 1) * LANE)
        z_own[cut, :] = padded_turn(joined_edges(z_left[:, cut], z_right[:, cut], 4))

    def get(s):
        lanes = own[pl.ds(s, GROUP), :]
        return [
            [tile_of(later, f, s, 0), tile_of(later, f, s, 1), pltpu.roll(lanes, spread_shift(f), 1)]
            for f in range(3)
        ]

    def put(s, new):
        lanes = z_own[pl.ds(s, GROUP), :]
        halo = []
        for f in range(3):
            for t in range(2):
                set_tile(pulled, f, s, t, tile_of(spread, f, s, t) - new[f][t])
            halo.append(pltpu.roll(lanes, spread_shift(f), 1) - new[f][2])
        own[pl.ds(s, GROUP), :] = pack_three(halo)

    run_adjoint(get, traj, packed, wide_a, wide_b, flux_a, flux_b, total, put)
    turn_out(own, pulled_edges)


def adjoint_first(later, later_edges, traj, packed, spread, z_left, z_right):
    rows = later.shape[1]
    return pl.pallas_call(
        adjoint_first_kernel,
        in_specs=whole(7),
        out_specs=whole(2),
        out_shape=[jax.ShapeDtypeStruct(later.shape, F32), jax.ShapeDtypeStruct((24, rows), F32)],
        scratch_shapes=[wide_scratch(rows)] * 4 + [pltpu.VMEM((rows, LANE), F32)] * 2,
        compiler_params=PARAMS,
        cost_estimate=cost(13),
        name="adjoint_first",
    )(later, later_edges, traj, packed, spread, z_left, z_right)


def tangent_second_kernel(
    earlier, earlier_edges, pulled, pulled_edges, variance, traj, packed, increment, ahead, wide_a, wide_b, e_own, p_own
):
    total = earlier.shape[1]
    turn_in(earlier_edges, e_own)
    turn_in(pulled_edges, p_own)

    def get(s):
        e_lanes = e_own[pl.ds(s, GROUP), :]
        p_lanes = p_own[pl.ds(s, GROUP), :]
        v_lanes = packed[pl.ds(s, GROUP), :]
        out = []
        for f in range(3):
            tiles = [tile_of(earlier, f, s, t) - tile_of(variance, f, s, t) * tile_of(pulled, f, s, t) for t in range(2)]
            for t in range(2):
                set_tile(increment, f, s, t, tiles[t])
            shift = spread_shift(f)
            tiles.append(
                pltpu.roll(e_lanes, shift, 1)
                - pltpu.roll(v_lanes, spread_shift(VAR + f), 1) * pltpu.roll(p_lanes, shift, 1)
            )
            out.append(tiles)
        return out

    def put(s, new):
        for f in range(3):
            for t in range(2):
                set_tile(ahead, f, s, t, -new[f][t])

    run_tangent(get, traj, packed, wide_a, wide_b, total, put)


def tangent_second(earlier, earlier_edges, pulled, pulled_edges, variance, traj, packed):
    rows = earlier.shape[1]
    return pl.pallas_call(
        tangent_second_kernel,
        in_specs=whole(7),
        out_specs=whole(2),
        out_shape=[jax.ShapeDtypeStruct(earlier.shape, F32)] * 2,
        scratch_shapes=[wide_scratch(rows)] * 2 + [pltpu.VMEM((rows, LANE), F32)] * 2,
        compiler_params=PARAMS,
        cost_estimate=cost(18),
        name="tangent_second",
    )(earlier, earlier_edges, pulled, pulled_edges, variance, traj, packed)


def adjoint_second_kernel(
    later, later_edges, traj, packed, spread, last, pulled, sums, wide_a, wide_b, flux_a, flux_b, own
):
    total = later.shape[1]
    turn_in(later_edges, own)
    sums[...] = jnp.zeros_like(sums)

    def get(s):
        lanes = own[pl.ds(s, GROUP), :]
        return [
            [tile_of(later, f, s, 0), tile_of(later, f, s, 1), pltpu.roll(lanes, spread_shift(f), 1)]
            for f in range(3)
        ]

    def put(s, new):
        parts = [jnp.zeros((GROUP, LANE), F32)] * 3
        for f in range(3):
            for t in range(2):
                value = tile_of(spread, f, s, t) - new[f][t]
                for k, other in enumerate((tile_of(last, f, s, t), tile_of(pulled, f, s, t), value)):
                    parts[k] = parts[k] + other * value
        for k in range(3):
            sums[k] = sums[k] + parts[k]

    run_adjoint(get, traj, packed, wide_a, wide_b, flux_a, flux_b, total, put)


def adjoint_second(later, later_edges, traj, packed, spread, last, pulled):
    rows = later.shape[1]
    return pl.pallas_call(
        adjoint_second_kernel,
        in_specs=whole(7),
        out_specs=pl.BlockSpec(memory_space=pltpu.VMEM),
        out_shape=jax.ShapeDtypeStruct((3, GROUP, LANE), F32),
        scratch_shapes=[wide_scratch(rows)] * 4 + [pltpu.VMEM((rows, LANE), F32)],
        compiler_params=PARAMS,
        cost_estimate=cost(16),
        name="adjoint_second",
    )(later, later_edges, traj, packed, spread, last, pulled)


def products_kernel(pairs, *refs):
    arrays, sums = refs[:-1], refs[-1]

    @pl.when(pl.program_id(0) == 0)
    def _():
        sums[...] = jnp.zeros_like(sums)

    for k, (i, j) in enumerate(pairs):
        product = arrays[i][...] * arrays[j][...]
        sums[k] = sums[k] + jnp.sum(product.reshape(-1, 8, product.shape[-1]), axis=0)


def products(pairs, arrays):
    rows = arrays[0].shape[1]
    block = pl.BlockSpec((3, LANE, 2 * LANE), lambda i: (0, i, 0))
    return pl.pallas_call(
        functools.partial(products_kernel, pairs),
        grid=(rows // LANE,),
        in_specs=[block] * len(arrays),
        out_specs=pl.BlockSpec((len(pairs), 8, 2 * LANE), lambda i: (0, 0, 0)),
        out_shape=jax.ShapeDtypeStruct((len(pairs), 8, 2 * LANE), F32),
        compiler_params=PARAMS,
        cost_estimate=cost(3 * len(arrays), 1),
        name="products",
    )(*arrays)


def mesh_sums(row):
    count = lax.axis_size("tm") * lax.axis_size("lon")
    sent = jnp.broadcast_to(row, (count, 8, LANE))
    received = lax.all_to_all(sent, ("tm", "lon"), 0, 0)
    return jnp.sum(received[:, 0, :], axis=0)


def weights(s00, s01, s02, s11, s12, s22):
    alpha = s01 / s00
    t11 = s11 - alpha * s01
    along = (s12 - alpha * s02) / t11
    beta = jnp.sqrt(s00)
    gamma = 1.0 / jnp.sqrt(t11)
    h00 = 1.0 + alpha
    h10_square = t11 / s00
    h10 = jnp.sqrt(h10_square)
    h01 = (s02 - alpha * s01) * gamma / beta
    h11 = 1.0 - alpha + along
    h21_square = (s22 - s02 * (s02 / s00) - along * (s12 - alpha * s02)) / t11
    g00 = h00 * h00 + h10_square
    g01 = h00 * h01 + h10 * h11
    g11 = h01 * h01 + h11 * h11 + h21_square
    q0 = beta * h00
    q1 = beta * h01
    det = g00 * g11 - g01 * g01
    y0 = (g11 * q0 - g01 * q1) / det
    y1 = (g00 * q1 - g01 * q0) / det
    c1 = y1 * gamma
    return (y0 / beta - c1 * alpha, c1)


def moved(block, axis, distance, wrap):
    size = lax.axis_size(axis)
    if wrap:
        route = [(i, (i + distance) % size) for i in range(size)]
    else:
        route = [(i, i + distance) for i in range(size) if 0 <= i + distance < size]
    return lax.ppermute(block, axis, route)


def shards(rhs_state, innovations, trajectory, model_var, obs_var, obs_index, control_rhs):
    rows, columns = rhs_state.shape[2:]
    first, last, variance = rhs_state[0], control_rhs[0], model_var[0]
    traj = trajectory.reshape(-1, rows, columns)
    middle, obs_part, where = innovations[0], obs_var[0], obs_index[0]

    def observed(field):
        return field.reshape(-1)[where]

    def spread(values):
        flat = jnp.zeros((3 * rows * columns,), F32).at[where].add(values / obs_part)
        return flat.reshape(3, rows, columns)

    later = moved(last, "tm", -1, False)
    to_right, to_left, inc0 = edges_call(first, last, variance, traj)
    from_left = moved(to_right, "lon", 1, True)
    from_right = moved(to_left, "lon", -1, True)
    ahead, ahead_edges, packed, last_edges = tangent_first(inc0, traj, from_left, from_right)
    a1 = moved(ahead, "tm", 1, False)
    a1_edges = moved(ahead_edges, "tm", 1, False)
    later_edges = moved(last_edges, "tm", -1, False)
    z0 = spread(middle)
    z_right, z_left = spread_edges_call(z0)
    z_left, z_right = moved(z_right, "lon", 1, True), moved(z_left, "lon", -1, True)
    m1 = observed(inc0)
    d1, d1_edges = adjoint_first(later, later_edges, traj, packed, z0, z_left, z_right)

    d1_later = moved(d1, "tm", -1, False)
    d1_later_edges = moved(d1_edges, "tm", -1, False)
    inc1, ahead2 = tangent_second(a1, a1_edges, d1, d1_edges, variance, traj, packed)
    a2 = moved(ahead2, "tm", 1, False)
    z1 = spread(m1)
    m2 = observed(inc1)
    early = products(((0, 0), (1, 1), (0, 2), (1, 3), (2, 2), (3, 3)), (first, last, a1, d1))
    d_sums = adjoint_second(d1_later, d1_later_edges, traj, packed, z1, last, d1)
    a_sums = products(((0, 2), (1, 2), (2, 2)), (first, a1, a2))

    early = jnp.sum(early, axis=(1, 2))
    d_sums = jnp.sum(d_sums, axis=(1, 2))
    a_sums = jnp.sum(a_sums, axis=(1, 2))
    scalars = jnp.stack(
        [
            early[0] + early[1] + jnp.sum(middle * middle),
            early[2] + early[3] + jnp.sum(middle * m1),
            d_sums[0] + a_sums[0] + jnp.sum(middle * m2),
            early[4] + early[5] + jnp.sum(m1 * m1),
            d_sums[1] + a_sums[1] + jnp.sum(m1 * m2),
            d_sums[2] + a_sums[2] + jnp.sum(m2 * m2),
        ]
    )
    total = mesh_sums(jnp.pad(scalars, (0, LANE - 6)))
    c0, c1 = weights(*[total[k] for k in range(6)])
    return (
        (c0 * last + c1 * d1)[None],
        ((c0 * middle + c1 * m1) / obs_part)[None],
        (c0 * inc0 + c1 * inc1)[None],
    )


def solution(mesh):
    in_specs = (
        P("tm", None, None, "lon"),
        P("tm", "lon"),
        P("tm", None, None, None, "lon"),
        P("tm", None, None, "lon"),
        P("tm", "lon"),
        P("tm", "lon"),
        P("tm", None, None, "lon"),
    )
    out_specs = (P("tm", None, None, "lon"), P("tm", "lon"), P("tm", None, None, "lon"))
    return jax.shard_map(shards, mesh=mesh, in_specs=in_specs, out_specs=out_specs, check_vma=False)
```

```python
import functools

import jax
import jax.numpy as jnp
from jax import lax
from jax.experimental import pallas as pl
from jax.experimental.pallas import tpu as pltpu
from jax.sharding import PartitionSpec as P

courant = 0.25
coriolis = 0.2
slope = 0.5 * courant

LANE = 128
BLOCK = 256
GROUP = 16
MARGIN = 8
HALO = 4
TRAJ, INC, VAR, LAST, PLANES = 0, 6, 9, 12, 16
F32 = jnp.float32
PARAMS = pltpu.CompilerParams(vmem_limit_bytes=56 * 1024 * 1024)


def iota(shape, dim):
    return lax.broadcasted_iota(jnp.int32, shape, dim)


def spread_shift(plane):
    return (LANE - (8 * plane + HALO)) % LANE


def pack_shift(plane):
    return (8 * plane + HALO) % LANE


def edges_of(planes, rows):
    lane = iota((rows, LANE), 1)
    packed = jnp.zeros((rows, LANE), F32)
    for number, plane in enumerate(planes):
        both = jnp.where(lane < LANE // 2, plane[:, :LANE], plane[:, LANE:])
        packed = jnp.where(lane // 8 == number, pltpu.roll(both, pack_shift(number), 1), packed)
    return packed


def split_edges(turned, to_right, to_left, count):
    top = iota((8, turned.shape[1]), 0) < HALO
    for pair in range(count // 2):
        even = turned[16 * pair : 16 * pair + 8]
        odd = turned[16 * pair + 8 : 16 * pair + 16]
        to_right[8 * pair : 8 * pair + 8, :] = jnp.where(top, even, pltpu.roll(odd, HALO, 0))
        to_left[8 * pair : 8 * pair + 8, :] = jnp.where(top, pltpu.roll(even, HALO, 0), odd)


def joined_edges(from_left, from_right, count):
    top = iota((8, from_left.shape[1]), 0) < HALO
    pieces = []
    for pair in range(count // 2):
        left = from_left[8 * pair : 8 * pair + 8]
        right = from_right[8 * pair : 8 * pair + 8]
        pieces.append(jnp.where(top, left, pltpu.roll(right, HALO, 0)))
        pieces.append(jnp.where(top, pltpu.roll(left, HALO, 0), right))
    return jnp.concatenate(pieces, axis=0)


def padded_turn(message):
    rest = LANE - message.shape[0]
    if rest:
        message = jnp.concatenate([message, jnp.zeros((rest, message.shape[1]), F32)], axis=0)
    return message.T


def edges_kernel(first, last, variance, traj, to_right, to_left, increment):
    rows = first.shape[1]
    planes = [traj[p].astype(F32) for p in range(6)]
    for f in range(3):
        value = first[f] - variance[f] * last[f]
        increment[f] = value
        planes.append(value)
    planes += [variance[f] for f in range(3)]
    planes += [last[f] for f in range(3)]
    split_edges(edges_of(planes, rows).T, to_right, to_left, PLANES)


def edges_call(first, last, variance, traj):
    rows = first.shape[1]
    block = pl.BlockSpec((3, BLOCK, 2 * LANE), lambda i: (0, i, 0))
    sent = pl.BlockSpec((PLANES * HALO, BLOCK), lambda i: (0, i))
    return pl.pallas_call(
        edges_kernel,
        grid=(rows // BLOCK,),
        in_specs=[block, block, block, pl.BlockSpec((6, BLOCK, 2 * LANE), lambda i: (0, i, 0))],
        out_specs=[sent, sent, block],
        out_shape=[jax.ShapeDtypeStruct((PLANES * HALO, rows), F32)] * 2
        + [jax.ShapeDtypeStruct(first.shape, F32)],
        compiler_params=PARAMS,
        cost_estimate=cost(16),
        name="edges",
    )(first, last, variance, traj)


def spread_edges_kernel(spread, to_right, to_left):
    planes = [spread[f] for f in range(3)]
    split_edges(edges_of(planes, spread.shape[1]).T, to_right, to_left, 4)


def spread_edges_call(spread):
    rows = spread.shape[1]
    sent = pl.BlockSpec((16, BLOCK), lambda i: (0, i))
    return pl.pallas_call(
        spread_edges_kernel,
        grid=(rows // BLOCK,),
        in_specs=[pl.BlockSpec((3, BLOCK, 2 * LANE), lambda i: (0, i, 0))],
        out_specs=[sent, sent],
        out_shape=[jax.ShapeDtypeStruct((16, rows), F32)] * 2,
        compiler_params=PARAMS,
        cost_estimate=cost(3),
        name="spread_edges",
    )(spread)


def x_differences(tiles, first_lane, last_lane):
    ahead = [pltpu.roll(t, LANE - 1, 1) for t in tiles]
    behind = [pltpu.roll(t, 1, 1) for t in tiles]
    return [
        jnp.where(last_lane, ahead[(t + 1) % 3], ahead[t])
        - jnp.where(first_lane, behind[(t - 1) % 3], behind[t])
        for t in range(3)
    ]


def rotation_at(start, total):
    position = (iota((GROUP, LANE), 0) + start).astype(F32)
    return coriolis * ((2.0 * position + 1.0) / total - 1.0)


def lane_ends():
    lane = iota((GROUP, LANE), 1)
    return lane == 0, lane == LANE - 1


def traj_tiles(traj, packed_ref, step, start):
    packed = packed_ref[pl.ds(start, GROUP), :]
    out = []
    for field in range(3):
        plane = 3 * step + field
        out.append(
            [traj[plane, pl.ds(start, GROUP), t * LANE : (t + 1) * LANE].astype(F32) for t in range(2)]
            + [pltpu.roll(packed, spread_shift(TRAJ + plane), 1)]
        )
    return out


def load_rows(ref, start, offset):
    return [[ref[f, t, pl.ds(start + (MARGIN + offset), GROUP), :] for t in range(3)] for f in range(3)]


def store_rows(ref, start, value):
    for f in range(3):
        for t in range(3):
            ref[f, t, pl.ds(start + MARGIN, GROUP), :] = value[f][t]


def clear_margins(ref):
    rows = ref.shape[2]
    zero = jnp.zeros((MARGIN, LANE), F32)
    for f in range(3):
        for t in range(3):
            ref[f, t, 0:MARGIN, :] = zero
            ref[f, t, rows - MARGIN : rows, :] = zero


def tangent_rows(source, traj, packed_ref, step, start, total):
    here, above, below = (load_rows(source, start, k) for k in (0, 1, -1))
    trajectory = traj_tiles(traj, packed_ref, step, start)
    turn = rotation_at(start, total)
    ends = lane_ends()
    dx = [x_differences(here[f], *ends) for f in range(3)]
    new = [[], [], []]
    for t in range(3):
        b, e, n = (trajectory[f][t] for f in range(3))
        h, u, v = (here[f][t] for f in range(3))
        xh, xu, xv = (dx[f][t] for f in range(3))
        yh, yu, yv = (above[f][t] - below[f][t] for f in range(3))
        new[0].append(h - slope * (b * (xu + yv) + e * xh + n * yh))
        new[1].append(u - slope * (xh + e * xu + n * yu) + turn * v)
        new[2].append(v - slope * (yh + e * xv + n * yv) - turn * u)
    return new


def north_rows(field, trajectory):
    out = [[], [], []]
    for t in range(3):
        b, _, n = (trajectory[f][t] for f in range(3))
        p, q, w = (field[f][t] for f in range(3))
        out[0].append(n * p + w)
        out[1].append(n * q)
        out[2].append(b * p + n * w)
    return out


def adjoint_rows(source, flux, traj, packed_ref, step, start, total):
    here = load_rows(source, start, 0)
    above, below = (load_rows(flux, start, k) for k in (1, -1))
    trajectory = traj_tiles(traj, packed_ref, step, start)
    turn = rotation_at(start, total)
    ends = lane_ends()
    east = [[], [], []]
    for t in range(3):
        b, e, _ = (trajectory[f][t] for f in range(3))
        p, q, w = (here[f][t] for f in range(3))
        east[0].append(e * p + q)
        east[1].append(b * p + e * q)
        east[2].append(e * w)
    dx = [x_differences(east[f], *ends) for f in range(3)]
    new = [[], [], []]
    for t in range(3):
        p, q, w = (here[f][t] for f in range(3))
        change = [slope * (dx[f][t] + (above[f][t] - below[f][t])) for f in range(3)]
        new[0].append(p + change[0])
        new[1].append(q + change[1] - turn * w)
        new[2].append(w + change[2] + turn * q)
    return new


def over_rows(total, body):
    def step(i, carry):
        body(pl.multiple_of(i * GROUP, GROUP))
        return carry

    lax.fori_loop(0, total // GROUP, step, 0, unroll=4)


def turn_in(message, packed_ref):
    for j in range(message.shape[1] // LANE):
        packed_ref[j * LANE : (j + 1) * LANE, :] = padded_turn(message[:, j * LANE : (j + 1) * LANE])


def turn_out(packed_ref, message):
    for j in range(message.shape[1] // LANE):
        turned = packed_ref[j * LANE : (j + 1) * LANE, :].T
        message[:, j * LANE : (j + 1) * LANE] = turned[: message.shape[0]]


def pack_three(halo_tiles):
    lane = iota((GROUP, LANE), 1) // 8
    packed = jnp.zeros((GROUP, LANE), F32)
    for f in range(3):
        packed = jnp.where(lane == f, pltpu.roll(halo_tiles[f], pack_shift(f), 1), packed)
    return packed


def wide_scratch(rows):
    return pltpu.VMEM((3, 3, rows + 2 * MARGIN, LANE), F32)


def tile_of(ref, f, start, t):
    return ref[f, pl.ds(start, GROUP), t * LANE : (t + 1) * LANE]


def set_tile(ref, f, start, t, value):
    ref[f, pl.ds(start, GROUP), t * LANE : (t + 1) * LANE] = value


def run_tangent(get, traj, packed_ref, wide_a, wide_b, total, put):
    clear_margins(wide_a)
    clear_margins(wide_b)
    over_rows(total, lambda s: store_rows(wide_a, s, get(s)))
    over_rows(
        total, lambda s: store_rows(wide_b, s, tangent_rows(wide_a, traj, packed_ref, 0, s, total))
    )
    over_rows(total, lambda s: put(s, tangent_rows(wide_b, traj, packed_ref, 1, s, total)))


def run_adjoint(get, traj, packed_ref, wide_a, wide_b, flux_a, flux_b, total, put):
    clear_margins(flux_a)
    clear_margins(flux_b)

    def begin(s):
        field = get(s)
        store_rows(wide_a, s, field)
        store_rows(flux_a, s, north_rows(field, traj_tiles(traj, packed_ref, 1, s)))

    def middle(s):
        field = adjoint_rows(wide_a, flux_a, traj, packed_ref, 1, s, total)
        store_rows(wide_b, s, field)
        store_rows(flux_b, s, north_rows(field, traj_tiles(traj, packed_ref, 0, s)))

    over_rows(total, begin)
    over_rows(total, middle)
    over_rows(total, lambda s: put(s, adjoint_rows(wide_b, flux_b, traj, packed_ref, 0, s, total)))


def tangent_first_kernel(
    increment, traj, from_left, from_right, ahead, ahead_edges, packed, last_edges, wide_a, wide_b, own
):
    total = increment.shape[1]
    for j in range(total // LANE):
        cut = slice(j * LANE, (j + 1) * LANE)
        joined = joined_edges(from_left[:, cut], from_right[:, cut], PLANES)
        last_edges[:, cut] = joined[8 * LAST : 8 * LAST + 24]
        packed[cut, :] = joined.T

    def get(s):
        lanes = packed[pl.ds(s, GROUP), :]
        return [
            [tile_of(increment, f, s, 0), tile_of(increment, f, s, 1), pltpu.roll(lanes, spread_shift(INC + f), 1)]
            for f in range(3)
        ]

    def put(s, new):
        for f in range(3):
            for t in range(2):
                set_tile(ahead, f, s, t, -new[f][t])
        own[pl.ds(s, GROUP), :] = pack_three([-new[f][2] for f in range(3)])

    run_tangent(get, traj, packed, wide_a, wide_b, total, put)
    turn_out(own, ahead_edges)


def whole(count):
    return [pl.BlockSpec(memory_space=pltpu.VMEM)] * count


def cost(mib, steps=2):
    return pl.CostEstimate(flops=steps * 2**10, bytes_accessed=mib * 2**10, transcendentals=0)


def tangent_first(increment, traj, from_left, from_right):
    rows = increment.shape[1]
    return pl.pallas_call(
        tangent_first_kernel,
        in_specs=whole(4),
        out_specs=whole(4),
        out_shape=[
            jax.ShapeDtypeStruct(increment.shape, F32),
            jax.ShapeDtypeStruct((24, rows), F32),
            jax.ShapeDtypeStruct((rows, LANE), F32),
            jax.ShapeDtypeStruct((24, rows), F32),
        ],
        scratch_shapes=[wide_scratch(rows)] * 2 + [pltpu.VMEM((rows, LANE), F32)],
        compiler_params=PARAMS,
        cost_estimate=cost(10),
        name="tangent_first",
    )(increment, traj, from_left, from_right)


def adjoint_first_kernel(
    later, later_edges, traj, packed, spread, z_left, z_right, pulled, pulled_edges,
    wide_a, wide_b, flux_a, flux_b, own, z_own,
):
    total = later.shape[1]
    turn_in(later_edges, own)
    for j in range(total // LANE):
        cut = slice(j * LANE, (j + 1) * LANE)
        z_own[cut, :] = padded_turn(joined_edges(z_left[:, cut], z_right[:, cut], 4))

    def get(s):
        lanes = own[pl.ds(s, GROUP), :]
        return [
            [tile_of(later, f, s, 0), tile_of(later, f, s, 1), pltpu.roll(lanes, spread_shift(f), 1)]
            for f in range(3)
        ]

    def put(s, new):
        lanes = z_own[pl.ds(s, GROUP), :]
        halo = []
        for f in range(3):
            for t in range(2):
                set_tile(pulled, f, s, t, tile_of(spread, f, s, t) - new[f][t])
            halo.append(pltpu.roll(lanes, spread_shift(f), 1) - new[f][2])
        own[pl.ds(s, GROUP), :] = pack_three(halo)

    run_adjoint(get, traj, packed, wide_a, wide_b, flux_a, flux_b, total, put)
    turn_out(own, pulled_edges)


def adjoint_first(later, later_edges, traj, packed, spread, z_left, z_right):
    rows = later.shape[1]
    return pl.pallas_call(
        adjoint_first_kernel,
        in_specs=whole(7),
        out_specs=whole(2),
        out_shape=[jax.ShapeDtypeStruct(later.shape, F32), jax.ShapeDtypeStruct((24, rows), F32)],
        scratch_shapes=[wide_scratch(rows)] * 4 + [pltpu.VMEM((rows, LANE), F32)] * 2,
        compiler_params=PARAMS,
        cost_estimate=cost(13),
        name="adjoint_first",
    )(later, later_edges, traj, packed, spread, z_left, z_right)


def tangent_second_kernel(
    earlier, earlier_edges, pulled, pulled_edges, variance, traj, packed, increment, ahead, wide_a, wide_b, e_own, p_own
):
    total = earlier.shape[1]
    turn_in(earlier_edges, e_own)
    turn_in(pulled_edges, p_own)

    def get(s):
        e_lanes = e_own[pl.ds(s, GROUP), :]
        p_lanes = p_own[pl.ds(s, GROUP), :]
        v_lanes = packed[pl.ds(s, GROUP), :]
        out = []
        for f in range(3):
            tiles = [tile_of(earlier, f, s, t) - tile_of(variance, f, s, t) * tile_of(pulled, f, s, t) for t in range(2)]
            for t in range(2):
                set_tile(increment, f, s, t, tiles[t])
            shift = spread_shift(f)
            tiles.append(
                pltpu.roll(e_lanes, shift, 1)
                - pltpu.roll(v_lanes, spread_shift(VAR + f), 1) * pltpu.roll(p_lanes, shift, 1)
            )
            out.append(tiles)
        return out

    def put(s, new):
        for f in range(3):
            for t in range(2):
                set_tile(ahead, f, s, t, -new[f][t])

    run_tangent(get, traj, packed, wide_a, wide_b, total, put)


def tangent_second(earlier, earlier_edges, pulled, pulled_edges, variance, traj, packed):
    rows = earlier.shape[1]
    return pl.pallas_call(
        tangent_second_kernel,
        in_specs=whole(7),
        out_specs=whole(2),
        out_shape=[jax.ShapeDtypeStruct(earlier.shape, F32)] * 2,
        scratch_shapes=[wide_scratch(rows)] * 2 + [pltpu.VMEM((rows, LANE), F32)] * 2,
        compiler_params=PARAMS,
        cost_estimate=cost(18),
        name="tangent_second",
    )(earlier, earlier_edges, pulled, pulled_edges, variance, traj, packed)


def adjoint_second_kernel(
    later, later_edges, traj, packed, spread, last, pulled, sums, wide_a, wide_b, flux_a, flux_b, own
):
    total = later.shape[1]
    turn_in(later_edges, own)
    sums[...] = jnp.zeros_like(sums)

    def get(s):
        lanes = own[pl.ds(s, GROUP), :]
        return [
            [tile_of(later, f, s, 0), tile_of(later, f, s, 1), pltpu.roll(lanes, spread_shift(f), 1)]
            for f in range(3)
        ]

    def put(s, new):
        parts = [jnp.zeros((GROUP, LANE), F32)] * 3
        for f in range(3):
            for t in range(2):
                value = tile_of(spread, f, s, t) - new[f][t]
                for k, other in enumerate((tile_of(last, f, s, t), tile_of(pulled, f, s, t), value)):
                    parts[k] = parts[k] + other * value
        for k in range(3):
            sums[k] = sums[k] + parts[k]

    run_adjoint(get, traj, packed, wide_a, wide_b, flux_a, flux_b, total, put)


def adjoint_second(later, later_edges, traj, packed, spread, last, pulled):
    rows = later.shape[1]
    return pl.pallas_call(
        adjoint_second_kernel,
        in_specs=whole(7),
        out_specs=pl.BlockSpec(memory_space=pltpu.VMEM),
        out_shape=jax.ShapeDtypeStruct((3, GROUP, LANE), F32),
        scratch_shapes=[wide_scratch(rows)] * 4 + [pltpu.VMEM((rows, LANE), F32)],
        compiler_params=PARAMS,
        cost_estimate=cost(16),
        name="adjoint_second",
    )(later, later_edges, traj, packed, spread, last, pulled)


def products_kernel(pairs, *refs):
    arrays, sums = refs[:-1], refs[-1]

    @pl.when(pl.program_id(0) == 0)
    def _():
        sums[...] = jnp.zeros_like(sums)

    add_products(pairs, arrays, sums)


def add_products(pairs, arrays, sums):
    def step(i, carry):
        start = pl.multiple_of(i * GROUP, GROUP)
        parts = [jnp.zeros((GROUP, 2 * LANE), F32)] * len(pairs)
        for f in range(3):
            tiles = [a[f, pl.ds(start, GROUP), :] for a in arrays]
            for k, (one, two) in enumerate(pairs):
                parts[k] = parts[k] + tiles[one] * tiles[two]
        return tuple(c + p for c, p in zip(carry, parts))

    begin = tuple(sums[k] for k in range(len(pairs)))
    for k, value in enumerate(lax.fori_loop(0, arrays[0].shape[1] // GROUP, step, begin)):
        sums[k] = value


def products(pairs, arrays):
    rows = arrays[0].shape[1]
    block = pl.BlockSpec((3, BLOCK, 2 * LANE), lambda i: (0, i, 0))
    shape = (len(pairs), GROUP, 2 * LANE)
    return pl.pallas_call(
        functools.partial(products_kernel, pairs),
        grid=(rows // BLOCK,),
        in_specs=[block] * len(arrays),
        out_specs=pl.BlockSpec(shape, lambda i: (0, 0, 0)),
        out_shape=jax.ShapeDtypeStruct(shape, F32),
        compiler_params=PARAMS,
        cost_estimate=cost(3 * len(arrays), 1),
        name="products",
    )(*arrays)


def one_sum(value):
    return jnp.sum(jnp.sum(value, axis=1, keepdims=True), axis=0, keepdims=True)


def last_products_kernel(first, a1, a2, early, d_sums, middle, m1, m2, sent, sums):
    @pl.when(pl.program_id(0) == 0)
    def _():
        sums[...] = jnp.zeros_like(sums)

    add_products(((0, 2), (1, 2), (2, 2)), (first, a1, a2), sums)

    @pl.when(pl.program_id(0) == pl.num_programs(0) - 1)
    def _():
        o0, o1, o2 = middle[...], m1[...], m2[...]
        values = (
            one_sum(early[0] + early[1]) + one_sum(o0 * o0),
            one_sum(early[2] + early[3]) + one_sum(o0 * o1),
            one_sum(sums[0]) + one_sum(d_sums[0]) + one_sum(o0 * o2),
            one_sum(early[4] + early[5]) + one_sum(o1 * o1),
            one_sum(sums[1]) + one_sum(d_sums[1]) + one_sum(o1 * o2),
            one_sum(sums[2]) + one_sum(d_sums[2]) + one_sum(o2 * o2),
        )
        lane = iota((8, LANE), 1)
        row = jnp.zeros((8, LANE), F32)
        for k, value in enumerate(values):
            row = jnp.where(lane == k, value, row)
        for k in range(sent.shape[0]):
            sent[k] = row


def last_products(count, first, a1, a2, early, d_sums, middle, m1, m2):
    rows = first.shape[1]
    block = pl.BlockSpec((3, BLOCK, 2 * LANE), lambda i: (0, i, 0))
    return pl.pallas_call(
        last_products_kernel,
        grid=(rows // BLOCK,),
        in_specs=[block] * 3 + whole(5),
        out_specs=pl.BlockSpec((count, 8, LANE), lambda i: (0, 0, 0)),
        out_shape=jax.ShapeDtypeStruct((count, 8, LANE), F32),
        scratch_shapes=[pltpu.VMEM((3, GROUP, 2 * LANE), F32)],
        compiler_params=PARAMS,
        cost_estimate=cost(9, 1),
        name="last_products",
    )(first, a1, a2, early, d_sums, middle, m1, m2)


def weights(s00, s01, s02, s11, s12, s22):
    alpha = s01 / s00
    t11 = s11 - alpha * s01
    along = (s12 - alpha * s02) / t11
    beta = jnp.sqrt(s00)
    gamma = 1.0 / jnp.sqrt(t11)
    h00 = 1.0 + alpha
    h10_square = t11 / s00
    h10 = jnp.sqrt(h10_square)
    h01 = (s02 - alpha * s01) * gamma / beta
    h11 = 1.0 - alpha + along
    h21_square = (s22 - s02 * (s02 / s00) - along * (s12 - alpha * s02)) / t11
    g00 = h00 * h00 + h10_square
    g01 = h00 * h01 + h10 * h11
    g11 = h01 * h01 + h11 * h11 + h21_square
    q0 = beta * h00
    q1 = beta * h01
    det = g00 * g11 - g01 * g01
    y0 = (g11 * q0 - g01 * q1) / det
    y1 = (g00 * q1 - g01 * q0) / det
    c1 = y1 * gamma
    return (y0 / beta - c1 * alpha, c1)


def result_kernel(received, last, d1, inc0, inc1, middle, m1, obs_part, multiplier, increment, dual, coefs):
    @pl.when(pl.program_id(0) == 0)
    def _():
        total = jnp.sum(received[...], axis=0)
        lane = iota((8, LANE), 1)
        scalars = [
            jnp.broadcast_to(jnp.sum(jnp.where(lane == k, total, 0.0), axis=1, keepdims=True), (8, LANE))
            for k in range(6)
        ]
        c0, c1 = weights(*scalars)
        coefs[0] = c0
        coefs[1] = c1
        dual[...] = (c0[0:1] * middle[...] + c1[0:1] * m1[...]) / obs_part[...]

    def step(i, carry):
        start = pl.multiple_of(i * 8, 8)
        c0, c1 = coefs[0], coefs[1]
        for f in range(3):
            for t in range(2):
                at = (f, pl.ds(start, 8), slice(t * LANE, (t + 1) * LANE))
                multiplier[at] = c0 * last[at] + c1 * d1[at]
                increment[at] = c0 * inc0[at] + c1 * inc1[at]
        return carry

    lax.fori_loop(0, last.shape[1] // 8, step, 0, unroll=4)


def result(received, last, d1, inc0, inc1, middle, m1, obs_part):
    rows = last.shape[1]
    block = pl.BlockSpec((3, BLOCK, 2 * LANE), lambda i: (0, i, 0))
    obs = pl.BlockSpec(middle.shape, lambda i: (0, 0))
    return pl.pallas_call(
        result_kernel,
        grid=(rows // BLOCK,),
        in_specs=whole(1) + [block] * 4 + whole(3),
        out_specs=[block, block, obs],
        out_shape=[jax.ShapeDtypeStruct(last.shape, F32)] * 2 + [jax.ShapeDtypeStruct(middle.shape, F32)],
        scratch_shapes=[pltpu.VMEM((2, 8, LANE), F32)],
        compiler_params=PARAMS,
        cost_estimate=cost(18, 1),
        name="result",
    )(received, last, d1, inc0, inc1, middle, m1, obs_part)


def moved(block, axis, distance, wrap):
    size = lax.axis_size(axis)
    if wrap:
        route = [(i, (i + distance) % size) for i in range(size)]
    else:
        route = [(i, i + distance) for i in range(size) if 0 <= i + distance < size]
    return lax.ppermute(block, axis, route)


def shards(rhs_state, innovations, trajectory, model_var, obs_var, obs_index, control_rhs):
    rows, columns = rhs_state.shape[2:]
    first, last, variance = rhs_state[0], control_rhs[0], model_var[0]
    traj = trajectory.reshape(-1, rows, columns)
    middle, obs_part, where = innovations[0], obs_var[0], obs_index[0]

    def observed(field):
        return field.reshape(-1)[where]

    def spread(values):
        flat = jnp.zeros((3 * rows * columns,), F32).at[where].add(values / obs_part)
        return flat.reshape(3, rows, columns)

    later = moved(last, "tm", -1, False)
    to_right, to_left, inc0 = edges_call(first, last, variance, traj)
    from_left = moved(to_right, "lon", 1, True)
    from_right = moved(to_left, "lon", -1, True)
    ahead, ahead_edges, packed, last_edges = tangent_first(inc0, traj, from_left, from_right)
    a1 = moved(ahead, "tm", 1, False)
    a1_edges = moved(ahead_edges, "tm", 1, False)
    later_edges = moved(last_edges, "tm", -1, False)
    z0 = spread(middle)
    z_right, z_left = spread_edges_call(z0)
    z_left, z_right = moved(z_right, "lon", 1, True), moved(z_left, "lon", -1, True)
    m1 = observed(inc0)
    d1, d1_edges = adjoint_first(later, later_edges, traj, packed, z0, z_left, z_right)

    d1_later = moved(d1, "tm", -1, False)
    d1_later_edges = moved(d1_edges, "tm", -1, False)
    inc1, ahead2 = tangent_second(a1, a1_edges, d1, d1_edges, variance, traj, packed)
    a2 = moved(ahead2, "tm", 1, False)
    z1 = spread(m1)
    m2 = observed(inc1)
    early = products(((0, 0), (1, 1), (0, 2), (1, 3), (2, 2), (3, 3)), (first, last, a1, d1))
    d_sums = adjoint_second(d1_later, d1_later_edges, traj, packed, z1, last, d1)
    count = lax.axis_size("tm") * lax.axis_size("lon")
    middle, m1, m2, obs_part = (o.reshape(-1, LANE) for o in (middle, m1, m2, obs_part))
    sent = last_products(count, first, a1, a2, early, d_sums, middle, m1, m2)
    received = lax.all_to_all(sent, ("tm", "lon"), 0, 0)
    multiplier, increment, dual = result(received, last, d1, inc0, inc1, middle, m1, obs_part)
    return (multiplier[None], dual.reshape(1, -1), increment[None])


def solution(mesh):
    in_specs = (
        P("tm", None, None, "lon"),
        P("tm", "lon"),
        P("tm", None, None, None, "lon"),
        P("tm", None, None, "lon"),
        P("tm", "lon"),
        P("tm", "lon"),
        P("tm", None, None, "lon"),
    )
    out_specs = (P("tm", None, None, "lon"), P("tm", "lon"), P("tm", None, None, "lon"))
    return jax.shard_map(shards, mesh=mesh, in_specs=in_specs, out_specs=out_specs, check_vma=False)
```

```python
import jax
import jax.numpy as jnp
from jax import lax
from jax.experimental import pallas as pl
from jax.experimental.pallas import tpu as pltpu
from jax.sharding import PartitionSpec as P

courant = 0.25
coriolis = 0.2
slope = 0.5 * courant

LANE = 128
BLOCK = 256
GROUP = 16
MARGIN = 8
HALO = 4
TRAJ, INC, VAR, LAST, PLANES = 0, 6, 9, 12, 16
F32 = jnp.float32
PARAMS = pltpu.CompilerParams(vmem_limit_bytes=56 * 1024 * 1024)


def iota(shape, dim):
    return lax.broadcasted_iota(jnp.int32, shape, dim)


def spread_shift(plane):
    return (LANE - (8 * plane + HALO)) % LANE


def pack_shift(plane):
    return (8 * plane + HALO) % LANE


def edges_of(planes, rows):
    lane = iota((rows, LANE), 1)
    packed = jnp.zeros((rows, LANE), F32)
    for number, plane in enumerate(planes):
        both = jnp.where(lane < LANE // 2, plane[:, :LANE], plane[:, LANE:])
        packed = jnp.where((lane >= 8 * number) & (lane < 8 * number + 8), pltpu.roll(both, pack_shift(number), 1), packed)
    return packed


def split_edges(turned, to_right, to_left, count):
    top = iota((8, turned.shape[1]), 0) < HALO
    for pair in range(count // 2):
        even = turned[16 * pair : 16 * pair + 8]
        odd = turned[16 * pair + 8 : 16 * pair + 16]
        to_right[8 * pair : 8 * pair + 8, :] = jnp.where(top, even, pltpu.roll(odd, HALO, 0))
        to_left[8 * pair : 8 * pair + 8, :] = jnp.where(top, pltpu.roll(even, HALO, 0), odd)


def joined_edges(from_left, from_right, count):
    top = iota((8, from_left.shape[1]), 0) < HALO
    pieces = []
    for pair in range(count // 2):
        left = from_left[8 * pair : 8 * pair + 8]
        right = from_right[8 * pair : 8 * pair + 8]
        pieces.append(jnp.where(top, left, pltpu.roll(right, HALO, 0)))
        pieces.append(jnp.where(top, pltpu.roll(left, HALO, 0), right))
    return jnp.concatenate(pieces, axis=0)


def padded_turn(message):
    rest = LANE - message.shape[0]
    if rest:
        message = jnp.concatenate([message, jnp.zeros((rest, message.shape[1]), F32)], axis=0)
    return message.T


def edges_kernel(first, last, variance, traj, to_right, to_left, increment):
    rows = first.shape[1]
    planes = [traj[p].astype(F32) for p in range(6)]
    for f in range(3):
        value = first[f] - variance[f] * last[f]
        increment[f] = value
        planes.append(value)
    planes += [variance[f] for f in range(3)]
    planes += [last[f] for f in range(3)]
    split_edges(edges_of(planes, rows).T, to_right, to_left, PLANES)


def edges_call(first, last, variance, traj):
    rows = first.shape[1]
    block = pl.BlockSpec((3, BLOCK, 2 * LANE), lambda i: (0, i, 0))
    sent = pl.BlockSpec((PLANES * HALO, BLOCK), lambda i: (0, i))
    return pl.pallas_call(
        edges_kernel,
        grid=(rows // BLOCK,),
        in_specs=[block, block, block, pl.BlockSpec((6, BLOCK, 2 * LANE), lambda i: (0, i, 0))],
        out_specs=[sent, sent, block],
        out_shape=[jax.ShapeDtypeStruct((PLANES * HALO, rows), F32)] * 2
        + [jax.ShapeDtypeStruct(first.shape, F32)],
        compiler_params=PARAMS,
        cost_estimate=cost(16),
        name="edges",
    )(first, last, variance, traj)


def spread_edges_kernel(spread, to_right, to_left):
    planes = [spread[f] for f in range(3)]
    split_edges(edges_of(planes, spread.shape[1]).T, to_right, to_left, 4)


def spread_edges_call(spread):
    rows = spread.shape[1]
    sent = pl.BlockSpec((16, BLOCK), lambda i: (0, i))
    return pl.pallas_call(
        spread_edges_kernel,
        grid=(rows // BLOCK,),
        in_specs=[pl.BlockSpec((3, BLOCK, 2 * LANE), lambda i: (0, i, 0))],
        out_specs=[sent, sent],
        out_shape=[jax.ShapeDtypeStruct((16, rows), F32)] * 2,
        compiler_params=PARAMS,
        cost_estimate=cost(3),
        name="spread_edges",
    )(spread)


def x_differences(tiles, first_lane, last_lane):
    ahead = [pltpu.roll(t, LANE - 1, 1) for t in tiles]
    behind = [pltpu.roll(t, 1, 1) for t in tiles]
    return [
        jnp.where(last_lane, ahead[(t + 1) % 3], ahead[t])
        - jnp.where(first_lane, behind[(t - 1) % 3], behind[t])
        for t in range(3)
    ]


def rotation_at(start, total):
    position = (iota((GROUP, LANE), 0) + start).astype(F32)
    return coriolis * ((2.0 * position + 1.0) / total - 1.0)


def lane_ends():
    lane = iota((GROUP, LANE), 1)
    return lane == 0, lane == LANE - 1


def rows_at(start, offset=0):
    return pl.ds(pl.multiple_of(start + offset, GROUP), GROUP)


def traj_tiles(traj, traj_halo, step, start):
    out = []
    for plane in range(3 * step, 3 * step + 3):
        tiles = [traj[plane, rows_at(start), t * LANE : (t + 1) * LANE] for t in range(2)]
        out.append([t.astype(F32) for t in tiles + [traj_halo[plane, rows_at(start), :]]])
    return out


def load_rows(ref, start, offset):
    return [[ref[f, t, pl.ds(start + (MARGIN + offset), GROUP), :] for t in range(3)] for f in range(3)]


def store_rows(ref, start, value):
    for f in range(3):
        for t in range(3):
            ref[f, t, pl.ds(start + MARGIN, GROUP), :] = value[f][t]


def clear_margins(ref):
    rows = ref.shape[2]
    zero = jnp.zeros((MARGIN, LANE), F32)
    for f in range(3):
        for t in range(3):
            ref[f, t, 0:MARGIN, :] = zero
            ref[f, t, rows - MARGIN : rows, :] = zero


def tangent_rows(source, traj, traj_halo, step, start, total):
    here, above, below = (load_rows(source, start, k) for k in (0, 1, -1))
    trajectory = traj_tiles(traj, traj_halo, step, start)
    turn = rotation_at(start, total)
    ends = lane_ends()
    dx = [x_differences(here[f], *ends) for f in range(3)]
    new = [[], [], []]
    for t in range(3):
        b, e, n = (trajectory[f][t] for f in range(3))
        h, u, v = (here[f][t] for f in range(3))
        xh, xu, xv = (dx[f][t] for f in range(3))
        yh, yu, yv = (above[f][t] - below[f][t] for f in range(3))
        new[0].append(h - slope * (b * (xu + yv) + e * xh + n * yh))
        new[1].append(u - slope * (xh + e * xu + n * yu) + turn * v)
        new[2].append(v - slope * (yh + e * xv + n * yv) - turn * u)
    return new


def north_rows(field, trajectory):
    out = [[], [], []]
    for t in range(3):
        b, _, n = (trajectory[f][t] for f in range(3))
        p, q, w = (field[f][t] for f in range(3))
        out[0].append(n * p + w)
        out[1].append(n * q)
        out[2].append(b * p + n * w)
    return out


def adjoint_rows(source, flux, traj, traj_halo, step, start, total):
    here = load_rows(source, start, 0)
    above, below = (load_rows(flux, start, k) for k in (1, -1))
    trajectory = traj_tiles(traj, traj_halo, step, start)
    turn = rotation_at(start, total)
    ends = lane_ends()
    east = [[], [], []]
    for t in range(3):
        b, e, _ = (trajectory[f][t] for f in range(3))
        p, q, w = (here[f][t] for f in range(3))
        east[0].append(e * p + q)
        east[1].append(b * p + e * q)
        east[2].append(e * w)
    dx = [x_differences(east[f], *ends) for f in range(3)]
    new = [[], [], []]
    for t in range(3):
        p, q, w = (here[f][t] for f in range(3))
        change = [slope * (dx[f][t] + (above[f][t] - below[f][t])) for f in range(3)]
        new[0].append(p + change[0])
        new[1].append(q + change[1] - turn * w)
        new[2].append(w + change[2] + turn * q)
    return new


def over_rows(begin, end, body):
    count = (end - begin) // GROUP
    unroll = next(u for u in (8, 6, 5, 4, 3, 2, 1) if count % u == 0)

    def step(i, carry):
        body(pl.multiple_of(begin + i * GROUP, GROUP))
        return carry

    lax.fori_loop(0, count, step, 0, unroll=unroll)


def padded(rows):
    return -(-rows // (2 * LANE)) * 2 * LANE


def extra(rows):
    return 8 * padded(rows) // (2 * LANE)


def turn_in(message, packed_ref):
    for j in range(message.shape[1] // LANE):
        packed_ref[j * LANE : (j + 1) * LANE, :] = padded_turn(message[:, j * LANE : (j + 1) * LANE])


def unfold_in(folded, packed_ref):
    for j in range(packed_ref.shape[0] // LANE):
        at = (slice(j // 2 * 8, j // 2 * 8 + 8), slice(j % 2 * LANE, (j % 2 + 1) * LANE))
        message = jnp.concatenate([folded[(f,) + at] for f in range(3)], axis=0)
        packed_ref[j * LANE : (j + 1) * LANE, :] = padded_turn(message)


def turn_out(halo, payload, behind):
    low = iota((8, LANE), 0) < HALO
    for j in range(halo.shape[1] // LANE):
        for f in range(3):
            turned = halo[f, j * LANE : (j + 1) * LANE, :].T
            ends = jnp.where(low, turned[:8], turned[LANE - 8 :])
            row = behind + j // 2 * 8
            payload[f, row : row + 8, j % 2 * LANE : (j % 2 + 1) * LANE] = pltpu.roll(ends, HALO, 0)


def wide_scratch(rows):
    return pltpu.VMEM((3, 3, rows + 2 * MARGIN, LANE), F32)


def tile_of(ref, f, start, t, offset=0):
    return ref[f, rows_at(start, offset), t * LANE : (t + 1) * LANE]


def set_tile(ref, f, start, t, value, offset=0):
    ref[f, rows_at(start, offset), t * LANE : (t + 1) * LANE] = value


class Copies:
    def __init__(self, sems):
        self.sems, self.used = sems, 0

    def rows(self, parts, begin, end, target):
        started = []
        for ref, at, count in parts:
            low, high = max(begin, at), min(end, at + count)
            if low < high:
                source = ref.at[..., low - at : high - at, :]
                goal = target.at[..., low - begin : high - begin, :]
                copy = pltpu.make_async_copy(source, goal, self.sems.at[self.used])
                self.used += 1
                copy.start()
                started.append(copy)
        return started


def placed(refs, parts):
    return [(ref, at, count) for ref, (_, at, count) in zip(refs, parts)]


def wait(copies):
    for copy in copies:
        copy.wait()


def segments(total):
    return [(at, min(at + BLOCK, total)) for at in range(0, total, BLOCK)]


def fetch(copies, total, *pairs):
    return [
        [copy for source, target in pairs for copy in copies.rows([(source, 0, total)], low, high, target.at[..., low:high, :])]
        for low, high in segments(total)
    ]


def run_tangent(total, get, ready, traj, traj_halo, wide_a, wide_b, traj_ready, put, done):
    clear_margins(wide_a)
    clear_margins(wide_b)
    for (low, high), copies in zip(segments(total), ready):
        wait(copies)
        over_rows(low, high, lambda s: store_rows(wide_a, s, get(s)))
    for (low, high), copies in zip(segments(total), traj_ready):
        wait(copies)
        over_rows(low, high, lambda s: store_rows(wide_b, s, tangent_rows(wide_a, traj, traj_halo, 0, s, total)))
    for low, high in segments(total):
        over_rows(low, high, lambda s: put(s, tangent_rows(wide_b, traj, traj_halo, 1, s, total)))
        done(low, high)


def run_adjoint(total, get, ready, traj, traj_halo, wide_a, wide_b, flux_a, flux_b, put, begin_put, done):
    clear_margins(flux_a)
    clear_margins(flux_b)

    def begin(s):
        field = get(s)
        store_rows(wide_a, s, field)
        store_rows(flux_a, s, north_rows(field, traj_tiles(traj, traj_halo, 1, s)))

    def middle(s):
        field = adjoint_rows(wide_a, flux_a, traj, traj_halo, 1, s, total)
        store_rows(wide_b, s, field)
        store_rows(flux_b, s, north_rows(field, traj_tiles(traj, traj_halo, 0, s)))

    for (low, high), copies in zip(segments(total), ready):
        wait(copies)
        over_rows(low, high, begin)
    over_rows(0, total, middle)
    for (low, high), copies in zip(segments(total), begin_put):
        wait(copies)
        over_rows(low, high, lambda s: put(s, adjoint_rows(wide_b, flux_b, traj, traj_halo, 0, s, total)))
        done(low, high)


def halo_of(lanes, plane):
    return pltpu.roll(lanes, spread_shift(plane), 1)


ANY = pl.BlockSpec(memory_space=pl.ANY)


def whole(count):
    return [pl.BlockSpec(memory_space=pltpu.VMEM)] * count


def cost(mib, steps=2):
    return pl.CostEstimate(flops=2**10, bytes_accessed=mib * 2**20, transcendentals=0)


def f32(*shape):
    return jax.ShapeDtypeStruct(shape, F32)


def vmem(*shape, dtype=F32):
    return pltpu.VMEM(shape, dtype)


def call(name, kernel, ins, outs, scratch, mib, *args, first_any=False, outs_any=False):
    specs = [ANY if outs_any or (first_any and k == 0) else whole(1)[0] for k in range(len(outs))]
    return pl.pallas_call(
        kernel,
        in_specs=ins,
        out_specs=specs,
        out_shape=outs,
        scratch_shapes=scratch,
        compiler_params=PARAMS,
        cost_estimate=cost(mib),
        name=name,
    )(*args)


def tangent_first(increment, traj, from_left, from_right):
    _, total, columns = increment.shape

    def kernel(inc_in, traj_in, from_left, from_right, ahead, traj_halo, var_halo, last_edges, inc, traj, wide_a, wide_b, halo, out, sems):
        copies = Copies(sems)
        ready = fetch(copies, total, (inc_in, inc))
        traj_ready = fetch(copies, total, (traj_in, traj))
        for j in range(total // LANE):
            cut = slice(j * LANE, (j + 1) * LANE)
            joined = joined_edges(from_left[:, cut], from_right[:, cut], PLANES)
            last_edges[:, cut] = joined[8 * LAST : 8 * LAST + 24]
            packed = joined.T
            for plane in range(6):
                traj_halo[plane, cut, :] = halo_of(packed, TRAJ + plane).astype(traj_halo.dtype)
            for f in range(3):
                var_halo[f, cut, :] = halo_of(packed, VAR + f)
                halo[f, cut, :] = halo_of(packed, INC + f)

        def get(s):
            return [[tile_of(inc, f, s, t) for t in range(2)] + [halo[f, rows_at(s), :]] for f in range(3)]

        def put(s, new):
            for f in range(3):
                for t in range(2):
                    set_tile(out, f, s, t, -new[f][t])
                halo[f, rows_at(s), :] = -new[f][2]

        leaving = []

        def done(low, high):
            leaving.extend(copies.rows([(out, 0, total)], low, high, ahead.at[:, low:high, :]))

        run_tangent(total, get, ready, traj, traj_halo, wide_a, wide_b, traj_ready, put, done)
        turn_out(halo, out, total)
        end = total + extra(total)
        leaving.extend(copies.rows([(out, 0, end)], total, end, ahead.at[:, total:end, :]))
        wait(leaving)

    outs = [f32(3, total + extra(total), columns), jax.ShapeDtypeStruct((6, total, LANE), traj.dtype)]
    outs += [f32(3, total, LANE), f32(24, total)]
    scratch = [vmem(*increment.shape), vmem(*traj.shape, dtype=traj.dtype)] + [wide_scratch(total)] * 2
    scratch += [vmem(3, total, LANE), vmem(3, total + extra(total), columns)]
    scratch += [pltpu.SemaphoreType.DMA((3 * len(segments(total)) + 1,))]
    return call(
        "tangent_first", kernel, [ANY, ANY] + whole(2), outs, scratch, 10, increment, traj, from_left, from_right, first_any=True
    )


def adjoint_first(later, later_edges, traj, traj_halo, spread, z_left, z_right):
    _, total, columns = later.shape

    def kernel(later_in, traj_in, traj_halo_in, spread_in, later_edges, z_left, z_right, pulled, later, traj, traj_halo, spread,
               wide_a, wide_b, flux_a, flux_b, own, z_own, halo, out, sems):
        copies = Copies(sems)
        ready = fetch(copies, total, (later_in, later), (traj_in, traj), (traj_halo_in, traj_halo))
        begin_put = fetch(copies, total, (spread_in, spread))
        turn_in(later_edges, own)
        for j in range(total // LANE):
            cut = slice(j * LANE, (j + 1) * LANE)
            z_own[cut, :] = padded_turn(joined_edges(z_left[:, cut], z_right[:, cut], 4))

        def get(s):
            lanes = own[rows_at(s), :]
            return [[tile_of(later, f, s, t) for t in range(2)] + [halo_of(lanes, f)] for f in range(3)]

        def put(s, new):
            lanes = z_own[rows_at(s), :]
            for f in range(3):
                for t in range(2):
                    set_tile(out, f, s, t, tile_of(spread, f, s, t) - new[f][t])
                halo[f, rows_at(s), :] = halo_of(lanes, f) - new[f][2]

        leaving = []

        def done(low, high):
            leaving.extend(copies.rows([(out, 0, total)], low, high, pulled.at[:, low:high, :]))

        run_adjoint(total, get, ready, traj, traj_halo, wide_a, wide_b, flux_a, flux_b, put, begin_put, done)
        turn_out(halo, out, total)
        end = total + extra(total)
        leaving.extend(copies.rows([(out, 0, end)], total, end, pulled.at[:, total:end, :]))
        wait(leaving)

    outs = [f32(3, total + extra(total), columns)]
    scratch = [vmem(3, total, columns), vmem(6, total, columns, dtype=traj.dtype), vmem(6, total, LANE, dtype=traj.dtype)]
    scratch += [vmem(3, total, columns)] + [wide_scratch(total)] * 4 + [vmem(total, LANE)] * 2
    scratch += [vmem(3, total, LANE), vmem(3, total + extra(total), columns)]
    scratch += [pltpu.SemaphoreType.DMA((5 * len(segments(total)) + 1,))]
    return call(
        "adjoint_first", kernel, [ANY] * 4 + whole(3), outs, scratch, 10,
        later, traj, traj_halo, spread, later_edges, z_left, z_right, first_any=True,
    )[0]


def tangent_second(earlier, pulled, variance, traj, traj_halo, var_halo):
    _, total, columns = variance.shape
    end = total + extra(total)

    def kernel(earlier_in, pulled_in, variance_in, traj_in, traj_halo_in, var_halo_in, ahead, increment, earl, pulled, variance,
               traj, traj_halo, var_halo, wide_a, wide_b, e_own, p_own, e_fold, p_fold, inc, out, sems):
        copies = Copies(sems)
        edge_copies = copies.rows([(earlier_in, 0, end)], total, end, e_fold)
        edge_copies += copies.rows([(pulled_in, 0, end)], total, end, p_fold)
        ready = fetch(copies, total, (earlier_in, earl), (pulled_in, pulled), (variance_in, variance), (var_halo_in, var_halo))
        traj_ready = fetch(copies, total, (traj_in, traj), (traj_halo_in, traj_halo))
        wait(edge_copies)
        unfold_in(e_fold, e_own)
        unfold_in(p_fold, p_own)

        def get(s):
            e_lanes, p_lanes = e_own[rows_at(s), :], p_own[rows_at(s), :]
            tiles = []
            for f in range(3):
                own = [tile_of(earl, f, s, t) - tile_of(variance, f, s, t) * tile_of(pulled, f, s, t) for t in range(2)]
                for t in range(2):
                    set_tile(inc, f, s, t, own[t])
                tiles.append(own + [halo_of(e_lanes, f) - var_halo[f, rows_at(s), :] * halo_of(p_lanes, f)])
            return tiles

        def put(s, new):
            for f in range(3):
                for t in range(2):
                    set_tile(out, f, s, t, -new[f][t])

        leaving = []

        def done(low, high):
            leaving.extend(copies.rows([(out, 0, total)], low, high, ahead.at[:, low:high, :]))
            leaving.extend(copies.rows([(inc, 0, total)], low, high, increment.at[:, low:high, :]))

        run_tangent(total, get, ready, traj, traj_halo, wide_a, wide_b, traj_ready, put, done)
        wait(leaving)

    outs = [f32(3, total, columns)] * 2
    scratch = [vmem(3, total, columns)] * 3 + [vmem(6, total, columns, dtype=traj.dtype), vmem(6, total, LANE, dtype=traj.dtype)]
    scratch += [vmem(3, total, LANE)] + [wide_scratch(total)] * 2 + [vmem(total, LANE)] * 2
    scratch += [vmem(3, extra(total), columns)] * 2 + [vmem(3, total, columns)] * 2
    scratch += [pltpu.SemaphoreType.DMA((8 * len(segments(total)) + 2,))]
    return call(
        "tangent_second", kernel, [ANY] * 6, outs, scratch, 16,
        earlier, pulled, variance, traj, traj_halo, var_halo, outs_any=True,
    )


def adjoint_second(later, traj, traj_halo, spread, last, pulled):
    _, total, columns = last.shape
    end = total + extra(total)

    def kernel(later_in, traj_in, traj_halo_in, spread_in, last_in, pulled_in, sums, later, traj, traj_halo, spread, last, pulled,
               wide_a, wide_b, flux_a, flux_b, own, fold, sems):
        copies = Copies(sems)
        edge_copies = copies.rows([(later_in, 0, end)], total, end, fold)
        ready = fetch(copies, total, (later_in, later), (traj_in, traj), (traj_halo_in, traj_halo))
        begin_put = fetch(copies, total, (spread_in, spread), (last_in, last), (pulled_in, pulled))
        wait(edge_copies)
        unfold_in(fold, own)
        sums[...] = jnp.zeros_like(sums)

        def get(s):
            lanes = own[rows_at(s), :]
            return [[tile_of(later, f, s, t) for t in range(2)] + [halo_of(lanes, f)] for f in range(3)]

        def put(s, new):
            parts = [jnp.zeros((GROUP, LANE), F32)] * 3
            for f in range(3):
                for t in range(2):
                    value = tile_of(spread, f, s, t) - new[f][t]
                    for k, other in enumerate((tile_of(last, f, s, t), tile_of(pulled, f, s, t), value)):
                        parts[k] = parts[k] + other * value
            for k in range(3):
                sums[k] = sums[k] + parts[k]

        run_adjoint(total, get, ready, traj, traj_halo, wide_a, wide_b, flux_a, flux_b, put, begin_put, lambda low, high: None)

    scratch = [vmem(3, total, columns), vmem(6, total, columns, dtype=traj.dtype), vmem(6, total, LANE, dtype=traj.dtype)]
    scratch += [vmem(3, total, columns)] * 3 + [wide_scratch(total)] * 4 + [vmem(total, LANE), vmem(3, extra(total), columns)]
    scratch += [pltpu.SemaphoreType.DMA((6 * len(segments(total)) + 1,))]
    outs = [f32(3, GROUP, LANE)]
    return call("adjoint_second", kernel, [ANY] * 6, outs, scratch, 16, later, traj, traj_halo, spread, last, pulled)[0]


def observe(parts, total, where):
    count = where.shape[0]

    def kernel(*refs):
        parts_in, (where_smem, column, out, field, picked, sems) = refs[: len(parts)], refs[len(parts) :]
        copies = Copies(sems)
        started = []
        for f in range(3):
            source = [(ref.at[f], at, rows) for ref, at, rows in placed(parts_in, parts)]
            started += copies.rows(source, 0, total, field.at[f * total : (f + 1) * total])
        wait(started)

        def step(i, carry):
            row = lax.shift_right_logical(where_smem[i], 8)
            picked[pl.ds(i, 1), :] = field[pl.ds(row, 1), :]
            return carry

        lax.fori_loop(0, count, step, 0, unroll=16)
        lane = iota((LANE, LANE), 1).astype(F32)
        for j in range(count // LANE):
            cut = slice(j * LANE, (j + 1) * LANE)
            at = jnp.broadcast_to(column[j : j + 1, :], (LANE, LANE)).T
            kept = jnp.where(lane == at, picked[cut, :LANE], 0.0)
            kept = kept + jnp.where(lane + float(LANE) == at, picked[cut, LANE:], 0.0)
            out[j : j + 1, :] = jnp.sum(kept.T, axis=0, keepdims=True)

    columns = 2 * LANE
    column = (where % columns).astype(F32).reshape(-1, LANE)
    return pl.pallas_call(
        kernel,
        in_specs=[ANY] * len(parts) + [pl.BlockSpec(memory_space=pltpu.SMEM)] + whole(1),
        out_specs=whole(1)[0],
        out_shape=f32(count // LANE, LANE),
        scratch_shapes=[vmem(3 * total, columns), vmem(count, columns), pltpu.SemaphoreType.DMA((3 * len(parts),))],
        compiler_params=PARAMS,
        cost_estimate=cost(3),
        name="observe",
    )(*[part[0] for part in parts], where, column)


def scatter(where, values, total):
    count = where.shape[0]

    def kernel(where_smem, values_smem, field):
        field[...] = jnp.zeros_like(field)
        lane = iota((1, 2 * LANE), 1)

        def step(i, carry):
            index = where_smem[i]
            at = (pl.ds(lax.shift_right_logical(index, 8), 1), slice(None))
            field[at] = field[at] + jnp.where(lane == (index & (2 * LANE - 1)), values_smem[i], 0.0)
            return carry

        lax.fori_loop(0, count, step, 0, unroll=8)

    return pl.pallas_call(
        kernel,
        in_specs=[pl.BlockSpec(memory_space=pltpu.SMEM)] * 2,
        out_specs=whole(1)[0],
        out_shape=f32(3 * total, 2 * LANE),
        compiler_params=PARAMS,
        cost_estimate=cost(3),
        name="scatter",
    )(where, values).reshape(3, total, 2 * LANE)


def one_sum(value):
    return jnp.sum(jnp.sum(value, axis=1, keepdims=True), axis=0, keepdims=True)


def pieces(cuts):
    return [(at, min(at + BLOCK, high)) for low, high in cuts for at in range(low, high, BLOCK)]


def summed(values):
    total = values[0]
    for value in values[1:]:
        total = total + value
    return total


def row_products(pairs, arrays, low, high, finish=None):
    columns = arrays[0][0][0].shape[2]
    counts = [len(parts) for parts in arrays]
    cuts = pieces([(low, high)])
    if finish:
        devices, early, a_before, d_parts, obs = finish
        scalars = [early] + a_before + d_parts + list(obs)
        out = f32(devices, 8, LANE)
    else:
        scalars = []
        out = f32(len(pairs), GROUP, columns)

    def kernel(*refs):
        refs = list(refs)
        inputs = []
        for parts in arrays:
            inputs.append([(refs.pop(0), at, count) for _, at, count in parts])
        extras, refs = refs[: len(scalars)], refs[len(scalars) :]
        out_ref, held, sems = refs[0], refs[1:-1], refs[-1]
        copies = Copies(sems)
        started = []
        for begin, end in cuts:
            group = []
            for parts, scratch in zip(inputs, held):
                group += copies.rows(parts, begin, end, scratch.at[:, begin - low : end - low, :])
            started.append(group)
        sums = tuple(jnp.zeros((GROUP, columns), F32) for _ in pairs)
        for (begin, end), group in zip(cuts, started):
            wait(group)

            def step(i, carry, begin=begin):
                at = pl.ds(pl.multiple_of(begin - low + i * GROUP, GROUP), GROUP)
                parts = list(carry)
                for f in range(3):
                    tiles = [a[f, at, :] for a in held]
                    for k, (one, two) in enumerate(pairs):
                        parts[k] = parts[k] + tiles[one] * tiles[two]
                return tuple(parts)

            sums = lax.fori_loop(0, (end - begin) // GROUP, step, sums)
        if not finish:
            for k, value in enumerate(sums):
                out_ref[k] = value
            return
        early_ref, extras = extras[0], extras[1:]
        before, d_refs, (o0, o1, o2) = extras[: len(a_before)], extras[len(a_before) : -3], (e[...] for e in extras[-3:])
        tail = [
            summed([one_sum(summed([sums[k]] + [r[k] for r in before]))] + [one_sum(summed([r[k] for r in d_refs]))])
            for k in range(3)
        ]
        head = [one_sum(early_ref[2 * k] + early_ref[2 * k + 1]) for k in range(3)]
        values = (
            head[0] + one_sum(o0 * o0),
            head[1] + one_sum(o0 * o1),
            tail[0] + one_sum(o0 * o2),
            head[2] + one_sum(o1 * o1),
            tail[1] + one_sum(o1 * o2),
            tail[2] + one_sum(o2 * o2),
        )
        lane = iota((8, LANE), 1)
        row = jnp.zeros((8, LANE), F32)
        for k, value in enumerate(values):
            row = jnp.where(lane == k, value, row)
        for k in range(devices):
            out_ref[k] = row

    return pl.pallas_call(
        kernel,
        in_specs=[ANY] * sum(counts) + whole(len(scalars)),
        out_specs=whole(1)[0],
        out_shape=out,
        scratch_shapes=[vmem(3, high - low, columns) for _ in arrays]
        + [pltpu.SemaphoreType.DMA((len(cuts) * (sum(counts)),))],
        compiler_params=PARAMS,
        cost_estimate=cost(9, 1),
        name="last_products" if finish else "products",
    )(*[part[0] for parts in arrays for part in parts], *scalars)


def weights(s00, s01, s02, s11, s12, s22):
    alpha = s01 / s00
    t11 = s11 - alpha * s01
    along = (s12 - alpha * s02) / t11
    beta = jnp.sqrt(s00)
    gamma = 1.0 / jnp.sqrt(t11)
    h00 = 1.0 + alpha
    h10_square = t11 / s00
    h10 = jnp.sqrt(h10_square)
    h01 = (s02 - alpha * s01) * gamma / beta
    h11 = 1.0 - alpha + along
    h21_square = (s22 - s02 * (s02 / s00) - along * (s12 - alpha * s02)) / t11
    g00 = h00 * h00 + h10_square
    g01 = h00 * h01 + h10 * h11
    g11 = h01 * h01 + h11 * h11 + h21_square
    q0 = beta * h00
    q1 = beta * h01
    det = g00 * g11 - g01 * g01
    y0 = (g11 * q0 - g01 * q1) / det
    y1 = (g00 * q1 - g01 * q0) / det
    c1 = y1 * gamma
    return (y0 / beta - c1 * alpha, c1)


def result(received, arrays, cuts, middle, m1, obs_part):
    total, columns = cuts[-1][1], arrays[0][0][0].shape[2]
    counts = [len(parts) for parts in arrays]
    small = pieces(cuts)

    def kernel(*refs):
        refs = list(refs)
        inputs = []
        for parts in arrays:
            inputs.append([(refs.pop(0), at, count) for _, at, count in parts])
        received, middle, m1, obs_part, multiplier, increment, dual = refs[:7]
        held, (multi, incr, coefs, sems) = refs[7:11], refs[11:]
        copies = Copies(sems)
        started = []
        for begin, end in small:
            group = []
            for parts, scratch in zip(inputs, held):
                group += copies.rows(parts, begin, end, scratch.at[:, begin:end, :])
            started.append(group)
        sums = jnp.sum(received[...], axis=0)
        lane = iota((8, LANE), 1)
        scalars = [
            jnp.broadcast_to(jnp.sum(jnp.where(lane == k, sums, 0.0), axis=1, keepdims=True), (8, LANE))
            for k in range(6)
        ]
        c0, c1 = weights(*scalars)
        coefs[0] = c0
        coefs[1] = c1
        dual[...] = (c0[0:1] * middle[...] + c1[0:1] * m1[...]) / obs_part[...]
        last, d1, inc0, inc1 = held
        leaving = []
        for (begin, end), group in zip(small, started):
            wait(group)

            def step(i, carry, begin=begin):
                start = pl.ds(pl.multiple_of(begin + i * GROUP, GROUP), GROUP)
                c0, c1 = (jnp.concatenate([coefs[k]] * 2, axis=0) for k in range(2))
                for f in range(3):
                    for t in range(2):
                        at = (f, start, slice(t * LANE, (t + 1) * LANE))
                        multi[at] = c0 * last[at] + c1 * d1[at]
                        incr[at] = c0 * inc0[at] + c1 * inc1[at]
                return carry

            lax.fori_loop(0, (end - begin) // GROUP, step, 0)
            leaving += copies.rows([(multi.at[:, begin:end, :], begin, end - begin)], begin, end, multiplier.at[:, begin:end, :])
            leaving += copies.rows([(incr.at[:, begin:end, :], begin, end - begin)], begin, end, increment.at[:, begin:end, :])
        wait(leaving)

    shape = (3, total, columns)
    return pl.pallas_call(
        kernel,
        in_specs=[ANY] * sum(counts) + whole(4),
        out_specs=[ANY, ANY] + whole(1),
        out_shape=[f32(*shape)] * 2 + [f32(*middle.shape)],
        scratch_shapes=[vmem(*shape)] * 6
        + [vmem(2, 8, LANE), pltpu.SemaphoreType.DMA((len(small) * (sum(counts) + 2),))],
        compiler_params=PARAMS,
        cost_estimate=cost(18, 1),
        name="result",
    )(*[part[0] for parts in arrays for part in parts], received, middle, m1, obs_part)


def moved(block, axis, distance, wrap):
    size = lax.axis_size(axis)
    if wrap:
        route = [(i, (i + distance) % size) for i in range(size)]
    else:
        route = [(i, i + distance) for i in range(size) if 0 <= i + distance < size]
    return lax.ppermute(block, axis, route)


def after(value, other):
    return lax.optimization_barrier((value, other))


def part(array, at, count=None):
    return (array, at, array.shape[1] if count is None else count)


def shards(rhs_state, innovations, trajectory, model_var, obs_var, obs_index, control_rhs):
    total, columns = rhs_state.shape[2:]
    first, last, variance = rhs_state[0], control_rhs[0], model_var[0]
    traj = trajectory.reshape(-1, total, columns)
    where = obs_index[0]
    middle, obs_part = innovations[0].reshape(-1, LANE), obs_var[0].reshape(-1, LANE)

    later = moved(last, "tm", -1, False)
    to_right, to_left, inc0 = edges_call(first, last, variance, traj)
    from_left = moved(to_right, "lon", 1, True)
    from_right = moved(to_left, "lon", -1, True)
    ahead, traj_halo, var_halo, last_edges = tangent_first(inc0, traj, from_left, from_right)
    later_edges = moved(last_edges, "tm", -1, False)
    a1 = moved(ahead, "tm", 1, False)
    z0 = scatter(where, (middle / obs_part).reshape(-1), total)
    z_right, z_left = spread_edges_call(z0)
    z_left, z_right = moved(z_right, "lon", 1, True), moved(z_left, "lon", -1, True)
    m1 = observe([part(inc0, 0)], total, where)
    m1, later_edges = after(m1, later_edges)
    d1 = adjoint_first(later, later_edges, traj, traj_halo, z0, z_left, z_right)

    d1_later = moved(d1, "tm", -1, False)
    ahead2, inc1 = tangent_second(a1, d1, variance, traj, traj_halo, var_halo)
    a2 = moved(ahead2, "tm", 1, False)
    z1 = scatter(where, (m1 / obs_part).reshape(-1), total)
    m2 = observe([part(inc1, 0)], total, where)
    a1, d1 = part(a1, 0, total), part(d1, 0, total)
    early = row_products(
        ((0, 0), (1, 1), (0, 2), (1, 3), (2, 2), (3, 3)), ([part(first, 0)], [part(last, 0)], [a1], [d1]), 0, total
    )
    d_sums = [adjoint_second(d1_later, traj, traj_halo, z1, last, d1[0])]
    devices = lax.axis_size("tm") * lax.axis_size("lon")
    sent = row_products(
        ((0, 2), (1, 2), (2, 2)),
        ([part(first, 0)], [a1], [part(a2, 0)]),
        0,
        total,
        (devices, early, [], d_sums, (middle, m1, m2)),
    )
    received = lax.all_to_all(sent, ("tm", "lon"), 0, 0)
    multiplier, increment, dual = result(
        received,
        ([part(last, 0)], [d1], [part(inc0, 0)], [part(inc1, 0)]),
        [(0, total)],
        middle,
        m1,
        obs_part,
    )
    return (multiplier[None], dual.reshape(1, -1), increment[None])


def solution(mesh):
    in_specs = (
        P("tm", None, None, "lon"),
        P("tm", "lon"),
        P("tm", None, None, None, "lon"),
        P("tm", None, None, "lon"),
        P("tm", "lon"),
        P("tm", "lon"),
        P("tm", None, None, "lon"),
    )
    out_specs = (P("tm", None, None, "lon"), P("tm", "lon"), P("tm", None, None, "lon"))
    return jax.shard_map(shards, mesh=mesh, in_specs=in_specs, out_specs=out_specs, check_vma=False)
```

```python
import jax
import jax.numpy as jnp
from jax import lax
from jax.experimental import pallas as pl
from jax.experimental.pallas import tpu as pltpu
from jax.sharding import PartitionSpec as P

courant = 0.25
coriolis = 0.2
slope = 0.5 * courant

LANE = 128
BLOCK = 256
GROUP = 16
MARGIN = 8
HALO = 4
TRAJ, INC, VAR, LAST, PLANES = 0, 6, 9, 12, 16
MAIN = PLANES * HALO
F32 = jnp.float32
PARAMS = pltpu.CompilerParams(vmem_limit_bytes=56 * 1024 * 1024)


def iota(shape, dim):
    return lax.broadcasted_iota(jnp.int32, shape, dim)


def spread_shift(plane):
    return (LANE - (8 * plane + HALO)) % LANE


def pack_shift(plane):
    return (8 * plane + HALO) % LANE


def edges_of(planes, rows):
    lane = iota((rows, LANE), 1)
    packed = jnp.zeros((rows, LANE), F32)
    for number, plane in enumerate(planes):
        both = jnp.where(lane < LANE // 2, plane[:, :LANE], plane[:, LANE:])
        packed = jnp.where((lane >= 8 * number) & (lane < 8 * number + 8), pltpu.roll(both, pack_shift(number), 1), packed)
    return packed


def split_edges(turned, to_right, to_left, count):
    top = iota((8, turned.shape[1]), 0) < HALO
    for pair in range(count // 2):
        even = turned[16 * pair : 16 * pair + 8]
        odd = turned[16 * pair + 8 : 16 * pair + 16]
        to_right[8 * pair : 8 * pair + 8, :] = jnp.where(top, even, pltpu.roll(odd, HALO, 0))
        to_left[8 * pair : 8 * pair + 8, :] = jnp.where(top, pltpu.roll(even, HALO, 0), odd)


def joined_edges(from_left, from_right, count):
    top = iota((8, from_left.shape[1]), 0) < HALO
    pieces = []
    for pair in range(count // 2):
        left = from_left[8 * pair : 8 * pair + 8]
        right = from_right[8 * pair : 8 * pair + 8]
        pieces.append(jnp.where(top, left, pltpu.roll(right, HALO, 0)))
        pieces.append(jnp.where(top, pltpu.roll(left, HALO, 0), right))
    return jnp.concatenate(pieces, axis=0)


def padded_turn(message):
    rest = LANE - message.shape[0]
    if rest:
        message = jnp.concatenate([message, jnp.zeros((rest, message.shape[1]), F32)], axis=0)
    return message.T


def edges_kernel(increment, last, variance, traj, spread, to_right, to_left):
    rows = last.shape[1]
    planes = [traj[p].astype(F32) for p in range(6)]
    planes += [increment[f] for f in range(3)]
    planes += [variance[f] for f in range(3)]
    planes += [last[f] for f in range(3)]
    split_edges(edges_of(planes, rows).T, to_right.at[:MAIN], to_left.at[:MAIN], PLANES)
    spread_planes = [spread[f] for f in range(3)]
    split_edges(edges_of(spread_planes, rows).T, to_right.at[MAIN:], to_left.at[MAIN:], 4)


def edges_call(increment, last, variance, traj, spread):
    rows = last.shape[1]
    block = pl.BlockSpec((3, BLOCK, 2 * LANE), lambda i: (0, i, 0))
    sent = pl.BlockSpec((MAIN + 4 * HALO, BLOCK), lambda i: (0, i))
    return pl.pallas_call(
        edges_kernel,
        grid=(rows // BLOCK,),
        in_specs=[block, block, block, pl.BlockSpec((6, BLOCK, 2 * LANE), lambda i: (0, i, 0)), block],
        out_specs=[sent, sent],
        out_shape=[jax.ShapeDtypeStruct((MAIN + 4 * HALO, rows), F32)] * 2,
        compiler_params=PARAMS,
        cost_estimate=cost(16),
        name="edges",
    )(increment, last, variance, traj, spread)


def x_differences(tiles, first_lane, last_lane, joined):
    count = len(tiles)
    ahead = [pltpu.roll(t, LANE - 1, 1) for t in tiles]
    behind = [pltpu.roll(t, 1, 1) for t in tiles]
    if not joined:
        return [a - b for a, b in zip(ahead, behind)]
    return [
        jnp.where(last_lane, ahead[(t + 1) % count], ahead[t])
        - jnp.where(first_lane, behind[(t - 1) % count], behind[t])
        for t in range(count)
    ]


def rotation_at(start, total):
    position = (iota((GROUP, LANE), 0) + start).astype(F32)
    return coriolis * ((2.0 * position + 1.0) / total - 1.0)


def lane_ends():
    lane = iota((GROUP, LANE), 1)
    return lane == 0, lane == LANE - 1


def rows_at(start, offset=0):
    return pl.ds(pl.multiple_of(start + offset, GROUP), GROUP)


def traj_tiles(traj, traj_halo, step, start):
    out = []
    for plane in range(3 * step, 3 * step + 3):
        tiles = []
        if traj is not None:
            tiles += [traj[plane, rows_at(start), t * LANE : (t + 1) * LANE] for t in range(2)]
        if traj_halo is not None:
            at = [traj_halo.at[plane]] if len(traj_halo.shape) == 3 else [traj_halo.at[plane, t] for t in range(2)]
            tiles += [ref[rows_at(start), :] for ref in at]
        out.append([t.astype(F32) for t in tiles])
    return out


def load_rows(ref, start, offset):
    return [
        [ref[f, t, pl.ds(start + (MARGIN + offset), GROUP), :] for t in range(ref.shape[1])] for f in range(3)
    ]


def store_rows(ref, start, value):
    for f in range(3):
        for t in range(ref.shape[1]):
            ref[f, t, pl.ds(start + MARGIN, GROUP), :] = value[f][t]


def clear_margins(ref):
    rows = ref.shape[2]
    zero = jnp.zeros((MARGIN, LANE), F32)
    for f in range(3):
        for t in range(ref.shape[1]):
            ref[f, t, 0:MARGIN, :] = zero
            ref[f, t, rows - MARGIN : rows, :] = zero


def tangent_rows(source, traj, traj_halo, step, start, total, joined=True):
    here, above, below = (load_rows(source, start, k) for k in (0, 1, -1))
    trajectory = traj_tiles(traj, traj_halo, step, start)
    turn = rotation_at(start, total)
    ends = lane_ends()
    dx = [x_differences(here[f], *ends, joined) for f in range(3)]
    new = [[], [], []]
    for t in range(source.shape[1]):
        b, e, n = (trajectory[f][t] for f in range(3))
        h, u, v = (here[f][t] for f in range(3))
        xh, xu, xv = (dx[f][t] for f in range(3))
        yh, yu, yv = (above[f][t] - below[f][t] for f in range(3))
        new[0].append(h - slope * (b * (xu + yv) + e * xh + n * yh))
        new[1].append(u - slope * (xh + e * xu + n * yu) + turn * v)
        new[2].append(v - slope * (yh + e * xv + n * yv) - turn * u)
    return new


def north_rows(field, trajectory):
    out = [[], [], []]
    for t in range(3):
        b, _, n = (trajectory[f][t] for f in range(3))
        p, q, w = (field[f][t] for f in range(3))
        out[0].append(n * p + w)
        out[1].append(n * q)
        out[2].append(b * p + n * w)
    return out


def adjoint_rows(source, flux, traj, traj_halo, step, start, total):
    here = load_rows(source, start, 0)
    above, below = (load_rows(flux, start, k) for k in (1, -1))
    trajectory = traj_tiles(traj, traj_halo, step, start)
    turn = rotation_at(start, total)
    ends = lane_ends()
    east = [[], [], []]
    for t in range(3):
        b, e, _ = (trajectory[f][t] for f in range(3))
        p, q, w = (here[f][t] for f in range(3))
        east[0].append(e * p + q)
        east[1].append(b * p + e * q)
        east[2].append(e * w)
    dx = [x_differences(east[f], *ends, True) for f in range(3)]
    new = [[], [], []]
    for t in range(3):
        p, q, w = (here[f][t] for f in range(3))
        change = [slope * (dx[f][t] + (above[f][t] - below[f][t])) for f in range(3)]
        new[0].append(p + change[0])
        new[1].append(q + change[1] - turn * w)
        new[2].append(w + change[2] + turn * q)
    return new


def over_rows(begin, end, body):
    count = (end - begin) // GROUP
    unroll = next(u for u in (8, 6, 5, 4, 3, 2, 1) if count % u == 0)

    def step(i, carry):
        body(pl.multiple_of(begin + i * GROUP, GROUP))
        return carry

    lax.fori_loop(0, count, step, 0, unroll=unroll)


def padded(rows):
    return -(-rows // (2 * LANE)) * 2 * LANE


def extra(rows):
    return 8 * padded(rows) // (2 * LANE)


def turn_in(message, packed_ref):
    for j in range(message.shape[1] // LANE):
        packed_ref[j * LANE : (j + 1) * LANE, :] = padded_turn(message[:, j * LANE : (j + 1) * LANE])


def unfold_in(folded, packed_ref):
    for j in range(packed_ref.shape[0] // LANE):
        at = (slice(j // 2 * 8, j // 2 * 8 + 8), slice(j % 2 * LANE, (j % 2 + 1) * LANE))
        message = jnp.concatenate([folded[(f,) + at] for f in range(folded.shape[0])], axis=0)
        packed_ref[j * LANE : (j + 1) * LANE, :] = padded_turn(message)


def turn_out(halo, payload, behind):
    low = iota((8, LANE), 0) < HALO
    for j in range(halo.shape[1] // LANE):
        for f in range(halo.shape[0]):
            turned = halo[f, j * LANE : (j + 1) * LANE, :].T
            ends = jnp.where(low, turned[:8], turned[LANE - 8 :])
            row = behind + j // 2 * 8
            payload[f, row : row + 8, j % 2 * LANE : (j % 2 + 1) * LANE] = pltpu.roll(ends, HALO, 0)


def wide_scratch(rows, tiles=3):
    return pltpu.VMEM((3, tiles, rows + 2 * MARGIN, LANE), F32)


def tile_of(ref, f, start, t, offset=0):
    return ref[f, rows_at(start, offset), t * LANE : (t + 1) * LANE]


def set_tile(ref, f, start, t, value, offset=0):
    ref[f, rows_at(start, offset), t * LANE : (t + 1) * LANE] = value


class Copies:
    def __init__(self, sems):
        self.sems, self.used = sems, 0

    def rows(self, parts, begin, end, target):
        started = []
        for ref, at, count in parts:
            low, high = max(begin, at), min(end, at + count)
            if low < high:
                source = ref.at[..., low - at : high - at, :]
                goal = target.at[..., low - begin : high - begin, :]
                copy = pltpu.make_async_copy(source, goal, self.sems.at[self.used])
                self.used += 1
                copy.start()
                started.append(copy)
        return started


def placed(refs, parts):
    return [(ref, at, count) for ref, (_, at, count) in zip(refs, parts)]


def wait(copies):
    for copy in copies:
        copy.wait()


def segments(total):
    return [(at, min(at + BLOCK, total)) for at in range(0, total, BLOCK)]


def fetch(copies, total, *pairs):
    return [
        [copy for source, target in pairs for copy in copies.rows([(source, 0, total)], low, high, target.at[..., low:high, :])]
        for low, high in segments(total)
    ]


def run_tangent(total, get, ready, traj, traj_halo, wide_a, wide_b, traj_ready, put, done, joined=True):
    clear_margins(wide_a)
    clear_margins(wide_b)
    for (low, high), copies in zip(segments(total), ready):
        wait(copies)
        over_rows(low, high, lambda s: store_rows(wide_a, s, get(s)))
    for (low, high), copies in zip(segments(total), traj_ready):
        wait(copies)
        over_rows(
            low, high, lambda s: store_rows(wide_b, s, tangent_rows(wide_a, traj, traj_halo, 0, s, total, joined))
        )
    for low, high in segments(total):
        over_rows(low, high, lambda s: put(s, tangent_rows(wide_b, traj, traj_halo, 1, s, total, joined)))
        done(low, high)


def run_adjoint(total, get, ready, traj, traj_halo, wide_a, wide_b, flux_a, flux_b, put, begin_put, done):
    clear_margins(flux_a)
    clear_margins(flux_b)

    def begin(s):
        field = get(s)
        store_rows(wide_a, s, field)
        store_rows(flux_a, s, north_rows(field, traj_tiles(traj, traj_halo, 1, s)))

    def middle(s):
        field = adjoint_rows(wide_a, flux_a, traj, traj_halo, 1, s, total)
        store_rows(wide_b, s, field)
        store_rows(flux_b, s, north_rows(field, traj_tiles(traj, traj_halo, 0, s)))

    for (low, high), copies in zip(segments(total), ready):
        wait(copies)
        over_rows(low, high, begin)
    over_rows(0, total, middle)
    for (low, high), copies in zip(segments(total), begin_put):
        wait(copies)
        over_rows(low, high, lambda s: put(s, adjoint_rows(wide_b, flux_b, traj, traj_halo, 0, s, total)))
        done(low, high)


def halo_of(lanes, plane):
    return pltpu.roll(lanes, spread_shift(plane), 1)


ANY = pl.BlockSpec(memory_space=pltpu.HBM)


def whole(count):
    return [pl.BlockSpec(memory_space=pltpu.VMEM)] * count


def cost(mib, steps=2):
    return pl.CostEstimate(flops=2**10, bytes_accessed=mib * 2**20, transcendentals=0)


def f32(*shape):
    return jax.ShapeDtypeStruct(shape, F32)


def vmem(*shape, dtype=F32):
    return pltpu.VMEM(shape, dtype)


def call(name, kernel, ins, outs, scratch, mib, *args, first_any=False, outs_any=False):
    specs = [ANY if outs_any or (first_any and k == 0) else whole(1)[0] for k in range(len(outs))]
    return pl.pallas_call(
        kernel,
        in_specs=ins,
        out_specs=specs,
        out_shape=outs,
        scratch_shapes=scratch,
        compiler_params=PARAMS,
        cost_estimate=cost(mib),
        name=name,
    )(*args)


def tangent_band(first, last, variance, traj):
    _, total, columns = first.shape

    def kernel(first_in, last_in, variance_in, traj_in, ahead, increment, first, last, variance, traj, wide_a, wide_b, out, sems):
        copies = Copies(sems)
        ready = fetch(copies, total, (first_in, first), (last_in, last), (variance_in, variance))
        traj_ready = fetch(copies, total, (traj_in, traj))

        def get(s):
            tiles = [
                [tile_of(first, f, s, t) - tile_of(variance, f, s, t) * tile_of(last, f, s, t) for t in range(2)]
                for f in range(3)
            ]
            for f in range(3):
                for t in range(2):
                    set_tile(first, f, s, t, tiles[f][t])
            return tiles

        def put(s, new):
            for f in range(3):
                for t in range(2):
                    set_tile(out, f, s, t, -new[f][t])

        leaving = []

        def done(low, high):
            leaving.extend(copies.rows([(out, 0, total)], low, high, ahead.at[:, low:high, :]))
            leaving.extend(copies.rows([(first, 0, total)], low, high, increment.at[:, low:high, :]))

        run_tangent(total, get, ready, traj, None, wide_a, wide_b, traj_ready, put, done)
        wait(leaving)

    outs = [f32(*first.shape)] * 2
    scratch = [vmem(*first.shape)] * 3 + [vmem(*traj.shape, dtype=traj.dtype)] + [wide_scratch(total, 2)] * 2
    scratch += [vmem(*first.shape), pltpu.SemaphoreType.DMA((6 * len(segments(total)),))]
    return call("tangent_band", kernel, [ANY] * 4, outs, scratch, 18, first, last, variance, traj, outs_any=True)


def tangent_seams(increment, traj, from_left, from_right):
    _, total, columns = increment.shape

    def kernel(inc_in, traj_in, from_left, from_right, edges, traj_halo, var_halo, last_edges, spread_halo, inc, traj, wide_a, wide_b, seams, inc_halo, out, sems):
        copies = Copies(sems)
        inc_ready = fetch(copies, total, (inc_in, inc))
        traj_ready = fetch(copies, total, (traj_in, traj))
        left_part = iota((LANE, LANE), 1) < LANE // 2
        for j in range(total // LANE):
            cut = slice(j * LANE, (j + 1) * LANE)
            joined = joined_edges(from_left[:MAIN, cut], from_right[:MAIN, cut], PLANES)
            last_edges[:, cut] = joined[8 * LAST : 8 * LAST + 24]
            packed = joined.T
            spread = padded_turn(joined_edges(from_left[MAIN:, cut], from_right[MAIN:, cut], 4))
            for plane in range(6):
                traj_halo[plane, cut, :] = halo_of(packed, TRAJ + plane).astype(traj_halo.dtype)
            for f in range(3):
                var_halo[f, cut, :] = halo_of(packed, VAR + f)
                inc_halo[f, cut, :] = halo_of(packed, INC + f)
                spread_halo[f, cut, :] = halo_of(spread, f)
        for copies_of in inc_ready + traj_ready:
            wait(copies_of)
        for j in range(total // LANE):
            cut = slice(j * LANE, (j + 1) * LANE)
            for plane in range(6):
                halo = traj_halo[plane, cut, :].astype(F32)
                own = [traj[plane, cut, t * LANE : (t + 1) * LANE].astype(F32) for t in range(2)]
                seams[plane, 0, cut, :] = jnp.where(left_part, own[0], halo).astype(seams.dtype)
                seams[plane, 1, cut, :] = jnp.where(left_part, halo, own[1]).astype(seams.dtype)

        def get(s):
            left = iota((GROUP, LANE), 1) < LANE // 2
            tiles = []
            for f in range(3):
                halo = inc_halo[f, rows_at(s), :]
                tiles.append([jnp.where(left, tile_of(inc, f, s, 0), halo), jnp.where(left, halo, tile_of(inc, f, s, 1))])
            return tiles

        def put(s, new):
            for f in range(3):
                for t in range(2):
                    out[2 * f + t, rows_at(s), :] = -new[f][t]

        nothing = [[] for _ in segments(total)]
        run_tangent(total, get, nothing, None, seams, wide_a, wide_b, nothing, put, lambda low, high: None, False)
        turn_out(out, edges, 0)

    outs = [f32(6, extra(total), columns), jax.ShapeDtypeStruct((6, total, LANE), traj.dtype)]
    outs += [f32(3, total, LANE), f32(24, total), f32(3, total, LANE)]
    scratch = [vmem(*increment.shape), vmem(*traj.shape, dtype=traj.dtype)] + [wide_scratch(total, 2)] * 2
    scratch += [vmem(6, 2, total, LANE, dtype=traj.dtype), vmem(3, total, LANE), vmem(6, total, LANE)]
    scratch += [pltpu.SemaphoreType.DMA((2 * len(segments(total)),))]
    return call("tangent_seams", kernel, [ANY, ANY] + whole(2), outs, scratch, 10, increment, traj, from_left, from_right)


def adjoint_first(later, later_edges, traj, traj_halo, spread, spread_halo):
    _, total, columns = later.shape

    def kernel(later_in, traj_in, traj_halo_in, spread_in, spread_halo_in, later_edges, pulled, later, traj, traj_halo, spread,
               wide_a, wide_b, flux_a, flux_b, own, halo, out, sems):
        copies = Copies(sems)
        ready = fetch(copies, total, (later_in, later), (traj_in, traj), (traj_halo_in, traj_halo))
        begin_put = fetch(copies, total, (spread_in, spread), (spread_halo_in, halo))
        turn_in(later_edges, own)

        def get(s):
            lanes = own[rows_at(s), :]
            return [[tile_of(later, f, s, t) for t in range(2)] + [halo_of(lanes, f)] for f in range(3)]

        def put(s, new):
            for f in range(3):
                for t in range(2):
                    set_tile(out, f, s, t, tile_of(spread, f, s, t) - new[f][t])
                halo[f, rows_at(s), :] = halo[f, rows_at(s), :] - new[f][2]

        leaving = []

        def done(low, high):
            leaving.extend(copies.rows([(out, 0, total)], low, high, pulled.at[:, low:high, :]))

        run_adjoint(total, get, ready, traj, traj_halo, wide_a, wide_b, flux_a, flux_b, put, begin_put, done)
        turn_out(halo, out, total)
        end = total + extra(total)
        leaving.extend(copies.rows([(out, 0, end)], total, end, pulled.at[:, total:end, :]))
        wait(leaving)

    outs = [f32(3, total + extra(total), columns)]
    scratch = [vmem(3, total, columns), vmem(6, total, columns, dtype=traj.dtype), vmem(6, total, LANE, dtype=traj.dtype)]
    scratch += [vmem(3, total, columns)] + [wide_scratch(total)] * 4 + [vmem(total, LANE)]
    scratch += [vmem(3, total, LANE), vmem(3, total + extra(total), columns)]
    scratch += [pltpu.SemaphoreType.DMA((6 * len(segments(total)) + 1,))]
    return call(
        "adjoint_first", kernel, [ANY] * 5 + whole(1), outs, scratch, 10,
        later, traj, traj_halo, spread, spread_halo, later_edges, first_any=True,
    )[0]


def tangent_second(earlier, earlier_edges, pulled, variance, traj, traj_halo, var_halo):
    _, total, columns = variance.shape
    end = total + extra(total)

    def kernel(earlier_in, edges_in, pulled_in, variance_in, traj_in, traj_halo_in, var_halo_in, ahead, increment, patched, earl, pulled, variance,
               traj, traj_halo, var_halo, wide_a, wide_b, e_own, p_own, e_fold, p_fold, inc, out, sems):
        copies = Copies(sems)
        edge_copies = copies.rows([(edges_in, 0, extra(total))], 0, extra(total), e_fold)
        edge_copies += copies.rows([(pulled_in, 0, end)], total, end, p_fold)
        ready = fetch(copies, total, (earlier_in, earl), (pulled_in, pulled), (variance_in, variance), (var_halo_in, var_halo))
        traj_ready = fetch(copies, total, (traj_in, traj), (traj_halo_in, traj_halo))
        wait(edge_copies)
        unfold_in(e_fold, e_own)
        unfold_in(p_fold, p_own)

        def get(s):
            e_lanes, p_lanes = e_own[rows_at(s), :], p_own[rows_at(s), :]
            lane = iota((GROUP, LANE), 1)
            tiles = []
            for f in range(3):
                left, right = halo_of(e_lanes, 2 * f), halo_of(e_lanes, 2 * f + 1)
                fixed = [
                    jnp.where(lane < 2, left, tile_of(earl, f, s, 0)),
                    jnp.where(lane >= LANE - 2, right, tile_of(earl, f, s, 1)),
                ]
                own = [fixed[t] - tile_of(variance, f, s, t) * tile_of(pulled, f, s, t) for t in range(2)]
                for t in range(2):
                    set_tile(earl, f, s, t, fixed[t])
                    set_tile(inc, f, s, t, own[t])
                beside = jnp.where(lane < LANE // 2, right, left)
                tiles.append(own + [beside - var_halo[f, rows_at(s), :] * halo_of(p_lanes, f)])
            return tiles

        def put(s, new):
            for f in range(3):
                for t in range(2):
                    set_tile(out, f, s, t, -new[f][t])

        leaving = []

        def done(low, high):
            leaving.extend(copies.rows([(out, 0, total)], low, high, ahead.at[:, low:high, :]))
            leaving.extend(copies.rows([(inc, 0, total)], low, high, increment.at[:, low:high, :]))
            leaving.extend(copies.rows([(earl, 0, total)], low, high, patched.at[:, low:high, :]))

        run_tangent(total, get, ready, traj, traj_halo, wide_a, wide_b, traj_ready, put, done)
        wait(leaving)

    outs = [f32(3, total, columns)] * 3
    scratch = [vmem(3, total, columns)] * 3 + [vmem(6, total, columns, dtype=traj.dtype), vmem(6, total, LANE, dtype=traj.dtype)]
    scratch += [vmem(3, total, LANE)] + [wide_scratch(total)] * 2 + [vmem(total, LANE)] * 2
    scratch += [vmem(6, extra(total), columns), vmem(3, extra(total), columns)] + [vmem(3, total, columns)] * 2
    scratch += [pltpu.SemaphoreType.DMA((9 * len(segments(total)) + 2,))]
    return call(
        "tangent_second", kernel, [ANY] * 7, outs, scratch, 16,
        earlier, earlier_edges, pulled, variance, traj, traj_halo, var_halo, outs_any=True,
    )


def adjoint_second(later, traj, traj_halo, spread, last, pulled):
    _, total, columns = last.shape
    end = total + extra(total)

    def kernel(later_in, traj_in, traj_halo_in, spread_in, last_in, pulled_in, sums, later, traj, traj_halo, spread, last, pulled,
               wide_a, wide_b, flux_a, flux_b, own, fold, sems):
        copies = Copies(sems)
        edge_copies = copies.rows([(later_in, 0, end)], total, end, fold)
        ready = fetch(copies, total, (later_in, later), (traj_in, traj), (traj_halo_in, traj_halo))
        begin_put = fetch(copies, total, (spread_in, spread), (last_in, last), (pulled_in, pulled))
        wait(edge_copies)
        unfold_in(fold, own)
        sums[...] = jnp.zeros_like(sums)

        def get(s):
            lanes = own[rows_at(s), :]
            return [[tile_of(later, f, s, t) for t in range(2)] + [halo_of(lanes, f)] for f in range(3)]

        def put(s, new):
            parts = [jnp.zeros((GROUP, LANE), F32)] * 3
            for f in range(3):
                for t in range(2):
                    value = tile_of(spread, f, s, t) - new[f][t]
                    for k, other in enumerate((tile_of(last, f, s, t), tile_of(pulled, f, s, t), value)):
                        parts[k] = parts[k] + other * value
            for k in range(3):
                sums[k] = sums[k] + parts[k]

        run_adjoint(total, get, ready, traj, traj_halo, wide_a, wide_b, flux_a, flux_b, put, begin_put, lambda low, high: None)

    scratch = [vmem(3, total, columns), vmem(6, total, columns, dtype=traj.dtype), vmem(6, total, LANE, dtype=traj.dtype)]
    scratch += [vmem(3, total, columns)] * 3 + [wide_scratch(total)] * 4 + [vmem(total, LANE), vmem(3, extra(total), columns)]
    scratch += [pltpu.SemaphoreType.DMA((6 * len(segments(total)) + 1,))]
    outs = [f32(3, GROUP, LANE)]
    return call("adjoint_second", kernel, [ANY] * 6, outs, scratch, 16, later, traj, traj_halo, spread, last, pulled)[0]


def observe(parts, total, where):
    count = where.shape[0]

    def kernel(*refs):
        parts_in, (where_smem, column, out, field, picked, sems) = refs[: len(parts)], refs[len(parts) :]
        copies = Copies(sems)
        started = []
        for f in range(3):
            source = [(ref.at[f], at, rows) for ref, at, rows in placed(parts_in, parts)]
            started += copies.rows(source, 0, total, field.at[f * total : (f + 1) * total])
        wait(started)

        def step(i, carry):
            row = lax.shift_right_logical(where_smem[i], 8)
            picked[pl.ds(i, 1), :] = field[pl.ds(row, 1), :]
            return carry

        lax.fori_loop(0, count, step, 0, unroll=16)
        lane = iota((LANE, LANE), 1).astype(F32)
        for j in range(count // LANE):
            cut = slice(j * LANE, (j + 1) * LANE)
            at = jnp.broadcast_to(column[j : j + 1, :], (LANE, LANE)).T
            kept = jnp.where(lane == at, picked[cut, :LANE], 0.0)
            kept = kept + jnp.where(lane + float(LANE) == at, picked[cut, LANE:], 0.0)
            out[j : j + 1, :] = jnp.sum(kept.T, axis=0, keepdims=True)

    columns = 2 * LANE
    column = (where % columns).astype(F32).reshape(-1, LANE)
    return pl.pallas_call(
        kernel,
        in_specs=[ANY] * len(parts) + [pl.BlockSpec(memory_space=pltpu.SMEM)] + whole(1),
        out_specs=whole(1)[0],
        out_shape=f32(count // LANE, LANE),
        scratch_shapes=[vmem(3 * total, columns), vmem(count, columns), pltpu.SemaphoreType.DMA((3 * len(parts),))],
        compiler_params=PARAMS,
        cost_estimate=cost(3),
        name="observe",
    )(*[part[0] for part in parts], where, column)


def scatter(where, values, total):
    count = where.shape[0]

    def kernel(where_smem, values_smem, field):
        field[...] = jnp.zeros_like(field)
        lane = iota((1, 2 * LANE), 1)

        def step(i, carry):
            index = where_smem[i]
            at = (pl.ds(lax.shift_right_logical(index, 8), 1), slice(None))
            field[at] = field[at] + jnp.where(lane == (index & (2 * LANE - 1)), values_smem[i], 0.0)
            return carry

        lax.fori_loop(0, count, step, 0, unroll=8)

    return pl.pallas_call(
        kernel,
        in_specs=[pl.BlockSpec(memory_space=pltpu.SMEM)] * 2,
        out_specs=whole(1)[0],
        out_shape=f32(3 * total, 2 * LANE),
        compiler_params=PARAMS,
        cost_estimate=cost(3),
        name="scatter",
    )(where, values).reshape(3, total, 2 * LANE)


def one_sum(value):
    return jnp.sum(jnp.sum(value, axis=1, keepdims=True), axis=0, keepdims=True)


def pieces(cuts):
    return [(at, min(at + BLOCK, high)) for low, high in cuts for at in range(low, high, BLOCK)]


def summed(values):
    total = values[0]
    for value in values[1:]:
        total = total + value
    return total


def row_products(pairs, arrays, low, high, finish=None):
    columns = arrays[0][0][0].shape[2]
    counts = [len(parts) for parts in arrays]
    cuts = pieces([(low, high)])
    if finish:
        devices, early, a_before, d_parts, obs = finish
        scalars = [early] + a_before + d_parts + list(obs)
        out = f32(devices, 8, LANE)
    else:
        scalars = []
        out = f32(len(pairs), GROUP, columns)

    def kernel(*refs):
        refs = list(refs)
        inputs = []
        for parts in arrays:
            inputs.append([(refs.pop(0), at, count) for _, at, count in parts])
        extras, refs = refs[: len(scalars)], refs[len(scalars) :]
        out_ref, held, sems = refs[0], refs[1:-1], refs[-1]
        copies = Copies(sems)
        started = []
        for begin, end in cuts:
            group = []
            for parts, scratch in zip(inputs, held):
                group += copies.rows(parts, begin, end, scratch.at[:, begin - low : end - low, :])
            started.append(group)
        sums = tuple(jnp.zeros((GROUP, columns), F32) for _ in pairs)
        for (begin, end), group in zip(cuts, started):
            wait(group)

            def step(i, carry, begin=begin):
                at = pl.ds(pl.multiple_of(begin - low + i * GROUP, GROUP), GROUP)
                parts = list(carry)
                for f in range(3):
                    tiles = [a[f, at, :] for a in held]
                    for k, (one, two) in enumerate(pairs):
                        parts[k] = parts[k] + tiles[one] * tiles[two]
                return tuple(parts)

            sums = lax.fori_loop(0, (end - begin) // GROUP, step, sums)
        if not finish:
            for k, value in enumerate(sums):
                out_ref[k] = value
            return
        early_ref, extras = extras[0], extras[1:]
        before, d_refs, (o0, o1, o2) = extras[: len(a_before)], extras[len(a_before) : -3], (e[...] for e in extras[-3:])
        tail = [
            summed([one_sum(summed([sums[k]] + [r[k] for r in before]))] + [one_sum(summed([r[k] for r in d_refs]))])
            for k in range(3)
        ]
        head = [one_sum(early_ref[2 * k] + early_ref[2 * k + 1]) for k in range(3)]
        values = (
            head[0] + one_sum(o0 * o0),
            head[1] + one_sum(o0 * o1),
            tail[0] + one_sum(o0 * o2),
            head[2] + one_sum(o1 * o1),
            tail[1] + one_sum(o1 * o2),
            tail[2] + one_sum(o2 * o2),
        )
        lane = iota((8, LANE), 1)
        row = jnp.zeros((8, LANE), F32)
        for k, value in enumerate(values):
            row = jnp.where(lane == k, value, row)
        for k in range(devices):
            out_ref[k] = row

    return pl.pallas_call(
        kernel,
        in_specs=[ANY] * sum(counts) + whole(len(scalars)),
        out_specs=whole(1)[0],
        out_shape=out,
        scratch_shapes=[vmem(3, high - low, columns) for _ in arrays]
        + [pltpu.SemaphoreType.DMA((len(cuts) * (sum(counts)),))],
        compiler_params=pltpu.CompilerParams(vmem_limit_bytes=20 * 1024 * 1024),
        cost_estimate=cost(9, 1),
        name="last_products" if finish else "products",
    )(*[part[0] for parts in arrays for part in parts], *scalars)


def weights(s00, s01, s02, s11, s12, s22):
    alpha = s01 / s00
    t11 = s11 - alpha * s01
    along = (s12 - alpha * s02) / t11
    beta = jnp.sqrt(s00)
    gamma = 1.0 / jnp.sqrt(t11)
    h00 = 1.0 + alpha
    h10_square = t11 / s00
    h10 = jnp.sqrt(h10_square)
    h01 = (s02 - alpha * s01) * gamma / beta
    h11 = 1.0 - alpha + along
    h21_square = (s22 - s02 * (s02 / s00) - along * (s12 - alpha * s02)) / t11
    g00 = h00 * h00 + h10_square
    g01 = h00 * h01 + h10 * h11
    g11 = h01 * h01 + h11 * h11 + h21_square
    q0 = beta * h00
    q1 = beta * h01
    det = g00 * g11 - g01 * g01
    y0 = (g11 * q0 - g01 * q1) / det
    y1 = (g00 * q1 - g01 * q0) / det
    c1 = y1 * gamma
    return (y0 / beta - c1 * alpha, c1)


def result(received, last, d1, inc0, inc1, middle, m1, obs_part):
    _, total, columns = last.shape

    def kernel(last, d1, inc0, inc1, received, middle, m1, obs_part, multiplier, increment, dual, multi, incr, sems):
        copies = Copies(sems)
        sums = jnp.sum(received[...], axis=0)
        lane = iota((8, LANE), 1)
        scalars = [
            jnp.broadcast_to(jnp.sum(jnp.where(lane == k, sums, 0.0), axis=1, keepdims=True), (8, LANE))
            for k in range(6)
        ]
        c0, c1 = weights(*scalars)
        dual[...] = (c0[0:1] * middle[...] + c1[0:1] * m1[...]) / obs_part[...]
        c0, c1 = (jnp.concatenate([c] * (GROUP // 8), axis=0) for c in (c0, c1))
        leaving = []
        for low, high in segments(total):

            def body(s):
                for f in range(3):
                    for t in range(2):
                        set_tile(multi, f, s, t, c0 * tile_of(last, f, s, t) + c1 * tile_of(d1, f, s, t))
                        set_tile(incr, f, s, t, c0 * tile_of(inc0, f, s, t) + c1 * tile_of(inc1, f, s, t))

            over_rows(low, high, body)
            leaving += copies.rows([(multi, 0, total)], low, high, multiplier.at[:, low:high, :])
            leaving += copies.rows([(incr, 0, total)], low, high, increment.at[:, low:high, :])
        wait(leaving)

    shape = (3, total, columns)
    return pl.pallas_call(
        kernel,
        in_specs=whole(8),
        out_specs=[ANY, ANY] + whole(1),
        out_shape=[f32(*shape)] * 2 + [f32(*middle.shape)],
        scratch_shapes=[vmem(*shape)] * 2 + [pltpu.SemaphoreType.DMA((2 * len(segments(total)),))],
        compiler_params=pltpu.CompilerParams(vmem_limit_bytes=40 * 1024 * 1024),
        cost_estimate=cost(18, 1),
        name="result",
    )(last, d1, inc0, inc1, received, middle, m1, obs_part)


def moved(block, axis, distance, wrap):
    size = lax.axis_size(axis)
    if wrap:
        route = [(i, (i + distance) % size) for i in range(size)]
    else:
        route = [(i, i + distance) for i in range(size) if 0 <= i + distance < size]
    return lax.ppermute(block, axis, route)


def after(value, other):
    return lax.optimization_barrier((value, other))


def part(array, at, count=None):
    return (array, at, array.shape[1] if count is None else count)


def shards(rhs_state, innovations, trajectory, model_var, obs_var, obs_index, control_rhs):
    total, columns = rhs_state.shape[2:]
    first, last, variance = rhs_state[0], control_rhs[0], model_var[0]
    traj = trajectory.reshape(-1, total, columns)
    where = obs_index[0]
    middle, obs_part = innovations[0].reshape(-1, LANE), obs_var[0].reshape(-1, LANE)

    later = moved(last, "tm", -1, False)
    ahead, inc0 = tangent_band(first, last, variance, traj)
    a1 = moved(ahead, "tm", 1, False)
    z0 = scatter(where, (middle / obs_part).reshape(-1), total)
    to_right, to_left = edges_call(inc0, last, variance, traj, z0)
    from_left = moved(to_right, "lon", 1, True)
    from_right = moved(to_left, "lon", -1, True)
    ahead_edges, traj_halo, var_halo, last_edges, z0_halo = tangent_seams(inc0, traj, from_left, from_right)
    later_edges = moved(last_edges, "tm", -1, False)
    a1_edges = moved(ahead_edges, "tm", 1, False)
    m1 = observe([part(inc0, 0)], total, where)
    m1, later_edges = after(m1, later_edges)
    d1 = adjoint_first(later, later_edges, traj, traj_halo, z0, z0_halo)

    d1_later = moved(d1, "tm", -1, False)
    ahead2, inc1, a1 = tangent_second(a1, a1_edges, d1, variance, traj, traj_halo, var_halo)
    a2 = moved(ahead2, "tm", 1, False)
    z1 = scatter(where, (m1 / obs_part).reshape(-1), total)
    m2 = observe([part(inc1, 0)], total, where)
    a1, d1 = part(a1, 0, total), part(d1, 0, total)
    early = row_products(
        ((0, 0), (1, 1), (0, 2), (1, 3), (2, 2), (3, 3)), ([part(first, 0)], [part(last, 0)], [a1], [d1]), 0, total
    )
    d_sums = [adjoint_second(d1_later, traj, traj_halo, z1, last, d1[0])]
    devices = lax.axis_size("tm") * lax.axis_size("lon")
    sent = row_products(
        ((0, 2), (1, 2), (2, 2)),
        ([part(first, 0)], [a1], [part(a2, 0)]),
        0,
        total,
        (devices, early, [], d_sums, (middle, m1, m2)),
    )
    received = lax.all_to_all(sent, ("tm", "lon"), 0, 0)
    multiplier, increment, dual = result(received, last, d1[0], inc0, inc1, middle, m1, obs_part)
    return (multiplier[None], dual.reshape(1, -1), increment[None])


def solution(mesh):
    in_specs = (
        P("tm", None, None, "lon"),
        P("tm", "lon"),
        P("tm", None, None, None, "lon"),
        P("tm", None, None, "lon"),
        P("tm", "lon"),
        P("tm", "lon"),
        P("tm", None, None, "lon"),
    )
    out_specs = (P("tm", None, None, "lon"), P("tm", "lon"), P("tm", None, None, "lon"))
    return jax.shard_map(shards, mesh=mesh, in_specs=in_specs, out_specs=out_specs, check_vma=False)
```

```python
import jax
import jax.numpy as jnp
from jax import lax
from jax.experimental import pallas as pl
from jax.experimental.pallas import tpu as pltpu
from jax.sharding import PartitionSpec as P

courant = 0.25
coriolis = 0.2
slope = 0.5 * courant

LANE = 128
BLOCK = 256
GROUP = 16
SHARE = 9
MARGIN = 8
HALO = 4
TRAJ, INC, VAR, LAST, PLANES = 0, 6, 9, 12, 16
MAIN = PLANES * HALO
F32 = jnp.float32
PARAMS = pltpu.CompilerParams(vmem_limit_bytes=56 * 1024 * 1024)


def iota(shape, dim):
    return lax.broadcasted_iota(jnp.int32, shape, dim)


def spread_shift(plane):
    return (LANE - (8 * plane + HALO)) % LANE


def pack_shift(plane):
    return (8 * plane + HALO) % LANE


def edges_of(planes, rows):
    lane = iota((rows, LANE), 1)
    packed = jnp.zeros((rows, LANE), F32)
    for number, plane in enumerate(planes):
        both = jnp.where(lane < LANE // 2, plane[:, :LANE], plane[:, LANE:])
        packed = jnp.where((lane >= 8 * number) & (lane < 8 * number + 8), pltpu.roll(both, pack_shift(number), 1), packed)
    return packed


def split_edges(turned, to_right, to_left, count):
    top = iota((8, turned.shape[1]), 0) < HALO
    for pair in range(count // 2):
        even = turned[16 * pair : 16 * pair + 8]
        odd = turned[16 * pair + 8 : 16 * pair + 16]
        to_right[8 * pair : 8 * pair + 8, :] = jnp.where(top, even, pltpu.roll(odd, HALO, 0))
        to_left[8 * pair : 8 * pair + 8, :] = jnp.where(top, pltpu.roll(even, HALO, 0), odd)


def joined_edges(from_left, from_right, count):
    top = iota((8, from_left.shape[1]), 0) < HALO
    pieces = []
    for pair in range(count // 2):
        left = from_left[8 * pair : 8 * pair + 8]
        right = from_right[8 * pair : 8 * pair + 8]
        pieces.append(jnp.where(top, left, pltpu.roll(right, HALO, 0)))
        pieces.append(jnp.where(top, pltpu.roll(left, HALO, 0), right))
    return jnp.concatenate(pieces, axis=0)


def padded_turn(message):
    rest = LANE - message.shape[0]
    if rest:
        message = jnp.concatenate([message, jnp.zeros((rest, message.shape[1]), F32)], axis=0)
    return message.T


def edges_kernel(increment, last, variance, traj, spread, to_right, to_left):
    rows = last.shape[1]
    planes = [traj[p].astype(F32) for p in range(6)]
    planes += [increment[f] for f in range(3)]
    planes += [variance[f] for f in range(3)]
    planes += [last[f] for f in range(3)]
    split_edges(edges_of(planes, rows).T, to_right.at[:MAIN], to_left.at[:MAIN], PLANES)
    spread_planes = [spread[f] for f in range(3)]
    split_edges(edges_of(spread_planes, rows).T, to_right.at[MAIN:], to_left.at[MAIN:], 4)


def edges_call(increment, last, variance, traj, spread):
    rows = last.shape[1]
    block = pl.BlockSpec((3, BLOCK, 2 * LANE), lambda i: (0, i, 0))
    sent = pl.BlockSpec((MAIN + 4 * HALO, BLOCK), lambda i: (0, i))
    return pl.pallas_call(
        edges_kernel,
        grid=(rows // BLOCK,),
        in_specs=[block, block, block, pl.BlockSpec((6, BLOCK, 2 * LANE), lambda i: (0, i, 0)), block],
        out_specs=[sent, sent],
        out_shape=[jax.ShapeDtypeStruct((MAIN + 4 * HALO, rows), F32)] * 2,
        compiler_params=PARAMS,
        cost_estimate=cost(16),
        name="edges",
    )(increment, last, variance, traj, spread)


def x_differences(tiles, first_lane, last_lane, joined):
    count = len(tiles)
    ahead = [pltpu.roll(t, LANE - 1, 1) for t in tiles]
    behind = [pltpu.roll(t, 1, 1) for t in tiles]
    if not joined:
        return [a - b for a, b in zip(ahead, behind)]
    return [
        jnp.where(last_lane, ahead[(t + 1) % count], ahead[t])
        - jnp.where(first_lane, behind[(t - 1) % count], behind[t])
        for t in range(count)
    ]


def rotation_at(start, total):
    position = (iota((GROUP, LANE), 0) + start).astype(F32)
    return coriolis * ((2.0 * position + 1.0) / total - 1.0)


def lane_ends():
    lane = iota((GROUP, LANE), 1)
    return lane == 0, lane == LANE - 1


def rows_at(start, offset=0):
    return pl.ds(pl.multiple_of(start + offset, GROUP), GROUP)


def traj_tiles(traj, traj_halo, step, start):
    out = []
    for plane in range(3 * step, 3 * step + 3):
        tiles = []
        if traj is not None:
            tiles += [traj[plane, rows_at(start), t * LANE : (t + 1) * LANE] for t in range(2)]
        if traj_halo is not None:
            at = [traj_halo.at[plane]] if len(traj_halo.shape) == 3 else [traj_halo.at[plane, t] for t in range(2)]
            tiles += [ref[rows_at(start), :] for ref in at]
        out.append([t.astype(F32) for t in tiles])
    return out


def load_rows(ref, start, offset):
    return [
        [ref[f, t, pl.ds(start + (MARGIN + offset), GROUP), :] for t in range(ref.shape[1])] for f in range(3)
    ]


def store_rows(ref, start, value):
    for f in range(3):
        for t in range(ref.shape[1]):
            ref[f, t, pl.ds(start + MARGIN, GROUP), :] = value[f][t]


def clear_margins(ref):
    rows = ref.shape[2]
    zero = jnp.zeros((MARGIN, LANE), F32)
    for f in range(3):
        for t in range(ref.shape[1]):
            ref[f, t, 0:MARGIN, :] = zero
            ref[f, t, rows - MARGIN : rows, :] = zero


def tangent_rows(source, traj, traj_halo, step, start, base, total, joined=True):
    here, above, below = (load_rows(source, start, k) for k in (0, 1, -1))
    trajectory = traj_tiles(traj, traj_halo, step, start)
    turn = rotation_at(start + base, total)
    ends = lane_ends()
    dx = [x_differences(here[f], *ends, joined) for f in range(3)]
    new = [[], [], []]
    for t in range(source.shape[1]):
        b, e, n = (trajectory[f][t] for f in range(3))
        h, u, v = (here[f][t] for f in range(3))
        xh, xu, xv = (dx[f][t] for f in range(3))
        yh, yu, yv = (above[f][t] - below[f][t] for f in range(3))
        new[0].append(h - slope * (b * (xu + yv) + e * xh + n * yh))
        new[1].append(u - slope * (xh + e * xu + n * yu) + turn * v)
        new[2].append(v - slope * (yh + e * xv + n * yv) - turn * u)
    return new


def north_rows(field, trajectory):
    out = [[], [], []]
    for t in range(3):
        b, _, n = (trajectory[f][t] for f in range(3))
        p, q, w = (field[f][t] for f in range(3))
        out[0].append(n * p + w)
        out[1].append(n * q)
        out[2].append(b * p + n * w)
    return out


def adjoint_rows(source, flux, traj, traj_halo, step, start, base, total):
    here = load_rows(source, start, 0)
    above, below = (load_rows(flux, start, k) for k in (1, -1))
    trajectory = traj_tiles(traj, traj_halo, step, start)
    turn = rotation_at(start + base, total)
    ends = lane_ends()
    east = [[], [], []]
    for t in range(3):
        b, e, _ = (trajectory[f][t] for f in range(3))
        p, q, w = (here[f][t] for f in range(3))
        east[0].append(e * p + q)
        east[1].append(b * p + e * q)
        east[2].append(e * w)
    dx = [x_differences(east[f], *ends, True) for f in range(3)]
    new = [[], [], []]
    for t in range(3):
        p, q, w = (here[f][t] for f in range(3))
        change = [slope * (dx[f][t] + (above[f][t] - below[f][t])) for f in range(3)]
        new[0].append(p + change[0])
        new[1].append(q + change[1] - turn * w)
        new[2].append(w + change[2] + turn * q)
    return new


def over_rows(begin, end, body):
    count = (end - begin) // GROUP
    unroll = next(u for u in (8, 6, 5, 4, 3, 2, 1) if count % u == 0)

    def step(i, carry):
        body(pl.multiple_of(begin + i * GROUP, GROUP))
        return carry

    lax.fori_loop(0, count, step, 0, unroll=unroll)


def padded(rows):
    return -(-rows // (2 * LANE)) * 2 * LANE


def extra(rows):
    return 8 * padded(rows) // (2 * LANE)


def turn_in(message, packed_ref):
    for j in range(message.shape[1] // LANE):
        packed_ref[j * LANE : (j + 1) * LANE, :] = padded_turn(message[:, j * LANE : (j + 1) * LANE])


def unfold_in(folded, packed_ref):
    for j in range(packed_ref.shape[0] // LANE):
        at = (slice(j // 2 * 8, j // 2 * 8 + 8), slice(j % 2 * LANE, (j % 2 + 1) * LANE))
        message = jnp.concatenate([folded[(f,) + at] for f in range(folded.shape[0])], axis=0)
        packed_ref[j * LANE : (j + 1) * LANE, :] = padded_turn(message)


def turn_out(halo, payload, behind):
    low = iota((8, LANE), 0) < HALO
    for j in range(halo.shape[1] // LANE):
        for f in range(halo.shape[0]):
            turned = halo[f, j * LANE : (j + 1) * LANE, :].T
            ends = jnp.where(low, turned[:8], turned[LANE - 8 :])
            row = behind + j // 2 * 8
            payload[f, row : row + 8, j % 2 * LANE : (j % 2 + 1) * LANE] = pltpu.roll(ends, HALO, 0)


def wide_scratch(rows, tiles=3):
    return pltpu.VMEM((3, tiles, rows + 2 * MARGIN, LANE), F32)


def tile_of(ref, f, start, t, offset=0):
    return ref[f, rows_at(start, offset), t * LANE : (t + 1) * LANE]


def set_tile(ref, f, start, t, value, offset=0):
    ref[f, rows_at(start, offset), t * LANE : (t + 1) * LANE] = value


class Copies:
    def __init__(self, sems):
        self.sems, self.used = sems, 0

    def rows(self, parts, begin, end, target):
        started = []
        for ref, at, count in parts:
            low, high = max(begin, at), min(end, at + count)
            if low < high:
                source = ref.at[..., low - at : high - at, :]
                goal = target.at[..., low - begin : high - begin, :]
                copy = pltpu.make_async_copy(source, goal, self.sems.at[self.used])
                self.used += 1
                copy.start()
                started.append(copy)
        return started


def placed(refs, parts):
    return [(ref, at, count) for ref, (_, at, count) in zip(refs, parts)]


def wait(copies):
    for copy in copies:
        copy.wait()


def segments(total):
    return [(at, min(at + BLOCK, total)) for at in range(0, total, BLOCK)]


def fetch(copies, begin, end, *pairs):
    return [
        [
            copy
            for parts, target in pairs
            for copy in copies.rows(parts, begin + low, begin + high, target.at[..., low:high, :])
        ]
        for low, high in segments(end - begin)
    ]


def leave(copies, source, begin, low, high, parts):
    started = []
    for target, at, count in parts:
        first, last = max(low, at), min(high, at + count)
        if first < last:
            started += copies.rows([(source, begin, source.shape[1])], first, last, target.at[:, first - at : last - at, :])
    return started


def run_tangent(span, total, get, ready, traj, traj_halo, wide_a, wide_b, traj_ready, put, done, joined=True):
    base, end, out_begin, out_end = span
    held = segments(end - base)
    clear_margins(wide_a)
    clear_margins(wide_b)
    for (low, high), copies in zip(held, ready):
        wait(copies)
        over_rows(low, high, lambda s: store_rows(wide_a, s, get(s)))
    for (low, high), copies in zip(held, traj_ready):
        wait(copies)
        over_rows(
            low, high, lambda s: store_rows(wide_b, s, tangent_rows(wide_a, traj, traj_halo, 0, s, base, total, joined))
        )
    for low, high in segments(out_end - out_begin):
        skip = out_begin - base
        over_rows(
            low + skip,
            high + skip,
            lambda s: put(s, tangent_rows(wide_b, traj, traj_halo, 1, s, base, total, joined)),
        )
        done(out_begin + low, out_begin + high)


def run_adjoint(span, total, get, ready, traj, traj_halo, wide_a, wide_b, flux_a, flux_b, put, begin_put, done):
    base, end, out_begin, out_end = span
    clear_margins(flux_a)
    clear_margins(flux_b)

    def begin(s):
        field = get(s)
        store_rows(wide_a, s, field)
        store_rows(flux_a, s, north_rows(field, traj_tiles(traj, traj_halo, 1, s)))

    def middle(s):
        field = adjoint_rows(wide_a, flux_a, traj, traj_halo, 1, s, base, total)
        store_rows(wide_b, s, field)
        store_rows(flux_b, s, north_rows(field, traj_tiles(traj, traj_halo, 0, s)))

    for (low, high), copies in zip(segments(end - base), ready):
        wait(copies)
        over_rows(low, high, begin)
    over_rows(0, end - base, middle)
    for (low, high), copies in zip(segments(out_end - out_begin), begin_put):
        wait(copies)
        skip = out_begin - base
        over_rows(
            low + skip, high + skip, lambda s: put(s, adjoint_rows(wide_b, flux_b, traj, traj_halo, 0, s, base, total))
        )
        done(out_begin + low, out_begin + high)


def halo_of(lanes, plane):
    return pltpu.roll(lanes, spread_shift(plane), 1)


ANY = pl.BlockSpec(memory_space=pltpu.HBM)


def whole(count):
    return [pl.BlockSpec(memory_space=pltpu.VMEM)] * count


def cost(mib, steps=2):
    return pl.CostEstimate(flops=2**10, bytes_accessed=mib * 2**20, transcendentals=0)


def f32(*shape):
    return jax.ShapeDtypeStruct(shape, F32)


def vmem(*shape, dtype=F32):
    return pltpu.VMEM(shape, dtype)


def call(name, kernel, ins, outs, scratch, mib, *args, first_any=False, outs_any=False):
    specs = [ANY if outs_any or (first_any and k == 0) else whole(1)[0] for k in range(len(outs))]
    return pl.pallas_call(
        kernel,
        in_specs=ins,
        out_specs=specs,
        out_shape=outs,
        scratch_shapes=scratch,
        compiler_params=PARAMS,
        cost_estimate=cost(mib),
        name=name,
    )(*args)


def tangent_band(first, last, variance, traj, cuts):
    _, total, columns = first.shape

    def kernel(first_in, last_in, variance_in, traj_in, *refs):
        aheads, refs = refs[: len(cuts)], refs[len(cuts) :]
        increment, first, last, variance, traj, wide_a, wide_b, out, sems = refs
        aheads = [(ref, low, high - low) for ref, (low, high) in zip(aheads, cuts)]
        copies = Copies(sems)
        ready = fetch(copies, 0, total, *[([(r, 0, total)], to) for r, to in ((first_in, first), (last_in, last), (variance_in, variance))])
        traj_ready = fetch(copies, 0, total, ([(traj_in, 0, total)], traj))

        def get(s):
            tiles = [
                [tile_of(first, f, s, t) - tile_of(variance, f, s, t) * tile_of(last, f, s, t) for t in range(2)]
                for f in range(3)
            ]
            for f in range(3):
                for t in range(2):
                    set_tile(first, f, s, t, tiles[f][t])
            return tiles

        def put(s, new):
            for f in range(3):
                for t in range(2):
                    set_tile(out, f, s, t, -new[f][t])

        leaving = []

        def done(low, high):
            leaving.extend(leave(copies, out, 0, low, high, aheads))
            leaving.extend(leave(copies, first, 0, low, high, [(increment, 0, total)]))

        run_tangent((0, total, 0, total), total, get, ready, traj, None, wide_a, wide_b, traj_ready, put, done)
        wait(leaving)

    outs = [f32(3, high - low, columns) for low, high in cuts] + [f32(*first.shape)]
    scratch = [vmem(*first.shape)] * 3 + [vmem(*traj.shape, dtype=traj.dtype)] + [wide_scratch(total, 2)] * 2
    scratch += [vmem(*first.shape), pltpu.SemaphoreType.DMA((7 * len(segments(total)),))]
    return call("tangent_band", kernel, [ANY] * 4, outs, scratch, 18, first, last, variance, traj, outs_any=True)


def tangent_seams(increment, traj, from_left, from_right):
    _, total, columns = increment.shape

    def kernel(inc_in, traj_in, from_left, from_right, edges, traj_halo, var_halo, last_edges, spread_halo, inc, traj, wide_a, wide_b, seams, inc_halo, out, sems):
        copies = Copies(sems)
        inc_ready = fetch(copies, 0, total, ([(inc_in, 0, total)], inc))
        traj_ready = fetch(copies, 0, total, ([(traj_in, 0, total)], traj))
        left_part = iota((LANE, LANE), 1) < LANE // 2
        for j in range(total // LANE):
            cut = slice(j * LANE, (j + 1) * LANE)
            joined = joined_edges(from_left[:MAIN, cut], from_right[:MAIN, cut], PLANES)
            last_edges[:, cut] = joined[8 * LAST : 8 * LAST + 24]
            packed = joined.T
            spread = padded_turn(joined_edges(from_left[MAIN:, cut], from_right[MAIN:, cut], 4))
            for plane in range(6):
                traj_halo[plane, cut, :] = halo_of(packed, TRAJ + plane).astype(traj_halo.dtype)
            for f in range(3):
                var_halo[f, cut, :] = halo_of(packed, VAR + f)
                inc_halo[f, cut, :] = halo_of(packed, INC + f)
                spread_halo[f, cut, :] = halo_of(spread, f)
        for copies_of in inc_ready + traj_ready:
            wait(copies_of)
        for j in range(total // LANE):
            cut = slice(j * LANE, (j + 1) * LANE)
            for plane in range(6):
                halo = traj_halo[plane, cut, :].astype(F32)
                own = [traj[plane, cut, t * LANE : (t + 1) * LANE].astype(F32) for t in range(2)]
                seams[plane, 0, cut, :] = jnp.where(left_part, own[0], halo).astype(seams.dtype)
                seams[plane, 1, cut, :] = jnp.where(left_part, halo, own[1]).astype(seams.dtype)

        def get(s):
            left = iota((GROUP, LANE), 1) < LANE // 2
            tiles = []
            for f in range(3):
                halo = inc_halo[f, rows_at(s), :]
                tiles.append([jnp.where(left, tile_of(inc, f, s, 0), halo), jnp.where(left, halo, tile_of(inc, f, s, 1))])
            return tiles

        def put(s, new):
            for f in range(3):
                for t in range(2):
                    out[2 * f + t, rows_at(s), :] = -new[f][t]

        nothing = [[] for _ in segments(total)]
        run_tangent((0, total, 0, total), total, get, nothing, None, seams, wide_a, wide_b, nothing, put, lambda low, high: None, False)
        turn_out(out, edges, 0)

    outs = [f32(6, extra(total), columns), jax.ShapeDtypeStruct((6, total, LANE), traj.dtype)]
    outs += [f32(3, total, LANE), f32(24, total), f32(3, total, LANE)]
    scratch = [vmem(*increment.shape), vmem(*traj.shape, dtype=traj.dtype)] + [wide_scratch(total, 2)] * 2
    scratch += [vmem(6, 2, total, LANE, dtype=traj.dtype), vmem(3, total, LANE), vmem(6, total, LANE)]
    scratch += [pltpu.SemaphoreType.DMA((2 * len(segments(total)),))]
    return call("tangent_seams", kernel, [ANY, ANY] + whole(2), outs, scratch, 10, increment, traj, from_left, from_right)


def whole_of(total, *pairs):
    return [([(ref, 0, total)], target) for ref, target in pairs]


def adjoint_first(span, later, later_edges, traj, traj_halo, spread, spread_halo):
    base, end, out_begin, out_end = span
    held, rows = end - base, out_end - out_begin
    total, columns = spread.shape[1:]
    count = len(later)

    def kernel(*refs):
        later_in, refs = placed(refs[:count], later), refs[count:]
        traj_in, traj_halo_in, spread_in, spread_halo_in, later_edges, pulled = refs[:6]
        field, traj, traj_halo, spread, wide_a, wide_b, flux_a, flux_b, own, halo, out, sems = refs[6:]
        copies = Copies(sems)
        ready = fetch(copies, base, end, (later_in, field), *whole_of(total, (traj_in, traj), (traj_halo_in, traj_halo)))
        begin_put = fetch(copies, out_begin, out_end, *whole_of(total, (spread_in, spread), (spread_halo_in, halo)))
        turn_in(later_edges, own)
        if rows < halo.shape[1]:
            halo[:, rows:, :] = jnp.zeros((3, halo.shape[1] - rows, LANE), F32)
        skip = base - out_begin

        def get(s):
            lanes = own[rows_at(s, base), :]
            return [[tile_of(field, f, s, t) for t in range(2)] + [halo_of(lanes, f)] for f in range(3)]

        def put(s, new):
            for f in range(3):
                for t in range(2):
                    set_tile(out, f, s, t, tile_of(spread, f, s, t, skip) - new[f][t], skip)
                halo[f, rows_at(s, skip), :] = halo[f, rows_at(s, skip), :] - new[f][2]

        leaving = []

        def done(low, high):
            leaving.extend(leave(copies, out, out_begin, low, high, [(pulled, out_begin, rows)]))

        run_adjoint(span, total, get, ready, traj, traj_halo, wide_a, wide_b, flux_a, flux_b, put, begin_put, done)
        turn_out(halo, out, rows)
        after_rows = rows + extra(rows)
        leaving.extend(copies.rows([(out, 0, after_rows)], rows, after_rows, pulled.at[:, rows:after_rows, :]))
        wait(leaving)

    outs = [f32(3, rows + extra(rows), columns)]
    scratch = [vmem(3, held, columns), vmem(6, held, columns, dtype=traj.dtype), vmem(6, held, LANE, dtype=traj.dtype)]
    scratch += [vmem(3, rows, columns)] + [wide_scratch(held)] * 4 + [vmem(total, LANE)]
    scratch += [vmem(3, padded(rows), LANE), vmem(3, rows + extra(rows), columns)]
    scratch += [pltpu.SemaphoreType.DMA(((6 + count) * len(segments(held)) + 1,))]
    return call(
        "adjoint_first", kernel, [ANY] * (count + 4) + whole(1), outs, scratch, 10,
        *[p[0] for p in later], traj, traj_halo, spread, spread_halo, later_edges, first_any=True,
    )[0]


def unfold_parts(copies, parts, folds):
    started = []
    for (ref, _, count), fold in zip(parts, folds):
        started += copies.rows([(ref, 0, count + extra(count))], count, count + extra(count), fold)
    return started


def unfold_all(parts, folds, packed_ref):
    for (_, at, count), fold in zip(parts, folds):
        unfold_in(fold, packed_ref.at[at : at + padded(count), :])


def tangent_second(span, earlier, earlier_edges, pulled, variance, traj, traj_halo, var_halo, new_begin):
    base, end, out_begin, out_end = span
    held, rows = end - base, out_end - out_begin
    _, total, columns = variance.shape
    n_earlier, n_pulled = len(earlier), len(pulled)

    def kernel(*refs):
        earlier_in, refs = placed(refs[:n_earlier], earlier), refs[n_earlier:]
        pulled_in, refs = placed(refs[:n_pulled], pulled), refs[n_pulled:]
        edges_in, variance_in, traj_in, traj_halo_in, var_halo_in, ahead, increment, patched = refs[:8]
        earl, pull, variance, traj, traj_halo, var_halo, wide_a, wide_b, e_own, p_own, e_fold = refs[8:19]
        p_folds, (inc, out, sems) = refs[19 : 19 + n_pulled], refs[19 + n_pulled :]
        copies = Copies(sems)
        edge_copies = copies.rows([(edges_in, 0, extra(total))], 0, extra(total), e_fold)
        edge_copies += unfold_parts(copies, pulled_in, p_folds)
        ready = fetch(
            copies, base, end, (earlier_in, earl), (pulled_in, pull), *whole_of(total, (variance_in, variance), (var_halo_in, var_halo))
        )
        traj_ready = fetch(copies, base, end, *whole_of(total, (traj_in, traj), (traj_halo_in, traj_halo)))
        wait(edge_copies)
        unfold_in(e_fold, e_own)
        unfold_all(pulled_in, p_folds, p_own)
        skip = base - out_begin

        def get(s):
            e_lanes, p_lanes = e_own[rows_at(s, base), :], p_own[rows_at(s, base), :]
            lane = iota((GROUP, LANE), 1)
            tiles = []
            for f in range(3):
                left, right = halo_of(e_lanes, 2 * f), halo_of(e_lanes, 2 * f + 1)
                fixed = [
                    jnp.where(lane < 2, left, tile_of(earl, f, s, 0)),
                    jnp.where(lane >= LANE - 2, right, tile_of(earl, f, s, 1)),
                ]
                own = [fixed[t] - tile_of(variance, f, s, t) * tile_of(pull, f, s, t) for t in range(2)]
                for t in range(2):
                    set_tile(earl, f, s, t, fixed[t])
                    set_tile(inc, f, s, t, own[t])
                beside = jnp.where(lane < LANE // 2, right, left)
                tiles.append(own + [beside - var_halo[f, rows_at(s), :] * halo_of(p_lanes, f)])
            return tiles

        def put(s, new):
            for f in range(3):
                for t in range(2):
                    set_tile(out, f, s, t, -new[f][t], skip)

        leaving = []

        def done(low, high):
            leaving.extend(leave(copies, out, out_begin, low, high, [(ahead, out_begin, rows)]))
            if low == out_begin:
                leaving.extend(leave(copies, inc, base, new_begin, end, [(increment, new_begin, end - new_begin)]))
                leaving.extend(leave(copies, earl, base, new_begin, end, [(patched, new_begin, end - new_begin)]))

        run_tangent(span, total, get, ready, traj, traj_halo, wide_a, wide_b, traj_ready, put, done)
        wait(leaving)

    outs = [f32(3, rows, columns)] + [f32(3, end - new_begin, columns)] * 2
    scratch = [vmem(3, held, columns)] * 3 + [vmem(6, held, columns, dtype=traj.dtype), vmem(6, held, LANE, dtype=traj.dtype)]
    scratch += [vmem(3, held, LANE)] + [wide_scratch(held)] * 2 + [vmem(total, LANE), vmem(total + 2 * LANE, LANE)]
    scratch += [vmem(6, extra(total), columns)] + [vmem(3, extra(p[2]), columns) for p in pulled]
    scratch += [vmem(3, held, columns), vmem(3, rows, columns)]
    scratch += [pltpu.SemaphoreType.DMA(((6 + n_earlier + n_pulled) * len(segments(held)) + 4 + n_pulled,))]
    return call(
        "tangent_second", kernel, [ANY] * (n_earlier + n_pulled + 5), outs, scratch, 16,
        *[p[0] for p in earlier], *[p[0] for p in pulled], earlier_edges, variance, traj, traj_halo, var_halo, outs_any=True,
    )


def adjoint_second(later, traj, traj_halo, spread, last, pulled):
    _, total, columns = last.shape
    n_later, n_pulled = len(later), len(pulled)

    def kernel(*refs):
        later_in, refs = placed(refs[:n_later], later), refs[n_later:]
        pulled_in, refs = placed(refs[:n_pulled], pulled), refs[n_pulled:]
        traj_in, traj_halo_in, spread_in, last_in, sums, field, traj, traj_halo, spread, last, pull = refs[:11]
        wide_a, wide_b, flux_a, flux_b, own = refs[11:16]
        folds, sems = refs[16:-1], refs[-1]
        copies = Copies(sems)
        edge_copies = unfold_parts(copies, later_in, folds)
        ready = fetch(copies, 0, total, (later_in, field), *whole_of(total, (traj_in, traj), (traj_halo_in, traj_halo)))
        begin_put = fetch(copies, 0, total, (pulled_in, pull), *whole_of(total, (spread_in, spread), (last_in, last)))
        wait(edge_copies)
        unfold_all(later_in, folds, own)
        sums[...] = jnp.zeros_like(sums)

        def get(s):
            lanes = own[rows_at(s), :]
            return [[tile_of(field, f, s, t) for t in range(2)] + [halo_of(lanes, f)] for f in range(3)]

        def put(s, new):
            parts = [jnp.zeros((GROUP, LANE), F32)] * 3
            for f in range(3):
                for t in range(2):
                    value = tile_of(spread, f, s, t) - new[f][t]
                    for k, other in enumerate((tile_of(last, f, s, t), tile_of(pull, f, s, t), value)):
                        parts[k] = parts[k] + other * value
            for k in range(3):
                sums[k] = sums[k] + parts[k]

        span = (0, total, 0, total)
        run_adjoint(
            span, total, get, ready, traj, traj_halo, wide_a, wide_b, flux_a, flux_b, put, begin_put, lambda low, high: None
        )

    scratch = [vmem(3, total, columns), vmem(6, total, columns, dtype=traj.dtype), vmem(6, total, LANE, dtype=traj.dtype)]
    scratch += [vmem(3, total, columns)] * 3 + [wide_scratch(total)] * 4 + [vmem(total + 2 * LANE, LANE)]
    scratch += [vmem(3, extra(p[2]), columns) for p in later]
    scratch += [pltpu.SemaphoreType.DMA(((4 + n_later + n_pulled) * len(segments(total)) + n_later,))]
    outs = [f32(3, GROUP, LANE)]
    return call(
        "adjoint_second", kernel, [ANY] * (n_later + n_pulled + 4), outs, scratch, 16,
        *[p[0] for p in later], *[p[0] for p in pulled], traj, traj_halo, spread, last,
    )[0]


def observe(parts, total, where):
    count = where.shape[0]

    def kernel(*refs):
        parts_in, (where_smem, column, out, field, picked, sems) = refs[: len(parts)], refs[len(parts) :]
        copies = Copies(sems)
        started = []
        for f in range(3):
            source = [(ref.at[f], at, rows) for ref, at, rows in placed(parts_in, parts)]
            started += copies.rows(source, 0, total, field.at[f * total : (f + 1) * total])
        wait(started)

        def step(i, carry):
            row = lax.shift_right_logical(where_smem[i], 8)
            picked[pl.ds(i, 1), :] = field[pl.ds(row, 1), :]
            return carry

        lax.fori_loop(0, count, step, 0, unroll=16)
        lane = iota((LANE, LANE), 1).astype(F32)
        for j in range(count // LANE):
            cut = slice(j * LANE, (j + 1) * LANE)
            at = jnp.broadcast_to(column[j : j + 1, :], (LANE, LANE)).T
            kept = jnp.where(lane == at, picked[cut, :LANE], 0.0)
            kept = kept + jnp.where(lane + float(LANE) == at, picked[cut, LANE:], 0.0)
            out[j : j + 1, :] = jnp.sum(kept.T, axis=0, keepdims=True)

    columns = 2 * LANE
    column = (where % columns).astype(F32).reshape(-1, LANE)
    return pl.pallas_call(
        kernel,
        in_specs=[ANY] * len(parts) + [pl.BlockSpec(memory_space=pltpu.SMEM)] + whole(1),
        out_specs=whole(1)[0],
        out_shape=f32(count // LANE, LANE),
        scratch_shapes=[vmem(3 * total, columns), vmem(count, columns), pltpu.SemaphoreType.DMA((3 * len(parts),))],
        compiler_params=PARAMS,
        cost_estimate=cost(3),
        name="observe",
    )(*[part[0] for part in parts], where, column)


def scatter(where, values, total):
    count = where.shape[0]

    def kernel(where_smem, values_smem, field):
        field[...] = jnp.zeros_like(field)
        lane = iota((1, 2 * LANE), 1)

        def step(i, carry):
            index = where_smem[i]
            at = (pl.ds(lax.shift_right_logical(index, 8), 1), slice(None))
            field[at] = field[at] + jnp.where(lane == (index & (2 * LANE - 1)), values_smem[i], 0.0)
            return carry

        lax.fori_loop(0, count, step, 0, unroll=8)

    return pl.pallas_call(
        kernel,
        in_specs=[pl.BlockSpec(memory_space=pltpu.SMEM)] * 2,
        out_specs=whole(1)[0],
        out_shape=f32(3 * total, 2 * LANE),
        compiler_params=PARAMS,
        cost_estimate=cost(3),
        name="scatter",
    )(where, values).reshape(3, total, 2 * LANE)


def one_sum(value):
    return jnp.sum(jnp.sum(value, axis=1, keepdims=True), axis=0, keepdims=True)


def pieces(cuts):
    return [(at, min(at + BLOCK, high)) for low, high in cuts for at in range(low, high, BLOCK)]


def summed(values):
    total = values[0]
    for value in values[1:]:
        total = total + value
    return total


def row_products(pairs, arrays, low, high, finish=None):
    columns = arrays[0][0][0].shape[2]
    counts = [len(parts) for parts in arrays]
    cuts = pieces([(low, high)])
    if finish:
        devices, early, a_before, d_parts, obs = finish
        scalars = [early] + a_before + d_parts + list(obs)
        out = f32(devices, 8, LANE)
    else:
        scalars = []
        out = f32(len(pairs), GROUP, columns)

    def kernel(*refs):
        refs = list(refs)
        inputs = []
        for parts in arrays:
            inputs.append([(refs.pop(0), at, count) for _, at, count in parts])
        extras, refs = refs[: len(scalars)], refs[len(scalars) :]
        out_ref, held, sems = refs[0], refs[1:-1], refs[-1]
        copies = Copies(sems)
        started = []
        for begin, end in cuts:
            group = []
            for parts, scratch in zip(inputs, held):
                group += copies.rows(parts, begin, end, scratch.at[:, begin - low : end - low, :])
            started.append(group)
        sums = tuple(jnp.zeros((GROUP, columns), F32) for _ in pairs)
        for (begin, end), group in zip(cuts, started):
            wait(group)

            def step(i, carry, begin=begin):
                at = pl.ds(pl.multiple_of(begin - low + i * GROUP, GROUP), GROUP)
                parts = list(carry)
                for f in range(3):
                    tiles = [a[f, at, :] for a in held]
                    for k, (one, two) in enumerate(pairs):
                        parts[k] = parts[k] + tiles[one] * tiles[two]
                return tuple(parts)

            sums = lax.fori_loop(0, (end - begin) // GROUP, step, sums)
        if not finish:
            for k, value in enumerate(sums):
                out_ref[k] = value
            return
        early_ref, extras = extras[0], extras[1:]
        before, d_refs, (o0, o1, o2) = extras[: len(a_before)], extras[len(a_before) : -3], (e[...] for e in extras[-3:])
        tail = [
            summed([one_sum(summed([sums[k]] + [r[k] for r in before]))] + [one_sum(summed([r[k] for r in d_refs]))])
            for k in range(3)
        ]
        head = [one_sum(early_ref[2 * k] + early_ref[2 * k + 1]) for k in range(3)]
        values = (
            head[0] + one_sum(o0 * o0),
            head[1] + one_sum(o0 * o1),
            tail[0] + one_sum(o0 * o2),
            head[2] + one_sum(o1 * o1),
            tail[1] + one_sum(o1 * o2),
            tail[2] + one_sum(o2 * o2),
        )
        lane = iota((8, LANE), 1)
        row = jnp.zeros((8, LANE), F32)
        for k, value in enumerate(values):
            row = jnp.where(lane == k, value, row)
        for k in range(devices):
            out_ref[k] = row

    return pl.pallas_call(
        kernel,
        in_specs=[ANY] * sum(counts) + whole(len(scalars)),
        out_specs=whole(1)[0],
        out_shape=out,
        scratch_shapes=[vmem(3, high - low, columns) for _ in arrays]
        + [pltpu.SemaphoreType.DMA((len(cuts) * (sum(counts)),))],
        compiler_params=pltpu.CompilerParams(vmem_limit_bytes=20 * 1024 * 1024),
        cost_estimate=cost(9, 1),
        name="last_products" if finish else "products",
    )(*[part[0] for parts in arrays for part in parts], *scalars)


def weights(s00, s01, s02, s11, s12, s22):
    alpha = s01 / s00
    t11 = s11 - alpha * s01
    along = (s12 - alpha * s02) / t11
    beta = jnp.sqrt(s00)
    gamma = 1.0 / jnp.sqrt(t11)
    h00 = 1.0 + alpha
    h10_square = t11 / s00
    h10 = jnp.sqrt(h10_square)
    h01 = (s02 - alpha * s01) * gamma / beta
    h11 = 1.0 - alpha + along
    h21_square = (s22 - s02 * (s02 / s00) - along * (s12 - alpha * s02)) / t11
    g00 = h00 * h00 + h10_square
    g01 = h00 * h01 + h10 * h11
    g11 = h01 * h01 + h11 * h11 + h21_square
    q0 = beta * h00
    q1 = beta * h01
    det = g00 * g11 - g01 * g01
    y0 = (g11 * q0 - g01 * q1) / det
    y1 = (g00 * q1 - g01 * q0) / det
    c1 = y1 * gamma
    return (y0 / beta - c1 * alpha, c1)


def result(received, last, d1, inc0, inc1, middle, m1, obs_part):
    _, total, columns = last.shape
    n_d1, n_inc1 = len(d1), len(inc1)

    def kernel(last, inc0, *refs):
        d1_in, refs = placed(refs[:n_d1], d1), refs[n_d1:]
        inc1_in, refs = placed(refs[:n_inc1], inc1), refs[n_inc1:]
        received, middle, m1, obs_part, multiplier, increment, dual, multi, incr, sems = refs
        copies = Copies(sems)
        sums = jnp.sum(received[...], axis=0)
        lane = iota((8, LANE), 1)
        scalars = [
            jnp.broadcast_to(jnp.sum(jnp.where(lane == k, sums, 0.0), axis=1, keepdims=True), (8, LANE))
            for k in range(6)
        ]
        c0, c1 = weights(*scalars)
        dual[...] = (c0[0:1] * middle[...] + c1[0:1] * m1[...]) / obs_part[...]
        c0, c1 = (jnp.concatenate([c] * (GROUP // 8), axis=0) for c in (c0, c1))
        leaving = []
        for out, whole_in, parts, target in ((multi, last, d1_in, multiplier), (incr, inc0, inc1_in, increment)):
            for ref, at, count in parts:
                for low, high in segments(count):

                    def body(s, out=out, whole_in=whole_in, ref=ref, at=at):
                        for f in range(3):
                            for t in range(2):
                                value = c0 * tile_of(whole_in, f, s, t, at) + c1 * tile_of(ref, f, s, t)
                                set_tile(out, f, s, t, value, at)

                    over_rows(low, high, body)
                    leaving += leave(copies, out, 0, at + low, at + high, [(target, 0, total)])
        wait(leaving)

    shape = (3, total, columns)
    return pl.pallas_call(
        kernel,
        in_specs=whole(6 + n_d1 + n_inc1),
        out_specs=[ANY, ANY] + whole(1),
        out_shape=[f32(*shape)] * 2 + [f32(*middle.shape)],
        scratch_shapes=[vmem(*shape)] * 2 + [pltpu.SemaphoreType.DMA((4 * len(segments(total)) + 4,))],
        compiler_params=pltpu.CompilerParams(vmem_limit_bytes=40 * 1024 * 1024),
        cost_estimate=cost(18, 1),
        name="result",
    )(last, inc0, *[p[0] for p in d1], *[p[0] for p in inc1], received, middle, m1, obs_part)


def moved(block, axis, distance, wrap):
    size = lax.axis_size(axis)
    if wrap:
        route = [(i, (i + distance) % size) for i in range(size)]
    else:
        route = [(i, i + distance) for i in range(size) if 0 <= i + distance < size]
    return lax.ppermute(block, axis, route)


def after(value, other):
    return lax.optimization_barrier((value, other))


def part(array, at, count=None):
    return (array, at, array.shape[1] if count is None else count)


def shards(rhs_state, innovations, trajectory, model_var, obs_var, obs_index, control_rhs):
    total, columns = rhs_state.shape[2:]
    first, last, variance = rhs_state[0], control_rhs[0], model_var[0]
    traj = trajectory.reshape(-1, total, columns)
    where = obs_index[0]
    middle, obs_part = innovations[0].reshape(-1, LANE), obs_var[0].reshape(-1, LANE)

    step = GROUP
    cut = total * SHARE // 16 // GROUP * GROUP
    one, two = cut - step, cut - 2 * step

    later = [part(moved(last, "tm", -1, False), 0)]
    ahead, inc0 = tangent_band(first, last, variance, traj, [(0, total)])
    a1 = [part(moved(ahead, "tm", 1, False), 0)]
    z0 = scatter(where, (middle / obs_part).reshape(-1), total)
    to_right, to_left = edges_call(inc0, last, variance, traj, z0)
    from_left = moved(to_right, "lon", 1, True)
    from_right = moved(to_left, "lon", -1, True)
    ahead_edges, traj_halo, var_halo, last_edges, z0_halo = tangent_seams(inc0, traj, from_left, from_right)
    later_edges = moved(last_edges, "tm", -1, False)
    a1_edges = moved(ahead_edges, "tm", 1, False)
    m1 = observe([part(inc0, 0)], total, where)
    m1, later_edges = after(m1, later_edges)

    d1, d1_later, a2, inc1, fixed = [], [], [], [], []
    spans = [(0, cut, 0, one), (one - step, total, one, total)]
    seconds = [(0, one, 0, two), (two - step, total, two, total)]
    for c, (span, second) in enumerate(zip(spans, seconds)):
        pulled = adjoint_first(span, later, later_edges, traj, traj_halo, z0, z0_halo)
        d1.append(part(pulled, span[2], span[3] - span[2]))
        d1_later.append(part(moved(pulled, "tm", -1, False), *d1[-1][1:]))
        ahead, increment, patched = tangent_second(
            second, a1, a1_edges, d1, variance, traj, traj_halo, var_halo, span[2]
        )
        a2.append(part(moved(ahead, "tm", 1, False), second[2]))
        inc1.append(part(increment, span[2]))
        fixed.append(part(patched, span[2]))
    a1 = fixed
    z1 = scatter(where, (m1 / obs_part).reshape(-1), total)
    m2 = observe(inc1, total, where)
    early = row_products(
        ((0, 0), (1, 1), (0, 2), (1, 3), (2, 2), (3, 3)), ([part(first, 0)], [part(last, 0)], a1, d1), 0, total
    )
    d_sums = [adjoint_second(d1_later, traj, traj_halo, z1, last, d1)]
    devices = lax.axis_size("tm") * lax.axis_size("lon")
    sent = row_products(
        ((0, 2), (1, 2), (2, 2)),
        ([part(first, 0)], a1, a2),
        0,
        total,
        (devices, early, [], d_sums, (middle, m1, m2)),
    )
    received = lax.all_to_all(sent, ("tm", "lon"), 0, 0)
    multiplier, increment, dual = result(received, last, d1, inc0, inc1, middle, m1, obs_part)
    return (multiplier[None], dual.reshape(1, -1), increment[None])


def solution(mesh):
    in_specs = (
        P("tm", None, None, "lon"),
        P("tm", "lon"),
        P("tm", None, None, None, "lon"),
        P("tm", None, None, "lon"),
        P("tm", "lon"),
        P("tm", "lon"),
        P("tm", None, None, "lon"),
    )
    out_specs = (P("tm", None, None, "lon"), P("tm", "lon"), P("tm", None, None, "lon"))
    return jax.shard_map(shards, mesh=mesh, in_specs=in_specs, out_specs=out_specs, check_vma=False)
```

```python
import jax
import jax.numpy as jnp
from jax import lax
from jax.experimental import pallas as pl
from jax.experimental.pallas import tpu as pltpu
from jax.sharding import PartitionSpec as P

courant = 0.25
coriolis = 0.2
slope = 0.5 * courant

LANE = 128
BLOCK = 256
SEGMENT = 128
GROUP = 16
SHARE = 9
MARGIN = 8
HALO = 4
TRAJ, INC, VAR, LAST, PLANES = 0, 6, 9, 12, 16
MAIN = PLANES * HALO
F32 = jnp.float32
PARAMS = pltpu.CompilerParams(vmem_limit_bytes=56 * 1024 * 1024)


def iota(shape, dim):
    return lax.broadcasted_iota(jnp.int32, shape, dim)


def spread_shift(plane):
    return (LANE - (8 * plane + HALO)) % LANE


def pack_shift(plane):
    return (8 * plane + HALO) % LANE


def edges_of(planes, rows):
    lane = iota((rows, LANE), 1)
    packed = jnp.zeros((rows, LANE), F32)
    for number, plane in enumerate(planes):
        both = jnp.where(lane < LANE // 2, plane[:, :LANE], plane[:, LANE:])
        packed = jnp.where((lane >= 8 * number) & (lane < 8 * number + 8), pltpu.roll(both, pack_shift(number), 1), packed)
    return packed


def split_edges(turned, to_right, to_left, count):
    top = iota((8, turned.shape[1]), 0) < HALO
    for pair in range(count // 2):
        even = turned[16 * pair : 16 * pair + 8]
        odd = turned[16 * pair + 8 : 16 * pair + 16]
        to_right[8 * pair : 8 * pair + 8, :] = jnp.where(top, even, pltpu.roll(odd, HALO, 0))
        to_left[8 * pair : 8 * pair + 8, :] = jnp.where(top, pltpu.roll(even, HALO, 0), odd)


def joined_edges(from_left, from_right, count):
    top = iota((8, from_left.shape[1]), 0) < HALO
    pieces = []
    for pair in range(count // 2):
        left = from_left[8 * pair : 8 * pair + 8]
        right = from_right[8 * pair : 8 * pair + 8]
        pieces.append(jnp.where(top, left, pltpu.roll(right, HALO, 0)))
        pieces.append(jnp.where(top, pltpu.roll(left, HALO, 0), right))
    return jnp.concatenate(pieces, axis=0)


def padded_turn(message):
    rest = LANE - message.shape[0]
    if rest:
        message = jnp.concatenate([message, jnp.zeros((rest, message.shape[1]), F32)], axis=0)
    return message.T


def edges_kernel(increment, last, variance, traj, spread, to_right, to_left):
    rows = last.shape[1]
    planes = [traj[p].astype(F32) for p in range(6)]
    planes += [increment[f] for f in range(3)]
    planes += [variance[f] for f in range(3)]
    planes += [last[f] for f in range(3)]
    split_edges(edges_of(planes, rows).T, to_right.at[:MAIN], to_left.at[:MAIN], PLANES)
    spread_planes = [spread[f] for f in range(3)]
    split_edges(edges_of(spread_planes, rows).T, to_right.at[MAIN:], to_left.at[MAIN:], 4)


def edges_call(increment, last, variance, traj, spread):
    rows = last.shape[1]
    block = pl.BlockSpec((3, BLOCK, 2 * LANE), lambda i: (0, i, 0))
    sent = pl.BlockSpec((MAIN + 4 * HALO, BLOCK), lambda i: (0, i))
    return pl.pallas_call(
        edges_kernel,
        grid=(rows // BLOCK,),
        in_specs=[block, block, block, pl.BlockSpec((6, BLOCK, 2 * LANE), lambda i: (0, i, 0)), block],
        out_specs=[sent, sent],
        out_shape=[jax.ShapeDtypeStruct((MAIN + 4 * HALO, rows), F32)] * 2,
        compiler_params=PARAMS,
        cost_estimate=cost(16),
        name="edges",
    )(increment, last, variance, traj, spread)


def x_differences(tiles, first_lane, last_lane, joined):
    count = len(tiles)
    ahead = [pltpu.roll(t, LANE - 1, 1) for t in tiles]
    behind = [pltpu.roll(t, 1, 1) for t in tiles]
    if not joined:
        return [a - b for a, b in zip(ahead, behind)]
    return [
        jnp.where(last_lane, ahead[(t + 1) % count], ahead[t])
        - jnp.where(first_lane, behind[(t - 1) % count], behind[t])
        for t in range(count)
    ]


def rotation_at(start, total):
    position = (iota((GROUP, LANE), 0) + start).astype(F32)
    return coriolis * ((2.0 * position + 1.0) / total - 1.0)


def lane_ends():
    lane = iota((GROUP, LANE), 1)
    return lane == 0, lane == LANE - 1


def rows_at(start, offset=0):
    return pl.ds(pl.multiple_of(start + offset, GROUP), GROUP)


def traj_tiles(traj, traj_halo, step, start):
    out = []
    for plane in range(3 * step, 3 * step + 3):
        tiles = []
        if traj is not None:
            tiles += [traj[plane, rows_at(start), t * LANE : (t + 1) * LANE] for t in range(2)]
        if traj_halo is not None:
            at = [traj_halo.at[plane]] if len(traj_halo.shape) == 3 else [traj_halo.at[plane, t] for t in range(2)]
            tiles += [ref[rows_at(start), :] for ref in at]
        out.append([t.astype(F32) for t in tiles])
    return out


def load_rows(ref, start, offset):
    return [
        [ref[f, t, pl.ds(start + (MARGIN + offset), GROUP), :] for t in range(ref.shape[1])] for f in range(3)
    ]


def store_rows(ref, start, value):
    for f in range(3):
        for t in range(ref.shape[1]):
            ref[f, t, pl.ds(start + MARGIN, GROUP), :] = value[f][t]


def clear_margins(ref):
    rows = ref.shape[2]
    zero = jnp.zeros((MARGIN, LANE), F32)
    for f in range(3):
        for t in range(ref.shape[1]):
            ref[f, t, 0:MARGIN, :] = zero
            ref[f, t, rows - MARGIN : rows, :] = zero


def tangent_rows(source, traj, traj_halo, step, start, base, total, joined=True):
    here, above, below = (load_rows(source, start, k) for k in (0, 1, -1))
    trajectory = traj_tiles(traj, traj_halo, step, start)
    turn = rotation_at(start + base, total)
    ends = lane_ends()
    dx = [x_differences(here[f], *ends, joined) for f in range(3)]
    new = [[], [], []]
    for t in range(source.shape[1]):
        b, e, n = (trajectory[f][t] for f in range(3))
        h, u, v = (here[f][t] for f in range(3))
        xh, xu, xv = (dx[f][t] for f in range(3))
        yh, yu, yv = (above[f][t] - below[f][t] for f in range(3))
        new[0].append(h - slope * (b * (xu + yv) + e * xh + n * yh))
        new[1].append(u - slope * (xh + e * xu + n * yu) + turn * v)
        new[2].append(v - slope * (yh + e * xv + n * yv) - turn * u)
    return new


def north_rows(field, trajectory):
    out = [[], [], []]
    for t in range(3):
        b, _, n = (trajectory[f][t] for f in range(3))
        p, q, w = (field[f][t] for f in range(3))
        out[0].append(n * p + w)
        out[1].append(n * q)
        out[2].append(b * p + n * w)
    return out


def adjoint_rows(source, flux, traj, traj_halo, step, start, base, total):
    here = load_rows(source, start, 0)
    above, below = (load_rows(flux, start, k) for k in (1, -1))
    trajectory = traj_tiles(traj, traj_halo, step, start)
    turn = rotation_at(start + base, total)
    ends = lane_ends()
    east = [[], [], []]
    for t in range(3):
        b, e, _ = (trajectory[f][t] for f in range(3))
        p, q, w = (here[f][t] for f in range(3))
        east[0].append(e * p + q)
        east[1].append(b * p + e * q)
        east[2].append(e * w)
    dx = [x_differences(east[f], *ends, True) for f in range(3)]
    new = [[], [], []]
    for t in range(3):
        p, q, w = (here[f][t] for f in range(3))
        change = [slope * (dx[f][t] + (above[f][t] - below[f][t])) for f in range(3)]
        new[0].append(p + change[0])
        new[1].append(q + change[1] - turn * w)
        new[2].append(w + change[2] + turn * q)
    return new


def over_rows(begin, end, body):
    count = (end - begin) // GROUP
    unroll = next(u for u in (8, 6, 5, 4, 3, 2, 1) if count % u == 0)

    def step(i, carry):
        body(pl.multiple_of(begin + i * GROUP, GROUP))
        return carry

    lax.fori_loop(0, count, step, 0, unroll=unroll)


def padded(rows):
    return -(-rows // (2 * LANE)) * 2 * LANE


def extra(rows):
    return 8 * padded(rows) // (2 * LANE)


def turn_in(message, packed_ref):
    for j in range(message.shape[1] // LANE):
        packed_ref[j * LANE : (j + 1) * LANE, :] = padded_turn(message[:, j * LANE : (j + 1) * LANE])


def unfold_in(folded, packed_ref):
    for j in range(packed_ref.shape[0] // LANE):
        at = (slice(j // 2 * 8, j // 2 * 8 + 8), slice(j % 2 * LANE, (j % 2 + 1) * LANE))
        message = jnp.concatenate([folded[(f,) + at] for f in range(folded.shape[0])], axis=0)
        packed_ref[j * LANE : (j + 1) * LANE, :] = padded_turn(message)


def turn_out(halo, payload, behind):
    low = iota((8, LANE), 0) < HALO
    for j in range(halo.shape[1] // LANE):
        for f in range(halo.shape[0]):
            turned = halo[f, j * LANE : (j + 1) * LANE, :].T
            ends = jnp.where(low, turned[:8], turned[LANE - 8 :])
            row = behind + j // 2 * 8
            payload[f, row : row + 8, j % 2 * LANE : (j % 2 + 1) * LANE] = pltpu.roll(ends, HALO, 0)


def wide_scratch(rows, tiles=3):
    return pltpu.VMEM((3, tiles, rows + 2 * MARGIN, LANE), F32)


def tile_of(ref, f, start, t, offset=0):
    return ref[f, rows_at(start, offset), t * LANE : (t + 1) * LANE]


def set_tile(ref, f, start, t, value, offset=0):
    ref[f, rows_at(start, offset), t * LANE : (t + 1) * LANE] = value


class Copies:
    def __init__(self, sems):
        self.sems, self.used = sems, 0

    def rows(self, parts, begin, end, target):
        started = []
        for ref, at, count in parts:
            low, high = max(begin, at), min(end, at + count)
            if low < high:
                source = ref.at[..., low - at : high - at, :]
                goal = target.at[..., low - begin : high - begin, :]
                copy = pltpu.make_async_copy(source, goal, self.sems.at[self.used])
                self.used += 1
                copy.start()
                started.append(copy)
        return started


def placed(refs, parts):
    return [(ref, at, count) for ref, (_, at, count) in zip(refs, parts)]


def wait(copies):
    for copy in copies:
        copy.wait()


def segments(total):
    return [(at, min(at + SEGMENT, total)) for at in range(0, total, SEGMENT)]


def fetch(copies, begin, end, *pairs):
    return [
        [
            copy
            for parts, target in pairs
            for copy in copies.rows(parts, begin + low, begin + high, target.at[..., low:high, :])
        ]
        for low, high in segments(end - begin)
    ]


def leave(copies, source, begin, low, high, parts):
    started = []
    for target, at, count in parts:
        first, last = max(low, at), min(high, at + count)
        if first < last:
            started += copies.rows([(source, begin, source.shape[1])], first, last, target.at[:, first - at : last - at, :])
    return started


def run_tangent(span, total, get, ready, traj, traj_halo, wide_a, wide_b, traj_ready, put, done, joined=True):
    base, end, out_begin, out_end = span
    held = segments(end - base)
    clear_margins(wide_a)
    clear_margins(wide_b)
    for (low, high), copies in zip(held, ready):
        wait(copies)
        over_rows(low, high, lambda s: store_rows(wide_a, s, get(s)))
    for (low, high), copies in zip(held, traj_ready):
        wait(copies)
        over_rows(
            low, high, lambda s: store_rows(wide_b, s, tangent_rows(wide_a, traj, traj_halo, 0, s, base, total, joined))
        )
    for low, high in segments(out_end - out_begin):
        skip = out_begin - base
        over_rows(
            low + skip,
            high + skip,
            lambda s: put(s, tangent_rows(wide_b, traj, traj_halo, 1, s, base, total, joined)),
        )
        done(out_begin + low, out_begin + high)


def run_adjoint(span, total, get, ready, traj, traj_halo, wide_a, wide_b, flux_a, flux_b, put, begin_put, done):
    base, end, out_begin, out_end = span
    clear_margins(flux_a)
    clear_margins(flux_b)

    def begin(s):
        field = get(s)
        store_rows(wide_a, s, field)
        store_rows(flux_a, s, north_rows(field, traj_tiles(traj, traj_halo, 1, s)))

    def middle(s):
        field = adjoint_rows(wide_a, flux_a, traj, traj_halo, 1, s, base, total)
        store_rows(wide_b, s, field)
        store_rows(flux_b, s, north_rows(field, traj_tiles(traj, traj_halo, 0, s)))

    for (low, high), copies in zip(segments(end - base), ready):
        wait(copies)
        over_rows(low, high, begin)
    over_rows(0, end - base, middle)
    for (low, high), copies in zip(segments(out_end - out_begin), begin_put):
        wait(copies)
        skip = out_begin - base
        over_rows(
            low + skip, high + skip, lambda s: put(s, adjoint_rows(wide_b, flux_b, traj, traj_halo, 0, s, base, total))
        )
        done(out_begin + low, out_begin + high)


def halo_of(lanes, plane):
    return pltpu.roll(lanes, spread_shift(plane), 1)


ANY = pl.BlockSpec(memory_space=pltpu.HBM)


def whole(count):
    return [pl.BlockSpec(memory_space=pltpu.VMEM)] * count


def cost(mib, steps=2):
    return pl.CostEstimate(flops=2**10, bytes_accessed=mib * 2**20, transcendentals=0)


def f32(*shape):
    return jax.ShapeDtypeStruct(shape, F32)


def vmem(*shape, dtype=F32):
    return pltpu.VMEM(shape, dtype)


def call(name, kernel, ins, outs, scratch, mib, *args, first_any=False, outs_any=False):
    specs = [ANY if outs_any or (first_any and k == 0) else whole(1)[0] for k in range(len(outs))]
    return pl.pallas_call(
        kernel,
        in_specs=ins,
        out_specs=specs,
        out_shape=outs,
        scratch_shapes=scratch,
        compiler_params=PARAMS,
        cost_estimate=cost(mib),
        name=name,
    )(*args)


def tangent_band(first, last, variance, traj, cuts):
    _, total, columns = first.shape

    def kernel(first_in, last_in, variance_in, traj_in, *refs):
        aheads, refs = refs[: len(cuts)], refs[len(cuts) :]
        increment, first, last, variance, traj, wide_a, wide_b, out, sems = refs
        aheads = [(ref, low, high - low) for ref, (low, high) in zip(aheads, cuts)]
        copies = Copies(sems)
        ready = fetch(copies, 0, total, *[([(r, 0, total)], to) for r, to in ((first_in, first), (last_in, last), (variance_in, variance))])
        traj_ready = fetch(copies, 0, total, ([(traj_in, 0, total)], traj))

        def get(s):
            tiles = [
                [tile_of(first, f, s, t) - tile_of(variance, f, s, t) * tile_of(last, f, s, t) for t in range(2)]
                for f in range(3)
            ]
            for f in range(3):
                for t in range(2):
                    set_tile(first, f, s, t, tiles[f][t])
            return tiles

        def put(s, new):
            for f in range(3):
                for t in range(2):
                    set_tile(out, f, s, t, -new[f][t])

        leaving = []

        def done(low, high):
            leaving.extend(leave(copies, out, 0, low, high, aheads))
            leaving.extend(leave(copies, first, 0, low, high, [(increment, 0, total)]))

        run_tangent((0, total, 0, total), total, get, ready, traj, None, wide_a, wide_b, traj_ready, put, done)
        wait(leaving)

    outs = [f32(3, high - low, columns) for low, high in cuts] + [f32(*first.shape)]
    scratch = [vmem(*first.shape)] * 3 + [vmem(*traj.shape, dtype=traj.dtype)] + [wide_scratch(total, 2)] * 2
    scratch += [vmem(*first.shape), pltpu.SemaphoreType.DMA((7 * len(segments(total)),))]
    return call("tangent_band", kernel, [ANY] * 4, outs, scratch, 18, first, last, variance, traj, outs_any=True)


def tangent_seams(increment, traj, from_left, from_right):
    _, total, columns = increment.shape

    def kernel(inc_in, traj_in, from_left, from_right, edges, traj_halo, var_halo, last_edges, spread_halo, inc, traj, wide_a, wide_b, seams, inc_halo, out, sems):
        copies = Copies(sems)
        inc_ready = fetch(copies, 0, total, ([(inc_in, 0, total)], inc))
        traj_ready = fetch(copies, 0, total, ([(traj_in, 0, total)], traj))
        left_part = iota((LANE, LANE), 1) < LANE // 2
        for j in range(total // LANE):
            cut = slice(j * LANE, (j + 1) * LANE)
            joined = joined_edges(from_left[:MAIN, cut], from_right[:MAIN, cut], PLANES)
            last_edges[:, cut] = joined[8 * LAST : 8 * LAST + 24]
            packed = joined.T
            spread = padded_turn(joined_edges(from_left[MAIN:, cut], from_right[MAIN:, cut], 4))
            for plane in range(6):
                traj_halo[plane, cut, :] = halo_of(packed, TRAJ + plane).astype(traj_halo.dtype)
            for f in range(3):
                var_halo[f, cut, :] = halo_of(packed, VAR + f)
                inc_halo[f, cut, :] = halo_of(packed, INC + f)
                spread_halo[f, cut, :] = halo_of(spread, f)
        for copies_of in inc_ready + traj_ready:
            wait(copies_of)
        for j in range(total // LANE):
            cut = slice(j * LANE, (j + 1) * LANE)
            for plane in range(6):
                halo = traj_halo[plane, cut, :].astype(F32)
                own = [traj[plane, cut, t * LANE : (t + 1) * LANE].astype(F32) for t in range(2)]
                seams[plane, 0, cut, :] = jnp.where(left_part, own[0], halo).astype(seams.dtype)
                seams[plane, 1, cut, :] = jnp.where(left_part, halo, own[1]).astype(seams.dtype)

        def get(s):
            left = iota((GROUP, LANE), 1) < LANE // 2
            tiles = []
            for f in range(3):
                halo = inc_halo[f, rows_at(s), :]
                tiles.append([jnp.where(left, tile_of(inc, f, s, 0), halo), jnp.where(left, halo, tile_of(inc, f, s, 1))])
            return tiles

        def put(s, new):
            for f in range(3):
                for t in range(2):
                    out[2 * f + t, rows_at(s), :] = -new[f][t]

        nothing = [[] for _ in segments(total)]
        run_tangent((0, total, 0, total), total, get, nothing, None, seams, wide_a, wide_b, nothing, put, lambda low, high: None, False)
        turn_out(out, edges, 0)

    outs = [f32(6, extra(total), columns), jax.ShapeDtypeStruct((6, total, LANE), traj.dtype)]
    outs += [f32(3, total, LANE), f32(24, total), f32(3, total, LANE)]
    scratch = [vmem(*increment.shape), vmem(*traj.shape, dtype=traj.dtype)] + [wide_scratch(total, 2)] * 2
    scratch += [vmem(6, 2, total, LANE, dtype=traj.dtype), vmem(3, total, LANE), vmem(6, total, LANE)]
    scratch += [pltpu.SemaphoreType.DMA((2 * len(segments(total)),))]
    return call("tangent_seams", kernel, [ANY, ANY] + whole(2), outs, scratch, 10, increment, traj, from_left, from_right)


def whole_of(total, *pairs):
    return [([(ref, 0, total)], target) for ref, target in pairs]


def adjoint_first(span, later, later_edges, traj, traj_halo, spread, spread_halo):
    base, end, out_begin, out_end = span
    held, rows = end - base, out_end - out_begin
    total, columns = spread.shape[1:]
    count = len(later)

    def kernel(*refs):
        later_in, refs = placed(refs[:count], later), refs[count:]
        traj_in, traj_halo_in, spread_in, spread_halo_in, later_edges, pulled = refs[:6]
        field, traj, traj_halo, spread, wide_a, wide_b, flux_a, flux_b, own, halo, out, sems = refs[6:]
        copies = Copies(sems)
        ready = fetch(copies, base, end, (later_in, field), *whole_of(total, (traj_in, traj), (traj_halo_in, traj_halo)))
        begin_put = fetch(copies, out_begin, out_end, *whole_of(total, (spread_in, spread), (spread_halo_in, halo)))
        turn_in(later_edges, own)
        if rows < halo.shape[1]:
            halo[:, rows:, :] = jnp.zeros((3, halo.shape[1] - rows, LANE), F32)
        skip = base - out_begin

        def get(s):
            lanes = own[rows_at(s, base), :]
            return [[tile_of(field, f, s, t) for t in range(2)] + [halo_of(lanes, f)] for f in range(3)]

        def put(s, new):
            for f in range(3):
                for t in range(2):
                    set_tile(out, f, s, t, tile_of(spread, f, s, t, skip) - new[f][t], skip)
                halo[f, rows_at(s, skip), :] = halo[f, rows_at(s, skip), :] - new[f][2]

        leaving = []

        def done(low, high):
            leaving.extend(leave(copies, out, out_begin, low, high, [(pulled, out_begin, rows)]))

        run_adjoint(span, total, get, ready, traj, traj_halo, wide_a, wide_b, flux_a, flux_b, put, begin_put, done)
        turn_out(halo, out, rows)
        after_rows = rows + extra(rows)
        leaving.extend(copies.rows([(out, 0, after_rows)], rows, after_rows, pulled.at[:, rows:after_rows, :]))
        wait(leaving)

    outs = [f32(3, rows + extra(rows), columns)]
    scratch = [vmem(3, held, columns), vmem(6, held, columns, dtype=traj.dtype), vmem(6, held, LANE, dtype=traj.dtype)]
    scratch += [vmem(3, rows, columns)] + [wide_scratch(held)] * 4 + [vmem(total, LANE)]
    scratch += [vmem(3, padded(rows), LANE), vmem(3, rows + extra(rows), columns)]
    scratch += [pltpu.SemaphoreType.DMA(((6 + count) * len(segments(held)) + 1,))]
    return call(
        "adjoint_first", kernel, [ANY] * (count + 4) + whole(1), outs, scratch, 10,
        *[p[0] for p in later], traj, traj_halo, spread, spread_halo, later_edges, first_any=True,
    )[0]


def unfold_parts(copies, parts, folds):
    started = []
    for (ref, _, count), fold in zip(parts, folds):
        started += copies.rows([(ref, 0, count + extra(count))], count, count + extra(count), fold)
    return started


def unfold_all(parts, folds, packed_ref):
    for (_, at, count), fold in zip(parts, folds):
        unfold_in(fold, packed_ref.at[at : at + padded(count), :])


def tangent_second(span, earlier, earlier_edges, pulled, variance, traj, traj_halo, var_halo, new_begin):
    base, end, out_begin, out_end = span
    held, rows = end - base, out_end - out_begin
    _, total, columns = variance.shape
    n_earlier, n_pulled = len(earlier), len(pulled)

    def kernel(*refs):
        earlier_in, refs = placed(refs[:n_earlier], earlier), refs[n_earlier:]
        pulled_in, refs = placed(refs[:n_pulled], pulled), refs[n_pulled:]
        edges_in, variance_in, traj_in, traj_halo_in, var_halo_in, ahead, increment, patched = refs[:8]
        earl, pull, variance, traj, traj_halo, var_halo, wide_a, wide_b, e_own, p_own, e_fold = refs[8:19]
        p_folds, (inc, out, sems) = refs[19 : 19 + n_pulled], refs[19 + n_pulled :]
        copies = Copies(sems)
        edge_copies = copies.rows([(edges_in, 0, extra(total))], 0, extra(total), e_fold)
        edge_copies += unfold_parts(copies, pulled_in, p_folds)
        ready = fetch(
            copies, base, end, (earlier_in, earl), (pulled_in, pull), *whole_of(total, (variance_in, variance), (var_halo_in, var_halo))
        )
        traj_ready = fetch(copies, base, end, *whole_of(total, (traj_in, traj), (traj_halo_in, traj_halo)))
        wait(edge_copies)
        unfold_in(e_fold, e_own)
        unfold_all(pulled_in, p_folds, p_own)
        skip = base - out_begin

        def get(s):
            e_lanes, p_lanes = e_own[rows_at(s, base), :], p_own[rows_at(s, base), :]
            lane = iota((GROUP, LANE), 1)
            tiles = []
            for f in range(3):
                left, right = halo_of(e_lanes, 2 * f), halo_of(e_lanes, 2 * f + 1)
                fixed = [
                    jnp.where(lane < 2, left, tile_of(earl, f, s, 0)),
                    jnp.where(lane >= LANE - 2, right, tile_of(earl, f, s, 1)),
                ]
                own = [fixed[t] - tile_of(variance, f, s, t) * tile_of(pull, f, s, t) for t in range(2)]
                for t in range(2):
                    set_tile(earl, f, s, t, fixed[t])
                    set_tile(inc, f, s, t, own[t])
                beside = jnp.where(lane < LANE // 2, right, left)
                tiles.append(own + [beside - var_halo[f, rows_at(s), :] * halo_of(p_lanes, f)])
            return tiles

        def put(s, new):
            for f in range(3):
                for t in range(2):
                    set_tile(out, f, s, t, -new[f][t], skip)

        leaving = []

        def done(low, high):
            leaving.extend(leave(copies, out, out_begin, low, high, [(ahead, out_begin, rows)]))
            if low == out_begin:
                leaving.extend(leave(copies, inc, base, new_begin, end, [(increment, new_begin, end - new_begin)]))
                leaving.extend(leave(copies, earl, base, new_begin, end, [(patched, new_begin, end - new_begin)]))

        run_tangent(span, total, get, ready, traj, traj_halo, wide_a, wide_b, traj_ready, put, done)
        wait(leaving)

    outs = [f32(3, rows, columns)] + [f32(3, end - new_begin, columns)] * 2
    scratch = [vmem(3, held, columns)] * 3 + [vmem(6, held, columns, dtype=traj.dtype), vmem(6, held, LANE, dtype=traj.dtype)]
    scratch += [vmem(3, held, LANE)] + [wide_scratch(held)] * 2 + [vmem(total, LANE), vmem(total + 2 * LANE, LANE)]
    scratch += [vmem(6, extra(total), columns)] + [vmem(3, extra(p[2]), columns) for p in pulled]
    scratch += [vmem(3, held, columns), vmem(3, rows, columns)]
    scratch += [pltpu.SemaphoreType.DMA(((6 + n_earlier + n_pulled) * len(segments(held)) + 4 + n_pulled,))]
    return call(
        "tangent_second", kernel, [ANY] * (n_earlier + n_pulled + 5), outs, scratch, 16,
        *[p[0] for p in earlier], *[p[0] for p in pulled], earlier_edges, variance, traj, traj_halo, var_halo, outs_any=True,
    )


def adjoint_second(span, later, traj, traj_halo, spread, last, pulled):
    base, end, out_begin, out_end = span
    held, rows = end - base, out_end - out_begin
    _, total, columns = last.shape
    n_later, n_pulled = len(later), len(pulled)

    def kernel(*refs):
        later_in, refs = placed(refs[:n_later], later), refs[n_later:]
        pulled_in, refs = placed(refs[:n_pulled], pulled), refs[n_pulled:]
        traj_in, traj_halo_in, spread_in, last_in, sums, field, traj, traj_halo, spread, last, pull = refs[:11]
        wide_a, wide_b, flux_a, flux_b, own = refs[11:16]
        folds, sems = refs[16:-1], refs[-1]
        copies = Copies(sems)
        edge_copies = unfold_parts(copies, later_in, folds)
        ready = fetch(copies, base, end, (later_in, field), *whole_of(total, (traj_in, traj), (traj_halo_in, traj_halo)))
        begin_put = fetch(copies, out_begin, out_end, (pulled_in, pull), *whole_of(total, (spread_in, spread), (last_in, last)))
        wait(edge_copies)
        unfold_all(later_in, folds, own)
        sums[...] = jnp.zeros_like(sums)
        skip = base - out_begin

        def get(s):
            lanes = own[rows_at(s, base), :]
            return [[tile_of(field, f, s, t) for t in range(2)] + [halo_of(lanes, f)] for f in range(3)]

        def put(s, new):
            parts = [jnp.zeros((GROUP, LANE), F32)] * 3
            for f in range(3):
                for t in range(2):
                    value = tile_of(spread, f, s, t, skip) - new[f][t]
                    for k, other in enumerate((tile_of(last, f, s, t, skip), tile_of(pull, f, s, t, skip), value)):
                        parts[k] = parts[k] + other * value
            for k in range(3):
                sums[k] = sums[k] + parts[k]

        run_adjoint(
            span, total, get, ready, traj, traj_halo, wide_a, wide_b, flux_a, flux_b, put, begin_put, lambda low, high: None
        )

    scratch = [vmem(3, held, columns), vmem(6, held, columns, dtype=traj.dtype), vmem(6, held, LANE, dtype=traj.dtype)]
    scratch += [vmem(3, rows, columns)] * 3 + [wide_scratch(held)] * 4 + [vmem(total + 2 * LANE, LANE)]
    scratch += [vmem(3, extra(p[2]), columns) for p in later]
    scratch += [pltpu.SemaphoreType.DMA(((4 + n_later + n_pulled) * len(segments(held)) + n_later,))]
    outs = [f32(3, GROUP, LANE)]
    return call(
        "adjoint_second", kernel, [ANY] * (n_later + n_pulled + 4), outs, scratch, 16,
        *[p[0] for p in later], *[p[0] for p in pulled], traj, traj_halo, spread, last,
    )[0]


def observe(parts, total, where):
    count = where.shape[0]

    def kernel(*refs):
        parts_in, (where_smem, column, out, field, picked, sems) = refs[: len(parts)], refs[len(parts) :]
        copies = Copies(sems)
        started = []
        for f in range(3):
            source = [(ref.at[f], at, rows) for ref, at, rows in placed(parts_in, parts)]
            started += copies.rows(source, 0, total, field.at[f * total : (f + 1) * total])
        wait(started)

        def step(i, carry):
            row = lax.shift_right_logical(where_smem[i], 8)
            picked[pl.ds(i, 1), :] = field[pl.ds(row, 1), :]
            return carry

        lax.fori_loop(0, count, step, 0, unroll=16)
        lane = iota((LANE, LANE), 1).astype(F32)
        for j in range(count // LANE):
            cut = slice(j * LANE, (j + 1) * LANE)
            at = jnp.broadcast_to(column[j : j + 1, :], (LANE, LANE)).T
            kept = jnp.where(lane == at, picked[cut, :LANE], 0.0)
            kept = kept + jnp.where(lane + float(LANE) == at, picked[cut, LANE:], 0.0)
            out[j : j + 1, :] = jnp.sum(kept.T, axis=0, keepdims=True)

    columns = 2 * LANE
    column = (where % columns).astype(F32).reshape(-1, LANE)
    return pl.pallas_call(
        kernel,
        in_specs=[ANY] * len(parts) + [pl.BlockSpec(memory_space=pltpu.SMEM)] + whole(1),
        out_specs=whole(1)[0],
        out_shape=f32(count // LANE, LANE),
        scratch_shapes=[vmem(3 * total, columns), vmem(count, columns), pltpu.SemaphoreType.DMA((3 * len(parts),))],
        compiler_params=PARAMS,
        cost_estimate=cost(3),
        name="observe",
    )(*[part[0] for part in parts], where, column)


def scatter(where, values, total):
    count = where.shape[0]

    def kernel(where_smem, values_smem, field):
        field[...] = jnp.zeros_like(field)
        lane = iota((1, 2 * LANE), 1)

        def step(i, carry):
            index = where_smem[i]
            at = (pl.ds(lax.shift_right_logical(index, 8), 1), slice(None))
            field[at] = field[at] + jnp.where(lane == (index & (2 * LANE - 1)), values_smem[i], 0.0)
            return carry

        lax.fori_loop(0, count, step, 0, unroll=8)

    return pl.pallas_call(
        kernel,
        in_specs=[pl.BlockSpec(memory_space=pltpu.SMEM)] * 2,
        out_specs=whole(1)[0],
        out_shape=f32(3 * total, 2 * LANE),
        compiler_params=PARAMS,
        cost_estimate=cost(3),
        name="scatter",
    )(where, values).reshape(3, total, 2 * LANE)


def one_sum(value):
    return jnp.sum(jnp.sum(value, axis=1, keepdims=True), axis=0, keepdims=True)


def pieces(cuts):
    return [(at, min(at + BLOCK, high)) for low, high in cuts for at in range(low, high, BLOCK)]


def summed(values):
    total = values[0]
    for value in values[1:]:
        total = total + value
    return total


def row_products(pairs, arrays, low, high, finish=None):
    columns = arrays[0][0][0].shape[2]
    counts = [len(parts) for parts in arrays]
    cuts = pieces([(low, high)])
    if finish:
        devices, early, a_before, d_parts, obs = finish
        scalars = [early] + a_before + d_parts + list(obs)
        out = f32(devices, 8, LANE)
    else:
        scalars = []
        out = f32(len(pairs), GROUP, columns)

    def kernel(*refs):
        refs = list(refs)
        inputs = []
        for parts in arrays:
            inputs.append([(refs.pop(0), at, count) for _, at, count in parts])
        extras, refs = refs[: len(scalars)], refs[len(scalars) :]
        out_ref, held, sems = refs[0], refs[1:-1], refs[-1]
        copies = Copies(sems)
        started = []
        for begin, end in cuts:
            group = []
            for parts, scratch in zip(inputs, held):
                group += copies.rows(parts, begin, end, scratch.at[:, begin - low : end - low, :])
            started.append(group)
        sums = tuple(jnp.zeros((GROUP, columns), F32) for _ in pairs)
        for (begin, end), group in zip(cuts, started):
            wait(group)

            def step(i, carry, begin=begin):
                at = pl.ds(pl.multiple_of(begin - low + i * GROUP, GROUP), GROUP)
                parts = list(carry)
                for f in range(3):
                    tiles = [a[f, at, :] for a in held]
                    for k, (one, two) in enumerate(pairs):
                        parts[k] = parts[k] + tiles[one] * tiles[two]
                return tuple(parts)

            sums = lax.fori_loop(0, (end - begin) // GROUP, step, sums)
        if not finish:
            for k, value in enumerate(sums):
                out_ref[k] = value
            return
        early_ref, extras = extras[0], extras[1:]
        before, d_refs, (o0, o1, o2) = extras[: len(a_before)], extras[len(a_before) : -3], (e[...] for e in extras[-3:])
        tail = [
            summed([one_sum(summed([sums[k]] + [r[k] for r in before]))] + [one_sum(summed([r[k] for r in d_refs]))])
            for k in range(3)
        ]
        head = [one_sum(early_ref[2 * k] + early_ref[2 * k + 1]) for k in range(3)]
        values = (
            head[0] + one_sum(o0 * o0),
            head[1] + one_sum(o0 * o1),
            tail[0] + one_sum(o0 * o2),
            head[2] + one_sum(o1 * o1),
            tail[1] + one_sum(o1 * o2),
            tail[2] + one_sum(o2 * o2),
        )
        lane = iota((8, LANE), 1)
        row = jnp.zeros((8, LANE), F32)
        for k, value in enumerate(values):
            row = jnp.where(lane == k, value, row)
        for k in range(devices):
            out_ref[k] = row

    return pl.pallas_call(
        kernel,
        in_specs=[ANY] * sum(counts) + whole(len(scalars)),
        out_specs=whole(1)[0],
        out_shape=out,
        scratch_shapes=[vmem(3, high - low, columns) for _ in arrays]
        + [pltpu.SemaphoreType.DMA((len(cuts) * (sum(counts)),))],
        compiler_params=pltpu.CompilerParams(vmem_limit_bytes=20 * 1024 * 1024),
        cost_estimate=cost(9, 1),
        name="last_products" if finish else "products",
    )(*[part[0] for parts in arrays for part in parts], *scalars)


def weights(s00, s01, s02, s11, s12, s22):
    alpha = s01 / s00
    t11 = s11 - alpha * s01
    along = (s12 - alpha * s02) / t11
    beta = jnp.sqrt(s00)
    gamma = 1.0 / jnp.sqrt(t11)
    h00 = 1.0 + alpha
    h10_square = t11 / s00
    h10 = jnp.sqrt(h10_square)
    h01 = (s02 - alpha * s01) * gamma / beta
    h11 = 1.0 - alpha + along
    h21_square = (s22 - s02 * (s02 / s00) - along * (s12 - alpha * s02)) / t11
    g00 = h00 * h00 + h10_square
    g01 = h00 * h01 + h10 * h11
    g11 = h01 * h01 + h11 * h11 + h21_square
    q0 = beta * h00
    q1 = beta * h01
    det = g00 * g11 - g01 * g01
    y0 = (g11 * q0 - g01 * q1) / det
    y1 = (g00 * q1 - g01 * q0) / det
    c1 = y1 * gamma
    return (y0 / beta - c1 * alpha, c1)


def result(received, last, d1, inc0, inc1, middle, m1, obs_part):
    _, total, columns = last.shape
    n_d1, n_inc1 = len(d1), len(inc1)

    def kernel(last, inc0, *refs):
        d1_in, refs = placed(refs[:n_d1], d1), refs[n_d1:]
        inc1_in, refs = placed(refs[:n_inc1], inc1), refs[n_inc1:]
        received, middle, m1, obs_part, multiplier, increment, dual, multi, incr, sems = refs
        copies = Copies(sems)
        sums = jnp.sum(received[...], axis=0)
        lane = iota((8, LANE), 1)
        scalars = [
            jnp.broadcast_to(jnp.sum(jnp.where(lane == k, sums, 0.0), axis=1, keepdims=True), (8, LANE))
            for k in range(6)
        ]
        c0, c1 = weights(*scalars)
        dual[...] = (c0[0:1] * middle[...] + c1[0:1] * m1[...]) / obs_part[...]
        c0, c1 = (jnp.concatenate([c] * (GROUP // 8), axis=0) for c in (c0, c1))
        leaving = []
        for out, whole_in, parts, target in ((multi, last, d1_in, multiplier), (incr, inc0, inc1_in, increment)):
            for ref, at, count in parts:
                for low, high in segments(count):

                    def body(s, out=out, whole_in=whole_in, ref=ref, at=at):
                        for f in range(3):
                            for t in range(2):
                                value = c0 * tile_of(whole_in, f, s, t, at) + c1 * tile_of(ref, f, s, t)
                                set_tile(out, f, s, t, value, at)

                    over_rows(low, high, body)
                    leaving += leave(copies, out, 0, at + low, at + high, [(target, 0, total)])
        wait(leaving)

    shape = (3, total, columns)
    return pl.pallas_call(
        kernel,
        in_specs=whole(6 + n_d1 + n_inc1),
        out_specs=[ANY, ANY] + whole(1),
        out_shape=[f32(*shape)] * 2 + [f32(*middle.shape)],
        scratch_shapes=[vmem(*shape)] * 2 + [pltpu.SemaphoreType.DMA((4 * len(segments(total)) + 4,))],
        compiler_params=pltpu.CompilerParams(vmem_limit_bytes=40 * 1024 * 1024),
        cost_estimate=cost(18, 1),
        name="result",
    )(last, inc0, *[p[0] for p in d1], *[p[0] for p in inc1], received, middle, m1, obs_part)


def moved(block, axis, distance, wrap):
    size = lax.axis_size(axis)
    if wrap:
        route = [(i, (i + distance) % size) for i in range(size)]
    else:
        route = [(i, i + distance) for i in range(size) if 0 <= i + distance < size]
    return lax.ppermute(block, axis, route)


def after(value, other):
    return lax.optimization_barrier((value, other))


def part(array, at, count=None):
    return (array, at, array.shape[1] if count is None else count)


def shards(rhs_state, innovations, trajectory, model_var, obs_var, obs_index, control_rhs):
    total, columns = rhs_state.shape[2:]
    first, last, variance = rhs_state[0], control_rhs[0], model_var[0]
    traj = trajectory.reshape(-1, total, columns)
    where = obs_index[0]
    middle, obs_part = innovations[0].reshape(-1, LANE), obs_var[0].reshape(-1, LANE)

    step = GROUP
    cut = total * SHARE // 16 // GROUP * GROUP
    one, two = cut - step, cut - 2 * step

    later = [part(moved(last, "tm", -1, False), 0)]
    ahead, inc0 = tangent_band(first, last, variance, traj, [(0, total)])
    a1 = [part(moved(ahead, "tm", 1, False), 0)]
    z0 = scatter(where, (middle / obs_part).reshape(-1), total)
    to_right, to_left = edges_call(inc0, last, variance, traj, z0)
    from_left = moved(to_right, "lon", 1, True)
    from_right = moved(to_left, "lon", -1, True)
    ahead_edges, traj_halo, var_halo, last_edges, z0_halo = tangent_seams(inc0, traj, from_left, from_right)
    later_edges = moved(last_edges, "tm", -1, False)
    a1_edges = moved(ahead_edges, "tm", 1, False)
    m1 = observe([part(inc0, 0)], total, where)
    m1, later_edges = after(m1, later_edges)

    d1, d1_later, a2, inc1, fixed = [], [], [], [], []
    spans = [(0, cut, 0, one), (one - step, total, one, total)]
    seconds = [(0, one, 0, two), (two - step, total, two, total)]
    for c, (span, second) in enumerate(zip(spans, seconds)):
        pulled = adjoint_first(span, later, later_edges, traj, traj_halo, z0, z0_halo)
        d1.append(part(pulled, span[2], span[3] - span[2]))
        d1_later.append(part(moved(pulled, "tm", -1, False), *d1[-1][1:]))
        ahead, increment, patched = tangent_second(
            second, a1, a1_edges, d1, variance, traj, traj_halo, var_halo, span[2]
        )
        a2.append(part(moved(ahead, "tm", 1, False), second[2]))
        inc1.append(part(increment, span[2]))
        fixed.append(part(patched, span[2]))
    a1 = fixed
    z1 = scatter(where, (m1 / obs_part).reshape(-1), total)
    m2 = observe(inc1, total, where)
    early = row_products(
        ((0, 0), (1, 1), (0, 2), (1, 3), (2, 2), (3, 3)), ([part(first, 0)], [part(last, 0)], a1, d1), 0, total
    )
    d_sums = [
        adjoint_second(second, d1_later[: c + 1], traj, traj_halo, z1, last, d1) for c, second in enumerate(seconds)
    ]
    devices = lax.axis_size("tm") * lax.axis_size("lon")
    sent = row_products(
        ((0, 2), (1, 2), (2, 2)),
        ([part(first, 0)], a1, a2),
        0,
        total,
        (devices, early, [], d_sums, (middle, m1, m2)),
    )
    received = lax.all_to_all(sent, ("tm", "lon"), 0, 0)
    multiplier, increment, dual = result(received, last, d1, inc0, inc1, middle, m1, obs_part)
    return (multiplier[None], dual.reshape(1, -1), increment[None])


def solution(mesh):
    in_specs = (
        P("tm", None, None, "lon"),
        P("tm", "lon"),
        P("tm", None, None, None, "lon"),
        P("tm", None, None, "lon"),
        P("tm", "lon"),
        P("tm", "lon"),
        P("tm", None, None, "lon"),
    )
    out_specs = (P("tm", None, None, "lon"), P("tm", "lon"), P("tm", None, None, "lon"))
    return jax.shard_map(shards, mesh=mesh, in_specs=in_specs, out_specs=out_specs, check_vma=False)
```
